32 devices in a mesh: ep: 8 (over z, y), ws: 4 (over x, core).
Axes of the slice: x: 2, y: 2, z: 4, core: 2. Of those that a mesh axis runs over, the one named last changes fastest.
Arguments:
- tokens: bfloat16 [4096, 2048], P('ep'), may hold values from -6 to 6
- grad_out: bfloat16 [4096, 2048], P('ep'), may hold values from -6 to 6
- norm1_gain: float32 [2048], replicated, may hold values from 0.5 to 1.5
- attn_router: bfloat16 [2048, 8], replicated, may hold values from -0.25 to 0.25
- attn_routes: int32 [4096, 2], P('ep'), may hold values from 0 to 7, all different within a row
- attn_order: int32 [8, 1024], P('ep'), may hold values from 0 to 1023, each once within a row
- w_query: bfloat16 [8, 2048, 2048], P(None, 'ep', 'ws'), may hold values from -0.125 to 0.125
- w_kv: bfloat16 [2, 2048, 2048], P(None, 'ep', 'ws'), may hold values from -0.125 to 0.125
- w_attn_out: bfloat16 [8, 2048, 2048], P(None, 'ep', 'ws'), may hold values from -0.75 to 0.75
- norm2_gain: float32 [2048], replicated, may hold values from 0.5 to 1.5
- mlp_router: bfloat16 [2048, 8], replicated, may hold values from -0.25 to 0.25
- mlp_routes: int32 [4096, 2], P('ep'), may hold values from 0 to 7, all different within a row
- mlp_order: int32 [8, 1024], P('ep'), may hold values from 0 to 1023, each once within a row
- w_gate: bfloat16 [2048, 45056], P(None, ('ep', 'ws')), may hold values from -0.125 to 0.125
- w_up: bfloat16 [2048, 45056], P(None, ('ep', 'ws')), may hold values from -0.125 to 0.125
- w_down: bfloat16 [2048, 45056], P(None, ('ep', 'ws')), may hold values from -0.078125 to 0.078125
Outputs:
- layer_out: bfloat16 [4096, 2048], P('ep')
- grad_tokens: float32 [4096, 2048], P('ep')
- grad_norm1: float32 [2048], replicated
- grad_attn_router: float32 [2048, 8], replicated
- grad_query: float32 [8, 2048, 2048], P(None, 'ep', 'ws')
- grad_kv: float32 [2, 2048, 2048], P(None, 'ep', 'ws')
- grad_attn_out: float32 [8, 2048, 2048], P(None, 'ep', 'ws')
- grad_norm2: float32 [2048], replicated
- grad_mlp_router: float32 [2048, 8], replicated
- grad_gate: float32 [2048, 45056], P(None, ('ep', 'ws'))
- grad_up: float32 [2048, 45056], P(None, ('ep', 'ws'))
- grad_down: float32 [2048, 45056], P(None, ('ep', 'ws'))
The draws below stay inside these ranges and needn't reach their ends.
Inputs may be any that keep to these rules, and one draw needn't show every extreme that they name: `attn_routes`: each token names two different experts. `mlp_routes`: each token names two different experts. `attn_order`: row g lists each of the group's 1024 pairs once, pair 2 i + c being local token i's route c. `mlp_order`: row g lists each of the group's 1024 pairs once, pair 2 i + c being local token i's route c.
All inputs are finite; a program needn't handle non-finite values.
Results may differ from the reference program's by a relative error of at most 0.022.
Values may be sent and summed in bfloat16 or wider, within the bound.
A program may use at most 320 MiB of HBM per device.

```python
import math
import jax
import jax.numpy as jnp
from jax import lax

D = 2048
HEADS = 16
HD = 128
KVH = 16
EA = 8
EM = 8
FF = 5632
TOPK = 2
PROMPT = 256
CLEN = 128
GTOK = 512
TOKENS = 4096
PAIRS = 1024
ACAP = 128
MCAP = 128
SLICES = 4
FS = 1408
N_EP = 8


def levels(stream_key, dims, cuts, smallest, high):
    factor_of, own = 1.0, jax.random.fold_in(stream_key, 6)
    for axis_at, blocks in cuts:
        steps = jnp.exp(jax.random.uniform(jax.random.fold_in(own, axis_at), (blocks,), jnp.float32, smallest / len(cuts), high / len(cuts)))
        factor_of = factor_of * jnp.repeat(steps, dims[axis_at] // blocks).reshape([-1 if axis == axis_at else 1 for axis in range(len(dims))])
    return factor_of


def picks_of(stream_key, rows, count, top, lift):
    ranking = jax.random.permutation(jax.random.fold_in(stream_key, 1), count)
    favour = ranking
    for power in range(3):
        favour = favour * favour // count
    favour = favour * lift // count
    chance = jax.random.randint(jax.random.fold_in(stream_key, 2), (rows, count), 0, 4096) + favour
    fixed_rows = jax.random.permutation(jax.random.fold_in(stream_key, 3), rows)[jnp.arange(count) % rows]
    chance = jnp.where(jnp.arange(rows)[:, None] == fixed_rows[None, :], 1 << 14, chance)
    priority = chance * count + jnp.arange(count)
    return lax.top_k(priority.astype(jnp.int32), top)[1].astype(jnp.int32)


def gaussian(key, dims, scale, reach, shards=(), kind=jnp.bfloat16):
    result = jax.random.normal(key, dims, jnp.float32) * scale
    if len(shards) > 0:
        result = levels(key, dims, shards, -0.22, 0.18) * result
    return jnp.clip(result, min=-reach, max=reach).astype(kind)


def setup_inputs(seed: int = 0) -> dict:
    streams_of = jax.random.split(jax.random.key(seed), 17)
    tokens = gaussian(streams_of[0], (TOKENS, D), 1.0, 6.0, ((0, 8),))
    grad_out = gaussian(streams_of[1], (TOKENS, D), 1.0, 6.0, ((0, 8),))
    norm1_gain = jnp.clip(1.0 + 0.1 * jax.random.normal(streams_of[2], (D,), jnp.float32), 0.5, 1.5)
    attn_router = gaussian(streams_of[3], (D, EA), (D // 4) ** -0.5, 0.25)
    attn_routes = picks_of(streams_of[4], TOKENS, EA, TOPK, 2048)
    attn_order = jax.vmap(lambda own: jax.random.permutation(own, PAIRS))(jax.random.split(streams_of[5], N_EP)).reshape((N_EP, PAIRS)).astype(jnp.int32)
    w_query = gaussian(streams_of[6], (EA, D, HEADS * HD), D ** -0.5, 0.125, ((1, 8), (2, 4)))
    w_kv = gaussian(streams_of[7], (2, D, KVH * HD), D ** -0.5, 0.125, ((1, 8), (2, 4)))
    w_attn_out = gaussian(streams_of[8], (EA, D, HEADS * HD), (max(HEADS * HD * 16 // GTOK, 1)) ** -0.5, 0.75, ((1, 8), (2, 4)))
    norm2_gain = jnp.clip(1.0 + 0.1 * jax.random.normal(streams_of[9], (D,), jnp.float32), 0.5, 1.5)
    mlp_router = gaussian(streams_of[10], (D, EM), (D // 4) ** -0.5, 0.25)
    mlp_routes = picks_of(streams_of[11], TOKENS, EM, TOPK, 2048)
    mlp_order = jax.vmap(lambda own: jax.random.permutation(own, PAIRS))(jax.random.split(streams_of[12], N_EP)).reshape((N_EP, PAIRS)).astype(jnp.int32)
    w_gate = gaussian(streams_of[13], (D, EM * FF), D ** -0.5, 0.125, ((1, 32),))
    w_up = gaussian(streams_of[14], (D, EM * FF), D ** -0.5, 0.125, ((1, 32),))
    w_down = gaussian(streams_of[15], (D, EM * FF), FF ** -0.5, 0.078125, ((1, 32),))
    return {"tokens": tokens, "grad_out": grad_out, "norm1_gain": norm1_gain, "attn_router": attn_router, "attn_routes": attn_routes, "attn_order": attn_order, "w_query": w_query, "w_kv": w_kv, "w_attn_out": w_attn_out, "norm2_gain": norm2_gain, "mlp_router": mlp_router, "mlp_routes": mlp_routes, "mlp_order": mlp_order, "w_gate": w_gate, "w_up": w_up, "w_down": w_down}


epsilon = 1e-06
rope_base = 10000.0
masked_value = -1e+30
highest = lax.Precision.HIGHEST

@jax.custom_vjp
def low(v):
    return lax.optimization_barrier(v.astype(jnp.bfloat16)).astype(jnp.float32)

@jax.custom_vjp
def low_back(v):
    return v

def low_keep(v):
    return (low(v), None)

def low_pass(kept, grad):
    return (grad,)

def back_keep(v):
    return (v, None)

def back_low(kept, grad):
    return (low(grad),)
low.defvjp(low_keep, low_pass)
low_back.defvjp(back_keep, back_low)

def slot_tables(routes, order_list, experts, capacity):
    pair_count = routes.shape[0] * routes.shape[1]
    pair_expert = routes.reshape(pair_count).astype(jnp.int32)
    ordered = order_list.reshape(pair_count).astype(jnp.int32)
    ordered_expert = jnp.take(pair_expert, ordered)
    onehot = (ordered_expert[:, None] == jnp.arange(experts, dtype=jnp.int32)[None, :]).astype(jnp.int32)
    ranked = lax.optimization_barrier(jnp.sum((jnp.cumsum(onehot, axis=0) - 1) * onehot, axis=1)).astype(jnp.int32)
    slot_of_pair = jnp.zeros((pair_count,), jnp.int32).at[ordered].set(ranked)
    keep_pair = slot_of_pair < capacity
    pair_dest = jnp.where(keep_pair, pair_expert * capacity + slot_of_pair, experts * capacity).astype(jnp.int32)
    owner_token = (jnp.arange(pair_count, dtype=jnp.int32) // routes.shape[1]).astype(jnp.int32)
    slot_token = jnp.zeros((experts * capacity + 1,), jnp.int32).at[pair_dest].set(owner_token)[:experts * capacity]
    filled = jnp.zeros((experts * capacity + 1,), jnp.float32).at[pair_dest].set(1.0)[:experts * capacity]
    return (pair_dest, keep_pair.astype(jnp.float32), slot_token, filled)

def rope_tables(positions, head_size):
    half_size = head_size // 2
    frequency = rope_base ** (-(jnp.arange(half_size, dtype=jnp.float32) * 2.0) / head_size)
    angles = positions.astype(jnp.float32)[:, None] * frequency[None, :]
    return (jnp.cos(angles), jnp.sin(angles))

def rotate(values, cosine, sine_table):
    half_size = values.shape[-1] // 2
    first_half = values[..., :half_size]
    second_half = values[..., half_size:]
    cos_rows = cosine[:, None, :]
    sin_rows = sine_table[:, None, :]
    return jnp.concatenate([first_half * cos_rows - second_half * sin_rows, second_half * cos_rows + first_half * sin_rows], axis=-1)

def route_gates(logits, routes):
    onehot = (routes[:, :, None] == jnp.arange(logits.shape[1], dtype=jnp.int32)[None, None, :]).astype(jnp.float32)
    chosen = lax.optimization_barrier(jnp.sum(onehot * logits[:, None, :], axis=2))
    exponent = jnp.exp(chosen - lax.optimization_barrier(jnp.max(chosen, axis=1, keepdims=True)))
    return exponent / lax.optimization_barrier(jnp.sum(exponent, axis=1, keepdims=True))

def pair_rows(slot_rows, pair_dest):
    padded = jnp.concatenate([slot_rows, jnp.zeros((1, slot_rows.shape[1]), slot_rows.dtype)], axis=0)
    return jnp.take(padded, pair_dest, axis=0)

def rms_norm(values, gain_vec):
    return values * lax.rsqrt(lax.optimization_barrier(jnp.mean(values * values, axis=-1, keepdims=True)) + epsilon) * gain_vec

def gather_slots(group_rows, slot_token, filled):
    return jnp.take(group_rows, slot_token, axis=0) * filled[:, None]

def reference(tokens, grad_out, norm1_gain, attn_router, attn_routes, attn_order, w_query, w_kv, w_attn_out, norm2_gain, mlp_router, mlp_routes, mlp_order, w_gate, w_up, w_down):
    a_routes = attn_routes.reshape(N_EP, GTOK, TOPK)
    m_routes = mlp_routes.reshape(N_EP, GTOK, TOPK)
    a_dest, a_keep, a_table, a_filled = jax.vmap(lambda route_rows, order_rows: slot_tables(route_rows, order_rows, EA, ACAP))(a_routes, attn_order)
    m_dest, m_keep, m_table, m_filled = jax.vmap(lambda route_rows, order_rows: slot_tables(route_rows, order_rows, EM, MCAP))(m_routes, mlp_order)
    token_index = jnp.arange(GTOK, dtype=jnp.int32)
    tail_index = jnp.maximum(token_index - PROMPT, 0)
    positions = jnp.where(token_index < PROMPT, token_index, PROMPT + tail_index % CLEN).astype(jnp.int32)
    segment = jnp.where(token_index < PROMPT, 0, 1 + tail_index // CLEN).astype(jnp.int32)
    cosine, sine_table = rope_tables(positions, HD)
    score_scale = 1.0 / math.sqrt(HD)
    slot_count = EA * ACAP

    def attend(xn_group, slot_token, filled, query_w, kv_w, out_w):
        slot_in = gather_slots(xn_group, slot_token, filled).reshape(EA, ACAP, D)
        query_pre = low_back(jnp.einsum('ecd,edj->ecj', slot_in, query_w, precision=highest))
        query = low(rotate(query_pre.reshape(slot_count, HEADS, HD), jnp.take(cosine, slot_token, axis=0), jnp.take(sine_table, slot_token, axis=0)))
        kv_pre = jnp.einsum('td,kdj->ktj', xn_group, kv_w, precision=highest)
        key_rot = low(rotate(low_back(kv_pre[0]).reshape(GTOK, KVH, HD), cosine, sine_table))
        value_rows = low(low_back(kv_pre[1])).reshape(GTOK, KVH, HD)
        scores = low_back(jnp.einsum('rhk,thk->hrt', query, key_rot, precision=highest) * score_scale)
        query_segment = jnp.take(segment, slot_token)
        allowed = (token_index[None, :] <= slot_token[:, None]) & ((segment[None, :] == 0) | (segment[None, :] == query_segment[:, None]))
        masked = jnp.where(allowed[None, :, :], scores, masked_value)
        exponent = jnp.exp(masked - lax.optimization_barrier(jnp.max(masked, axis=2, keepdims=True)))
        probs = exponent / lax.optimization_barrier(jnp.sum(exponent, axis=2, keepdims=True))
        attn_o = low(low_back(jnp.einsum('hrt,thk->rhk', low(probs), value_rows, precision=highest)))
        slot_out = low_back(jnp.einsum('ecj,edj->ecd', attn_o.reshape(EA, ACAP, HEADS * HD), out_w, precision=highest))
        return slot_out.reshape(slot_count, D)

    def forward(tok, gain_one, router_a, query_w, kv_w, out_w, gain_two, router_m, gate_w, up_w, down_w):
        x_rows = tok.reshape(N_EP, GTOK, D)
        xn = low(rms_norm(x_rows, gain_one))
        logits_a = low_back(jnp.einsum('gtd,de->gte', xn, router_a, precision=highest))
        gate_a = jax.vmap(route_gates)(logits_a, a_routes)

        def attend_group(packed):
            xn_group, slot_token, filled = packed
            return attend(xn_group, slot_token, filled, query_w, kv_w, out_w)
        slot_out = lax.map(jax.checkpoint(attend_group), (xn, a_table, a_filled))
        pair_out = jax.vmap(pair_rows)(slot_out, a_dest)
        weight_a = gate_a.reshape(N_EP, PAIRS) * a_keep
        attn_branch = lax.optimization_barrier(jnp.sum((pair_out * weight_a[..., None]).reshape(N_EP, GTOK, TOPK, D), axis=2))
        hidden_in = x_rows + attn_branch
        hn = low(rms_norm(hidden_in, gain_two))
        logits_m = low_back(jnp.einsum('gtd,de->gte', hn, router_m, precision=highest))
        gate_m = jax.vmap(route_gates)(logits_m, m_routes)
        slots_in = jax.vmap(gather_slots)(hn, m_table, m_filled)
        expert_in = jnp.transpose(slots_in.reshape(N_EP, EM, MCAP, D), (1, 0, 2, 3)).reshape(EM, N_EP * MCAP, D)

        def column_blocks(weight):
            return jnp.transpose(weight.reshape(D, EM, SLICES, FS), (1, 0, 2, 3))

        def expert_group(packed):
            rows_in, gate_e, up_e, down_e = packed
            copies = jax.vmap(low_back)(jnp.broadcast_to(rows_in, (SLICES,) + rows_in.shape))
            gate_pre = low_back(jnp.einsum('srd,dsf->srf', copies, gate_e, precision=highest))
            up_pre = low_back(jnp.einsum('srd,dsf->srf', copies, up_e, precision=highest))
            act_rows = low(gate_pre * jax.nn.sigmoid(gate_pre) * up_pre)
            parts = low(jnp.einsum('srf,dsf->srd', act_rows, down_e, precision=highest))
            return low_back(lax.optimization_barrier(jnp.sum(parts, axis=0)))
        expert_out = lax.map(jax.checkpoint(expert_group), (expert_in, column_blocks(gate_w), column_blocks(up_w), column_blocks(down_w)))
        expert_out = jnp.transpose(expert_out.reshape(EM, N_EP, MCAP, D), (1, 0, 2, 3)).reshape(N_EP, EM * MCAP, D)
        pair_mlp = jax.vmap(pair_rows)(expert_out, m_dest)
        weight_m = gate_m.reshape(N_EP, PAIRS) * m_keep
        mlp_branch = lax.optimization_barrier(jnp.sum((pair_mlp * weight_m[..., None]).reshape(N_EP, GTOK, TOPK, D), axis=2))
        return (hidden_in + mlp_branch).reshape(N_EP * GTOK, D)
    primal = (tokens.astype(jnp.float32), norm1_gain.astype(jnp.float32), attn_router.astype(jnp.float32), w_query.astype(jnp.float32), w_kv.astype(jnp.float32), w_attn_out.astype(jnp.float32), norm2_gain.astype(jnp.float32), mlp_router.astype(jnp.float32), w_gate.astype(jnp.float32), w_up.astype(jnp.float32), w_down.astype(jnp.float32))
    layer_value, pullback = jax.vjp(forward, *primal)
    grads = pullback(grad_out.astype(jnp.float32))
    return (layer_value.astype(jnp.bfloat16), grads[0], grads[1], grads[2], grads[3], grads[4], grads[5], grads[6], grads[7], grads[8], grads[9], grads[10])
```

```python
import math

import jax
import jax.numpy as jnp
from jax import lax
from jax.sharding import PartitionSpec as P

HD = 128
PROMPT = 256
CLEN = 128
EPS = 1e-06
ROPE_BASE = 10000.0
MASKED = -1e30
BF = jnp.bfloat16
F32 = jnp.float32
RING_MAX = 8


def mm(eq, a, b):
    return jnp.einsum(eq, a, b, preferred_element_type=F32)


def after(value, *deps):
    return lax.optimization_barrier((value,) + deps)[0]


def ring_index(p, n):
    h = p // (n // 2)
    return 2 * p * (1 - h) + h * (2 * (n - 1 - p) + 1)


def ring_pos(n):
    i = lax.axis_index("ep")
    h = i // 2
    return h + (i % 2) * (n - 1 - 2 * h)


def ring_perms(n):
    fw = [(ring_index(p, n), ring_index((p + 1) % n, n)) for p in range(n)]
    return fw, [(b, a) for a, b in fw]


def ring_gather(x, dim):
    n = lax.axis_size("ep")
    if n > RING_MAX:
        full = lax.all_gather(x, "ep", axis=dim, tiled=True)
        return full, (full,)
    fw, bw = ring_perms(n)
    pos = ring_pos(n)
    half = x.shape[0] // 2
    a, b = x[:half], x[half:]
    shape = list(a.shape)
    size = shape[dim]
    shape[dim] = size * n
    out_a, out_b = jnp.zeros(shape, x.dtype), jnp.zeros(shape, x.dtype)
    me = lax.axis_index("ep")
    out_a = lax.dynamic_update_slice_in_dim(out_a, a, me * size, dim)
    out_b = lax.dynamic_update_slice_in_dim(out_b, b, me * size, dim)
    for s in range(1, n):
        a = lax.ppermute(a, "ep", fw)
        b = lax.ppermute(b, "ep", bw)
        src_a = ring_index((pos + n - s) % n, n)
        src_b = ring_index((pos + s) % n, n)
        out_a = lax.dynamic_update_slice_in_dim(out_a, a, src_a * size, dim)
        out_b = lax.dynamic_update_slice_in_dim(out_b, b, src_b * size, dim)
    return jnp.concatenate([out_a, out_b], axis=0), (a, b)


def ring_scatter(parts):
    n = lax.axis_size("ep")
    if n > RING_MAX:
        return lax.psum_scatter(parts.astype(BF), "ep", scatter_dimension=1).astype(F32)
    fw, bw = ring_perms(n)
    pos = ring_pos(n)
    acc = [None, None]
    for s in range(n):
        for k, (perm, sign) in enumerate(((fw, n - 1 - s), (bw, s + 1))):
            blk = ring_index((pos + sign) % n, n)
            term = lax.dynamic_index_in_dim(parts[k], blk, 0, keepdims=False)
            if s > 0:
                term = term + lax.ppermute(acc[k], "ep", perm).astype(F32)
            acc[k] = term if s == n - 1 else term.astype(BF)
    return jnp.stack(acc)


CORE = [(0, 1), (1, 0), (2, 3), (3, 2)]
CROSS = [(0, 2), (2, 0), (1, 3), (3, 1)]


def ws_gather(q):
    w = lax.axis_index("ws")
    x, c = w // 2, w % 2
    rows, cols = q.shape
    other = lax.ppermute(q, "ws", CROSS)
    mine = jnp.where(x == 0, jnp.stack([q, other]), jnp.stack([other, q]))
    peer = lax.ppermute(mine, "ws", CORE)
    both = jnp.where(c == 0, jnp.stack([mine, peer], 1), jnp.stack([peer, mine], 1))
    return jnp.transpose(both.reshape(4, rows, cols), (1, 0, 2)).reshape(rows, 4 * cols)


def ws_scatter(p):
    w = lax.axis_index("ws")
    x, c = w // 2, w % 2
    rows, cols = p.shape[0], p.shape[1] // 4
    p = p.reshape(rows, 2, 2, cols)
    pick = lambda v, i, d: lax.dynamic_index_in_dim(v, i, d, keepdims=False)
    got = lax.ppermute(pick(p, 1 - c, 2).astype(BF), "ws", CORE)
    p = pick(p, c, 2) + got.astype(F32)
    got = lax.ppermute(pick(p, 1 - x, 1).astype(BF), "ws", CROSS)
    return pick(p, x, 1) + got.astype(F32)


def slot_dest(routes, order, experts, capacity):
    pairs = routes.shape[0] * 2
    expert = routes.reshape(pairs)
    index = jnp.arange(pairs, dtype=jnp.int32)
    place = jnp.sum(
        jnp.where(order.reshape(1, pairs) == index[:, None], index[None, :], 0), axis=1
    )
    ahead = (place[None, :] < place[:, None]) & (expert[None, :] == expert[:, None])
    slot = jnp.sum(ahead.astype(jnp.int32), axis=1)
    dest = jnp.where(slot < capacity, expert * capacity + slot, -1)
    return dest.reshape(-1, 2)


def slot_onehot(dest, slots):
    index = jnp.arange(slots, dtype=jnp.int32)[:, None]
    return ((dest[None, :, 0] == index) | (dest[None, :, 1] == index)).astype(BF)


def slot_values(dest, values, slots):
    index = jnp.arange(slots, dtype=jnp.int32)[:, None]
    zero = jnp.zeros((), values.dtype)
    return jnp.sum(
        jnp.where(dest[None, :, 0] == index, values[None, :, 0], zero)
        + jnp.where(dest[None, :, 1] == index, values[None, :, 1], zero),
        axis=1,
    )


def router_gates(logits, hot):
    top = jnp.max(jnp.where(hot, logits, MASKED), axis=1, keepdims=True)
    e = jnp.where(hot, jnp.exp(logits - top), 0.0)
    return e / jnp.sum(e, axis=1, keepdims=True)


def chosen(gates, routes):
    index = jnp.arange(gates.shape[1], dtype=jnp.int32)
    return jnp.sum(jnp.where(routes[:, :, None] == index, gates[:, None, :], 0.0), axis=2)


def rotate(v, cos, sin):
    h = v.shape[-1] // 2
    a, b = v[..., :h], v[..., h:]
    cos, sin = cos[:, None, :], sin[:, None, :]
    return jnp.concatenate([a * cos - b * sin, b * cos + a * sin], axis=-1)


def angles(positions):
    half = HD // 2
    freq = ROPE_BASE ** (-(jnp.arange(half, dtype=F32) * 2.0) / HD)
    a = positions.astype(F32)[:, None] * freq[None, :]
    return jnp.cos(a), jnp.sin(a)


def place_of(index):
    tail = jnp.maximum(index - PROMPT, 0)
    position = jnp.where(index < PROMPT, index, PROMPT + tail % CLEN)
    segment = jnp.where(index < PROMPT, 0, 1 + tail // CLEN)
    return position, segment


def per_device(
    tokens,
    grad_out,
    norm1_gain,
    attn_router,
    attn_routes,
    attn_order,
    w_query,
    w_kv,
    w_attn_out,
    norm2_gain,
    mlp_router,
    mlp_routes,
    mlp_order,
    w_gate,
    w_up,
    w_down,
):
    glen, width = tokens.shape
    n = lax.axis_size("ep")
    nw = lax.axis_size("ws")
    ep, ws = lax.axis_index("ep"), lax.axis_index("ws")
    ea, em = attn_router.shape[1], mlp_router.shape[1]
    acap, mcap = 2 * glen // ea, 2 * glen // em
    owners = n // em
    slots, mslots = ea * acap, em * mcap
    heads = w_query.shape[2] // HD
    block = w_query.shape[1]
    quarter = width // nw
    scale = 1.0 / math.sqrt(HD)
    cut = lambda v: lax.dynamic_slice_in_dim(v, ws * quarter, quarter, v.ndim - 1)
    cut0 = lambda v: lax.dynamic_slice_in_dim(v, ws * quarter, quarter, 0)

    full_kv, tail = ring_gather(w_kv, 1)
    full_query, tail = ring_gather(after(w_query, *tail), 1)
    full_out, tail = ring_gather(after(w_attn_out, *tail), 1)

    a_dest = slot_dest(attn_routes, attn_order, ea, acap)
    m_dest = slot_dest(mlp_routes, mlp_order, em, mcap)
    a_sel = slot_onehot(a_dest, slots)
    m_sel = slot_onehot(m_dest, mslots)
    hot_index = jnp.arange(ea, dtype=jnp.int32)
    a_hot = jnp.any(attn_routes[:, :, None] == hot_index, axis=1)
    m_hot = jnp.any(mlp_routes[:, :, None] == jnp.arange(em, dtype=jnp.int32), axis=1)
    token_index = jnp.arange(glen, dtype=jnp.int32)
    position, segment = place_of(token_index)
    a_token = slot_values(a_dest, jnp.stack([token_index, token_index], 1), slots)
    slot_position, slot_segment = place_of(a_token)

    dy_q = cut(grad_out)
    dy_slots = mm("st,td->sd", m_sel, dy_q).astype(BF)
    send = lambda v: lax.all_to_all(
        jnp.repeat(v.reshape(em, mcap, quarter), owners, axis=0), "ep", 0, 0, tiled=True
    )
    dy_rows = ws_gather(send(dy_slots).reshape(n * mcap, quarter))
    other = slot_values(m_dest, mlp_routes[:, ::-1], mslots).reshape(em, mcap)
    other = lax.all_to_all(jnp.repeat(other, owners, axis=0), "ep", 0, 0, tiled=True).reshape(-1)
    dy_down = mm("rd,df->rf", dy_rows, w_down)

    x = tokens.astype(F32)
    inv1 = lax.rsqrt(jnp.mean(x * x, axis=1, keepdims=True) + EPS)
    xn = (x * inv1 * norm1_gain).astype(BF)
    a_logits = mm("td,de->te", xn, attn_router)
    a_gate = router_gates(a_logits, a_hot)
    a_slot_gate = slot_values(a_dest, chosen(a_gate, attn_routes), slots)
    slot_in = mm("st,td->sd", a_sel, xn).astype(BF).reshape(ea, acap, width)
    q_pre = mm("ecd,edj->ecj", slot_in, full_query)
    q_cos, q_sin = angles(slot_position)
    cos, sin = angles(position)
    q = rotate(q_pre.reshape(slots, heads, HD), q_cos, q_sin).astype(BF)
    kv = mm("td,kdj->ktj", xn, full_kv)
    k = rotate(kv[0].reshape(glen, heads, HD), cos, sin).astype(BF)
    v = kv[1].reshape(glen, heads, HD).astype(BF)
    allowed = (token_index[None, :] <= a_token[:, None]) & (
        (segment[None, :] == 0) | (segment[None, :] == slot_segment[:, None])
    )

    def scores_of(q, k):
        return jnp.where(allowed[None], mm("rhk,thk->hrt", q, k) * scale, MASKED)

    scores = scores_of(q, k)
    peak = jnp.max(scores, axis=2, keepdims=True)
    log_total = peak + jnp.log(jnp.sum(jnp.exp(scores - peak), axis=2, keepdims=True))
    probs = jnp.exp(scores - log_total)
    attn_o = mm("hrt,thk->rhk", probs.astype(BF), v).reshape(slots, heads * HD)
    gated_o = (attn_o * a_slot_gate[:, None]).astype(BF).reshape(ea, acap, heads * HD)
    slot_out = mm("ecj,edj->ecd", gated_o, full_out).astype(BF).reshape(slots, width)
    branch = ws_scatter(mm("st,sd->td", a_sel, slot_out))

    x_q = cut(tokens).astype(F32)
    hidden = x_q + branch
    inv2 = lax.rsqrt(
        lax.psum(jnp.sum(hidden * hidden, axis=1, keepdims=True), "ws") / width + EPS
    )
    unit2 = hidden * inv2
    gain2 = cut0(norm2_gain)
    hn = (unit2 * gain2).astype(BF)
    router_q = lax.dynamic_slice_in_dim(mlp_router, ws * quarter, quarter, 0)
    hn_slots = mm("st,td->sd", m_sel, hn).astype(BF)
    rows = ws_gather(send(hn_slots).reshape(n * mcap, quarter))
    slots_travel = n * slots <= ea * width
    if slots_travel:
        all_o, tail = ring_gather(after(gated_o, rows), 1)
    m_logits = lax.psum(mm("td,de->te", hn, router_q), "ws")
    m_gate = router_gates(m_logits, m_hot)
    m_slot_gate = slot_values(m_dest, chosen(m_gate, mlp_routes), mslots)

    row_logits = mm("rd,de->re", rows, mlp_router)
    expert_index = jnp.arange(em, dtype=jnp.int32)
    own = jnp.sum(jnp.where(expert_index == ep // owners, row_logits, 0.0), axis=1)
    oth = jnp.sum(jnp.where(expert_index == other[:, None], row_logits, 0.0), axis=1)
    top = jnp.maximum(own, oth)
    own, oth = jnp.exp(own - top), jnp.exp(oth - top)
    row_gate = (own / (own + oth))[:, None]
    gate_pre = mm("rd,df->rf", rows, w_gate)
    up_pre = mm("rd,df->rf", rows, w_up)
    sig = jax.nn.sigmoid(gate_pre)
    act = gate_pre * sig * up_pre
    d_act = dy_down * row_gate
    d_gate = (d_act * up_pre * sig * (1.0 + gate_pre * (1.0 - sig))).astype(BF)
    d_up = (d_act * gate_pre * sig).astype(BF)
    part = mm("rf,df->rd", act.astype(BF), w_down)
    d_part = mm("rf,df->rd", d_gate, w_gate) + mm("rf,df->rd", d_up, w_up)

    def give_back(v):
        v = ws_scatter(v).astype(BF).reshape(n, mcap, quarter)
        v = lax.all_to_all(v, "ep", 0, 0, tiled=True)
        if owners > 1:
            v = jnp.sum(v.astype(F32).reshape(em, owners, mcap, quarter), axis=1).astype(BF)
        return v.reshape(mslots, quarter)

    expert_out = give_back(part)
    d_rows = give_back(d_part)
    grad_gate = mm("rd,rf->df", rows, d_gate)
    grad_up = mm("rd,rf->df", rows, d_up)
    grad_down = mm("rd,rf->df", dy_rows, (act * row_gate).astype(BF))

    mlp_branch = mm("st,sd->td", m_sel, (expert_out.astype(F32) * m_slot_gate[:, None]).astype(BF))
    layer_out = ws_gather((hidden + mlp_branch).astype(BF))

    def router_back(sel, slot_dgate, gates, experts):
        terms = sel.reshape(experts, -1, glen).astype(F32) * slot_dgate.reshape(experts, -1, 1)
        dgate = jnp.sum(terms, axis=1).T
        return (gates * (dgate - jnp.sum(gates * dgate, axis=1, keepdims=True))).astype(BF)

    m_dgate = lax.psum(
        jnp.sum(dy_slots.astype(F32) * expert_out.astype(F32), axis=1, keepdims=True), "ws"
    )
    d_m_logits = router_back(m_sel, m_dgate, m_gate, em)
    grad_mlp_router = mm("td,te->ed", hn, d_m_logits)
    d_hn = mm("st,sd->td", m_sel, d_rows) + mm("te,de->td", d_m_logits, router_q)
    grad_norm2 = jnp.sum(d_hn * unit2, axis=0, keepdims=True)
    w2 = d_hn * gain2
    mean2 = lax.psum(jnp.sum(w2 * unit2, axis=1, keepdims=True), "ws") / width
    d_hidden = dy_q.astype(F32) + inv2 * (w2 - unit2 * mean2)
    d_hid = ws_gather(d_hidden.astype(BF))

    dh_slots = mm("st,td->sd", a_sel, d_hid).astype(BF).reshape(ea, acap, width)
    raw_do = mm("ecd,edj->ecj", dh_slots, full_out).reshape(slots, heads * HD)
    a_dgate = lax.psum(jnp.sum(raw_do * attn_o, axis=1, keepdims=True), "ws")
    d_o = (raw_do * a_slot_gate[:, None]).astype(BF).reshape(slots, heads, HD)
    probs2 = jnp.exp(scores_of(q, k) - log_total)
    d_probs = mm("rhk,thk->hrt", d_o, v)
    d_scores = (
        probs2 * (d_probs - jnp.sum(probs2 * d_probs, axis=2, keepdims=True))
    ).astype(BF)
    d_q = rotate(mm("hrt,thk->rhk", d_scores, k) * scale, q_cos, -q_sin)
    d_q = d_q.reshape(ea, acap, heads * HD).astype(BF)
    d_k = rotate(mm("hrt,rhk->thk", d_scores, q) * scale, cos, -sin).astype(BF)
    d_v = mm("hrt,rhk->thk", probs2.astype(BF), d_o).astype(BF)
    d_kv = jnp.stack([d_k, d_v]).reshape(2, glen, heads * HD)
    if slots_travel:
        all_dq, tail = ring_gather(d_q, 1)
    kv_terms = mm("td,ktj->kdj", xn, d_kv)
    grad_kv = ring_scatter(kv_terms.reshape(2, n, block, heads * HD))

    d_slot_in = mm("ecj,edj->ecd", d_q, full_query).astype(BF).reshape(slots, width)
    d_xn = ws_scatter(mm("st,sd->td", a_sel, d_slot_in) + mm("ktj,kdj->td", d_kv, full_kv))
    d_a_logits = router_back(a_sel, a_dgate, a_gate, ea)
    arouter_q = lax.dynamic_slice_in_dim(attn_router, ws * quarter, quarter, 0)
    xn_q = cut(xn)
    grad_attn_router = mm("td,te->ed", xn_q, d_a_logits)
    d_xn = d_xn + mm("te,de->td", d_a_logits, arouter_q)
    unit1 = x_q * inv1
    grad_norm1 = jnp.sum(d_xn * unit1, axis=0, keepdims=True)
    w1 = d_xn * cut0(norm1_gain)
    mean1 = lax.psum(jnp.sum(w1 * unit1, axis=1, keepdims=True), "ws") / width
    grad_tokens = d_hidden + inv1 * (w1 - unit1 * mean1)
    grad_tokens = ws_gather(grad_tokens.astype(BF)).astype(F32)

    def spread(v):
        rows_w = glen // nw
        mine = lax.dynamic_slice_in_dim(v, ws * rows_w, rows_w, 0)
        mine = jnp.transpose(mine.reshape(rows_w, n, block), (1, 0, 2))
        got = lax.all_to_all(mine, "ep", 0, 0, tiled=True)
        return lax.all_gather(got, "ws", axis=1, tiled=True)

    if slots_travel:
        all_dest = lax.all_gather(a_dest, "ep")
        all_sel = jax.vmap(lambda d: slot_onehot(d, slots))(all_dest)
        x_slots = mm("gst,gtd->gsd", all_sel, spread(xn)).astype(BF)
        h_slots = mm("gst,gtd->gsd", all_sel, spread(d_hid)).astype(BF)
        by_expert = lambda v: jnp.transpose(v.reshape(n, ea, acap, block), (1, 0, 2, 3)).reshape(
            ea, n * acap, block
        )
        grad_query = mm("esd,esj->edj", by_expert(x_slots), all_dq)
        grad_attn_out = mm("esd,esj->edj", by_expert(h_slots), all_o)
    else:
        scatter = lambda g: lax.psum_scatter(g.astype(BF), "ep", scatter_dimension=1, tiled=True)
        grad_query = scatter(mm("ecd,ecj->edj", slot_in, d_q)).astype(F32)
        grad_attn_out = scatter(mm("ecd,ecj->edj", dh_slots, gated_o)).astype(F32)

    def collect(norm, router):
        rows_q = lax.psum(jnp.concatenate([norm, router], axis=0), "ep")
        full = lax.all_gather(rows_q, "ws", axis=1, tiled=True)
        return full[0], full[1:].T

    grad_norm1, grad_attn_router = collect(grad_norm1, grad_attn_router)
    grad_norm2, grad_mlp_router = collect(grad_norm2, grad_mlp_router)
    return (
        layer_out,
        grad_tokens,
        grad_norm1,
        grad_attn_router,
        grad_query,
        grad_kv,
        grad_attn_out,
        grad_norm2,
        grad_mlp_router,
        grad_gate,
        grad_up,
        grad_down,
    )


def solution(mesh):
    rows, wide = P("ep", None), P(None, ("ep", "ws"))
    attn = P(None, "ep", "ws")
    return jax.shard_map(
        per_device,
        mesh=mesh,
        in_specs=(rows, rows, P(), P(), rows, rows, attn, attn, attn, P(), P(), rows, rows)
        + (wide,) * 3,
        out_specs=(rows, rows, P(), P(), attn, attn, attn, P(), P()) + (wide,) * 3,
        check_vma=False,
    )
```

```python
import functools
import math

import jax
import jax.numpy as jnp
from jax import lax
from jax.experimental import pallas as pl
from jax.experimental.pallas import tpu as pltpu
from jax.sharding import PartitionSpec as P

HD = 128
PROMPT = 256
CLEN = 128
EPS = 1e-06
ROPE_BASE = 10000.0
MASKED = -1e30
BF = jnp.bfloat16
F32 = jnp.float32
RING_MAX = 8


def mm(eq, a, b):
    return jnp.einsum(eq, a, b, preferred_element_type=F32)


def after(value, *deps):
    return lax.optimization_barrier((value,) + deps)[0]


def ring_index(p, n):
    h = p // (n // 2)
    return 2 * p * (1 - h) + h * (2 * (n - 1 - p) + 1)


def ring_pos(n):
    i = lax.axis_index("ep")
    h = i // 2
    return h + (i % 2) * (n - 1 - 2 * h)


def ring_perms(n):
    fw = [(ring_index(p, n), ring_index((p + 1) % n, n)) for p in range(n)]
    return fw, [(b, a) for a, b in fw]


def ring_gather(x, dim):
    n = lax.axis_size("ep")
    half = x.shape[0] // 2
    if n > RING_MAX:
        full = lax.all_gather(x, "ep", axis=dim, tiled=True)
        return (full[:half], full[half:]), (full,)
    fw, bw = ring_perms(n)
    pos = ring_pos(n)
    a, b = x[:half], x[half:]
    shape = list(a.shape)
    size = shape[dim]
    shape[dim] = size * n
    out_a, out_b = jnp.zeros(shape, x.dtype), jnp.zeros(shape, x.dtype)
    me = lax.axis_index("ep")
    out_a = lax.dynamic_update_slice_in_dim(out_a, a, me * size, dim)
    out_b = lax.dynamic_update_slice_in_dim(out_b, b, me * size, dim)
    for s in range(1, n):
        a = lax.ppermute(a, "ep", fw)
        b = lax.ppermute(b, "ep", bw)
        src_a = ring_index((pos + n - s) % n, n)
        src_b = ring_index((pos + s) % n, n)
        out_a = lax.dynamic_update_slice_in_dim(out_a, a, src_a * size, dim)
        out_b = lax.dynamic_update_slice_in_dim(out_b, b, src_b * size, dim)
    return (out_a, out_b), (a, b)


class GatherRing:
    def __init__(self, x):
        half = x.shape[0] // 2
        self.moving = [x[:half], x[half:]]
        self.got = [[self.moving[0]], [self.moving[1]]]

    def hop(self):
        perms = ring_perms(lax.axis_size("ep"))
        self.moving = [lax.ppermute(v, "ep", p) for v, p in zip(self.moving, perms)]
        for k in range(2):
            self.got[k].append(self.moving[k])

    def settle(self, values):
        self.moving = list(values)
        for k in range(2):
            self.got[k][-1] = self.moving[k]


def lock(rings, *values):
    flat = [m for r in rings for m in r.moving] + list(values)
    flat = list(lax.optimization_barrier(tuple(flat)))
    for r in rings:
        r.settle([flat.pop(0), flat.pop(0)])
    return flat


def hop(rings):
    for r in rings:
        r.hop()


CORE = [(0, 1), (1, 0), (2, 3), (3, 2)]
CROSS = [(0, 2), (2, 0), (1, 3), (3, 1)]


def ws_stack(q):
    w = lax.axis_index("ws")
    x, c = w // 2, w % 2
    other = lax.ppermute(q, "ws", CROSS)
    mine = jnp.where(x == 0, jnp.stack([q, other]), jnp.stack([other, q]))
    peer = lax.ppermute(mine, "ws", CORE)
    both = jnp.where(c == 0, jnp.stack([mine, peer], 1), jnp.stack([peer, mine], 1))
    return both.reshape((4,) + q.shape)


def ws_gather(q):
    rows, cols = q.shape
    return jnp.transpose(ws_stack(q), (1, 0, 2)).reshape(rows, 4 * cols)


def ws_to_core(p):
    w = lax.axis_index("ws")
    x, c = w // 2, w % 2
    cols = p.shape[1] // 4
    take = lambda q: lax.dynamic_slice_in_dim(p, q * cols, cols, 1)
    far = lax.ppermute(take((1 - x) * 2 + 1 - c), "ws", CORE).astype(F32)
    near = lax.ppermute(take(x * 2 + 1 - c), "ws", CORE).astype(F32)
    far = (take((1 - x) * 2 + c).astype(F32) + far).astype(BF)
    return far, take(x * 2 + c).astype(F32) + near


def ws_to_cross(far, near):
    return near + lax.ppermute(far, "ws", CROSS).astype(F32)


MESH_ID = pl.DeviceIdType.MESH
VMEM_CAP = 60 * 1024 * 1024


def any_spec():
    return pl.BlockSpec(memory_space=pl.ANY)


def vmem_spec():
    return pl.BlockSpec(memory_space=pltpu.VMEM)


def ws_places():
    w = lax.axis_index("ws")
    x, c = w // 2, w % 2
    return w, x, c, x * 2 + 1 - c, (1 - x) * 2 + c


def meet(peers):
    barrier = pltpu.get_barrier_semaphore()
    for peer in peers:
        pl.semaphore_signal(barrier, inc=1, device_id=peer, device_id_type=MESH_ID)
    pl.semaphore_wait(barrier, len(peers))


def push(src, dst, send, recv, peer):
    return pltpu.make_async_remote_copy(
        src_ref=src, dst_ref=dst, send_sem=send, recv_sem=recv, device_id=peer, device_id_type=MESH_ID
    )


def columns(q, cols):
    return pl.ds(pl.multiple_of(q * cols, cols), cols)


def params(cid):
    return pltpu.CompilerParams(
        collective_id=cid, has_side_effects=True, vmem_limit_bytes=VMEM_CAP
    )


def reduce_kernel(chunks, p, o, rc, sx, rx, cs, cr, xs, xr):
    w, x, c, core, cross = ws_places()
    rows, cols = o.shape
    step = rows // chunks
    meet([{"ws": core}, {"ws": cross}])
    sent = []
    for k in range(chunks):
        r = pl.ds(k * step, step)
        for j, far in enumerate((1 - x, x)):
            src = p.at[r, columns(far * 2 + 1 - c, cols)]
            copy = push(src, rc.at[j, r], cs.at[j, k], cr.at[j, k], {"ws": core})
            copy.start()
            sent.append(copy)
    cross_sent = []
    for k in range(chunks):
        r = pl.ds(k * step, step)
        sent[2 * k].wait_recv()
        total = p[r, columns((1 - x) * 2 + c, cols)].astype(F32) + rc[0, r].astype(F32)
        sx[r] = total.astype(BF)
        copy = push(sx.at[r], rx.at[r], xs.at[k], xr.at[k], {"ws": cross})
        copy.start()
        cross_sent.append(copy)
    for k in range(chunks):
        r = pl.ds(k * step, step)
        sent[2 * k + 1].wait_recv()
        near = p[r, columns(x * 2 + c, cols)].astype(F32) + rc[1, r].astype(F32)
        cross_sent[k].wait_recv()
        o[r] = near + rx[r].astype(F32)
    for copy in sent + cross_sent:
        copy.wait_send()


def ws_reduce(p, cid, chunks=4):
    rows, cols = p.shape[0], p.shape[1] // 4
    dma = pltpu.SemaphoreType.DMA
    return pl.pallas_call(
        functools.partial(reduce_kernel, chunks),
        out_shape=jax.ShapeDtypeStruct((rows, cols), F32),
        in_specs=[vmem_spec()],
        out_specs=vmem_spec(),
        scratch_shapes=[
            pltpu.VMEM((2, rows, cols), BF),
            pltpu.VMEM((rows, cols), BF),
            pltpu.VMEM((rows, cols), BF),
            dma((2, chunks)),
            dma((2, chunks)),
            dma((chunks,)),
            dma((chunks,)),
        ],
        compiler_params=params(cid),
        name=f"ws_reduce_{cid}",
    )(p)


def to_lanes(column):
    return jnp.broadcast_to(column, (column.shape[0], 128)).T[:8]


def to_column(lanes):
    return jnp.broadcast_to(lanes[:1], (128, lanes.shape[1])).T[:, :1]


def sum_over_ws(stat, stats, send, recv, mates):
    copies = []
    for j, peer in enumerate(mates):
        copy = push(stat, stats.at[j], send.at[j], recv.at[j], peer)
        copy.start()
        copies.append(copy)
    for copy in copies:
        copy.wait()
    return stat[...] + stats[0] + stats[1] + stats[2]


def mix_kernel(chunks, p, xq, gain, sel, o, inv, hn, picked, rc, sx, rx, stat, stats, cs, cr, xs, xr, ss, sr):
    w, x, c, core, cross = ws_places()
    mates = [{"ws": core}, {"ws": cross}, {"ws": (1 - x) * 2 + 1 - c}]
    rows, cols = o.shape
    step = rows // chunks
    meet(mates)
    sent = []
    for k in range(chunks):
        r = pl.ds(k * step, step)
        for j, far in enumerate((1 - x, x)):
            src = p.at[r, columns(far * 2 + 1 - c, cols)]
            copy = push(src, rc.at[j, r], cs.at[j, k], cr.at[j, k], {"ws": core})
            copy.start()
            sent.append(copy)
    cross_sent = []
    for k in range(chunks):
        r = pl.ds(k * step, step)
        sent[2 * k].wait_recv()
        total = p[r, columns((1 - x) * 2 + c, cols)].astype(F32) + rc[0, r].astype(F32)
        sx[r] = total.astype(BF)
        copy = push(sx.at[r], rx.at[r], xs.at[k], xr.at[k], {"ws": cross})
        copy.start()
        cross_sent.append(copy)
    for k in range(chunks):
        r = pl.ds(k * step, step)
        sent[2 * k + 1].wait_recv()
        near = p[r, columns(x * 2 + c, cols)].astype(F32) + rc[1, r].astype(F32)
        cross_sent[k].wait_recv()
        total = near + rx[r].astype(F32) + xq[r].astype(F32)
        o[r] = total
        stat[:, k * step : (k + 1) * step] = to_lanes(jnp.sum(total * total, axis=1, keepdims=True))
    total = sum_over_ws(stat, stats, ss, sr, mates)
    inverse = lax.rsqrt(to_column(total) / (4 * cols) + EPS)
    inv[...] = inverse
    hn[...] = (o[...] * inverse * gain[...]).astype(BF)
    picked[...] = jnp.dot(sel[...], hn[...], preferred_element_type=F32).astype(BF)
    for copy in sent + cross_sent:
        copy.wait_send()


def mix(p, xq, gain, sel, cid, chunks=4):
    rows, cols = xq.shape
    slots = sel.shape[0]
    dma = pltpu.SemaphoreType.DMA
    return pl.pallas_call(
        functools.partial(mix_kernel, chunks),
        out_shape=(
            jax.ShapeDtypeStruct((rows, cols), F32),
            jax.ShapeDtypeStruct((rows, 1), F32),
            jax.ShapeDtypeStruct((rows, cols), BF),
            jax.ShapeDtypeStruct((slots, cols), BF),
        ),
        in_specs=[vmem_spec()] * 4,
        out_specs=(vmem_spec(),) * 4,
        scratch_shapes=[
            pltpu.VMEM((2, rows, cols), BF),
            pltpu.VMEM((rows, cols), BF),
            pltpu.VMEM((rows, cols), BF),
            pltpu.VMEM((8, rows), F32),
            pltpu.VMEM((3, 8, rows), F32),
            dma((2, chunks)),
            dma((2, chunks)),
            dma((chunks,)),
            dma((chunks,)),
            dma((3,)),
            dma((3,)),
        ],
        compiler_params=params(cid),
        name=f"mix_{cid}",
    )(p, xq, gain, sel)


def home_kernel(sel, d, extra, hidden, inv, gain, dy, dh, gn, o, stat, stats, mine, own, ss, sr, xs, xr, cs, cr):
    w, x, c, core, cross = ws_places()
    mates = [{"ws": core}, {"ws": cross}, {"ws": (1 - x) * 2 + 1 - c}]
    rows, cols = hidden.shape
    meet(mates)
    total = lax.dot_general(sel[...], d[...], (((0,), (0,)), ((), ())), preferred_element_type=F32)
    total += extra[...]
    unit = hidden[...] * inv[...]
    gn[...] = jnp.broadcast_to(jnp.sum(total * unit, axis=0, keepdims=True), gn.shape)
    weighted = total * gain[...]
    stat[...] = to_lanes(jnp.sum(weighted * unit, axis=1, keepdims=True))
    mean = to_column(sum_over_ws(stat, stats, ss, sr, mates)) / (4 * cols)
    result = dy[...].astype(F32) + inv[...] * (weighted - unit * mean)
    dh[...] = result
    mine[...] = result.astype(BF)
    place = o.at[:, columns(w, cols)]
    local = pltpu.make_async_copy(mine, place, own)
    over = push(mine, place, xs, xr, {"ws": cross})
    beside_ = push(mine, place, cs.at[0], cr.at[0], {"ws": core})
    for copy in (local, over, beside_):
        copy.start()
    over.wait_recv()
    block = o.at[:, columns(cross, cols)]
    onward = push(block, block, cs.at[1], cr.at[1], {"ws": core})
    onward.start()
    for copy in (local, beside_, onward):
        copy.wait()
    over.wait_send()


def home(sel, d, extra, hidden, inv, gain, dy, cid):
    rows, cols = hidden.shape
    dma = pltpu.SemaphoreType.DMA
    return pl.pallas_call(
        home_kernel,
        out_shape=(
            jax.ShapeDtypeStruct((rows, cols), F32),
            jax.ShapeDtypeStruct((8, cols), F32),
            jax.ShapeDtypeStruct((rows, 4 * cols), BF),
        ),
        in_specs=[vmem_spec()] * 7,
        out_specs=(vmem_spec(), vmem_spec(), any_spec()),
        scratch_shapes=[
            pltpu.VMEM((8, rows), F32),
            pltpu.VMEM((3, 8, rows), F32),
            pltpu.VMEM((rows, cols), BF),
            dma,
            dma((3,)),
            dma((3,)),
            dma,
            dma,
            dma((2,)),
            dma((2,)),
        ],
        compiler_params=params(cid),
        name=f"home_{cid}",
    )(sel, d, extra, hidden, inv, gain, dy)


def spread_kernel(chunks, q, o, own, cs, cr, xs, xr):
    w, x, c, core, cross = ws_places()
    rows, cols = q.shape
    step = rows // chunks
    meet([{"ws": core}, {"ws": cross}])
    local = pltpu.make_async_copy(q, o.at[:, columns(w, cols)], own)
    local.start()
    crossing, coring = [], []
    for k in range(chunks):
        r = pl.ds(k * step, step)
        dst = o.at[r, columns(w, cols)]
        copy = push(q.at[r], dst, xs.at[k], xr.at[k], {"ws": cross})
        copy.start()
        crossing.append(copy)
        copy = push(q.at[r], dst, cs.at[0, k], cr.at[0, k], {"ws": core})
        copy.start()
        coring.append(copy)
    for k in range(chunks):
        r = pl.ds(k * step, step)
        crossing[k].wait_recv()
        block = o.at[r, columns(cross, cols)]
        copy = push(block, block, cs.at[1, k], cr.at[1, k], {"ws": core})
        copy.start()
        coring.append(copy)
    local.wait()
    for copy in coring:
        copy.wait()
    for copy in crossing:
        copy.wait_send()


def ws_spread(q, cid, chunks=4):
    rows, cols = q.shape
    dma = pltpu.SemaphoreType.DMA
    return pl.pallas_call(
        functools.partial(spread_kernel, chunks),
        out_shape=jax.ShapeDtypeStruct((rows, 4 * cols), q.dtype),
        in_specs=[any_spec()],
        out_specs=any_spec(),
        scratch_shapes=[dma, dma((2, chunks)), dma((2, chunks)), dma((chunks,)), dma((chunks,))],
        compiler_params=params(cid),
        name=f"ws_spread_{cid}",
    )(q)


class Dispatch:
    def __init__(self, n, axes, qs, os, own, ps, pr, cs, cr, xs, xr):
        self.n, self.axes, self.qs, self.os = n, axes, qs, os
        self.own, self.ps, self.pr, self.cs, self.cr, self.xs, self.xr = own, ps, pr, cs, cr, xs, xr
        self.e = lax.axis_index("ep")
        self.w, _, _, self.core, self.cross = ws_places()
        self.steps = [(i, k) for k in range(n) for i in range(len(axes))]

    def window(self, i, g, q):
        rows, cols = self.qs[i].shape[1:]
        if self.axes[i] == 0:
            return self.os[i].at[g, pl.ds(pl.multiple_of(q * rows, rows), rows)]
        return self.os[i].at[g, :, columns(q, cols)]

    def local(self, i):
        return pltpu.make_async_copy(
            self.qs[i].at[self.e], self.window(i, self.e, self.w), self.own.at[i]
        )

    def sent(self, i, k):
        d = (self.e + k) % self.n
        dst = self.window(i, self.e, self.w)
        return push(self.qs[i].at[d], dst, self.ps.at[i, k], self.pr.at[i, k], {"ep": d})

    def to_cross(self, i, k):
        block = self.window(i, (self.e + self.n - k) % self.n, self.w)
        return push(block, block, self.xs.at[i, k], self.xr.at[i, k], {"ws": self.cross})

    def to_core(self, i, j, k):
        block = self.window(i, (self.e + self.n - k) % self.n, self.cross if j else self.w)
        return push(block, block, self.cs.at[i, j, k], self.cr.at[i, j, k], {"ws": self.core})

    def start(self):
        for i, k in self.steps:
            (self.local(i) if k == 0 else self.sent(i, k)).start()

    def hand_on(self):
        for i, k in self.steps:
            if k == 0:
                self.local(i).wait()
            else:
                self.sent(i, k).wait_recv()
            self.to_cross(i, k).start()
            self.to_core(i, 0, k).start()

    def onward(self):
        for i, k in self.steps:
            self.to_cross(i, k).wait_recv()
            self.to_core(i, 1, k).start()

    def run(self):
        self.hand_on()
        self.onward()

    def finish(self):
        for i, k in self.steps:
            if k > 0:
                self.sent(i, k).wait_send()
            self.to_cross(i, k).wait_send()
            self.to_core(i, 0, k).wait()
            self.to_core(i, 1, k).wait()


def dispatch_peers(n):
    e = lax.axis_index("ep")
    _, _, _, core, cross = ws_places()
    return [{"ep": (e + k) % n} for k in range(1, n)] + [{"ws": core}, {"ws": cross}]


def dispatch_sems(m, n):
    dma = pltpu.SemaphoreType.DMA
    return [dma((m,))] + [dma((m, n))] * 2 + [dma((m, 2, n))] * 2 + [dma((m, n))] * 2


def dispatched(q, axis):
    n, rows, cols = q.shape
    shape = (n, 4 * rows, cols) if axis == 0 else (n, rows, 4 * cols)
    return jax.ShapeDtypeStruct(shape, q.dtype)


def dispatch_kernel(n, axes, *refs):
    m = len(axes)
    meet(dispatch_peers(n))
    work = Dispatch(n, axes, refs[:m], refs[m : 2 * m], *refs[2 * m :])
    work.start()
    work.run()
    work.finish()


def dispatch(cid, *payloads):
    n = payloads[0][0].shape[0]
    m = len(payloads)
    return pl.pallas_call(
        functools.partial(dispatch_kernel, n, [axis for _, axis in payloads]),
        out_shape=[dispatched(*payload) for payload in payloads],
        in_specs=[any_spec()] * m,
        out_specs=[any_spec()] * m,
        scratch_shapes=dispatch_sems(m, n),
        compiler_params=params(cid),
        name=f"dispatch_{cid}",
    )(*[q for q, _ in payloads])


def return_kernel(n, p, dg, o, dgo, rc, sx, rx, st, dgr, dgs, own, cs, cr, xs, xr, ps, pr, gs, gr, hs, hr):
    e = lax.axis_index("ep")
    w, x, c, core, cross = ws_places()
    diag = (1 - x) * 2 + 1 - c
    cols = o.shape[2]
    peers = [{"ep": (e + k) % n} for k in range(1, n)]
    meet(peers + [{"ws": core}, {"ws": cross}, {"ws": diag}])
    order = list(range(1, n)) + [0]
    coring = {}
    for k in order:
        g = (e + k) % n
        for j, far in enumerate((1 - x, x)):
            src = p.at[g, :, columns(far * 2 + 1 - c, cols)]
            copy = push(src, rc.at[j, k], cs.at[j, k], cr.at[j, k], {"ws": core})
            copy.start()
            coring[j, k] = copy
    gates = []
    for j, peer in enumerate((core, cross, diag)):
        copy = push(dg, dgr.at[j], gs.at[j], gr.at[j], {"ws": peer})
        copy.start()
        gates.append(copy)
    crossing = {}
    for k in order:
        g = (e + k) % n
        coring[0, k].wait_recv()
        total = p[g, :, columns((1 - x) * 2 + c, cols)].astype(F32) + rc[0, k].astype(F32)
        sx[k] = total.astype(BF)
        crossing[k] = push(sx.at[k], rx.at[k], xs.at[k], xr.at[k], {"ws": cross})
        crossing[k].start()
    for copy in gates:
        copy.wait_recv()
    dgs[...] = dg[...] + dgr[0] + dgr[1] + dgr[2]
    home = []
    for k in order:
        g = (e + k) % n
        coring[1, k].wait_recv()
        near = p[g, :, columns(x * 2 + c, cols)].astype(F32) + rc[1, k].astype(F32)
        crossing[k].wait_recv()
        st[k] = (near + rx[k].astype(F32)).astype(BF)
        if k > 0:
            copy = push(st.at[k], o.at[e], ps.at[k], pr.at[k], peers[k - 1])
            copy.start()
            home.append(copy)
            copy = push(dgs.at[g], dgo.at[e], hs.at[k], hr.at[k], peers[k - 1])
            copy.start()
            home.append(copy)
        else:
            copy = pltpu.make_async_copy(st.at[0], o.at[e], own.at[0])
            copy.start()
            home.append(copy)
            copy = pltpu.make_async_copy(dgs.at[g], dgo.at[e], own.at[1])
            copy.start()
            home.append(copy)
    for copy in home:
        copy.wait()
    for copy in gates + list(coring.values()) + list(crossing.values()):
        copy.wait_send()


def give_back(p, dg, cid):
    n, rows, cols = p.shape[0], p.shape[1], p.shape[2] // 4
    dma = pltpu.SemaphoreType.DMA
    return pl.pallas_call(
        functools.partial(return_kernel, n),
        out_shape=(jax.ShapeDtypeStruct((n, rows, cols), BF), jax.ShapeDtypeStruct(dg.shape, F32)),
        in_specs=[vmem_spec(), vmem_spec()],
        out_specs=(any_spec(), any_spec()),
        scratch_shapes=[
            pltpu.VMEM((2, n, rows, cols), BF),
            pltpu.VMEM((n, rows, cols), BF),
            pltpu.VMEM((n, rows, cols), BF),
            pltpu.VMEM((n, rows, cols), BF),
            pltpu.VMEM((3,) + dg.shape, F32),
            pltpu.VMEM(dg.shape, F32),
            dma((2,)),
            dma((2, n)),
            dma((2, n)),
            dma((n,)),
            dma((n,)),
            dma((n,)),
            dma((n,)),
            dma((3,)),
            dma((3,)),
            dma((n,)),
            dma((n,)),
        ],
        compiler_params=params(cid),
        name=f"give_back_{cid}",
    )(p, dg)


def return_part_kernel(n, p, dg, act_h, down_h, o, dgo, part, rc, sx, rx, st, dgr, dgs,
                       act, down, stage, own, cs, cr, xs, xr, ps, pr, gs, gr, hs, hr, ls, os_):
    e = lax.axis_index("ep")
    w, x, c, core, cross = ws_places()
    diag = (1 - x) * 2 + 1 - c
    cols = o.shape[2]
    size = down.shape[0] // n
    meet([{"ep": (e + k) % n} for k in range(1, n)] + [{"ws": core}, {"ws": cross}, {"ws": diag}])

    def to_core(k, j):
        far = (1 - x) if j == 0 else x
        src = p.at[(e + k) % n, :, columns(far * 2 + 1 - c, cols)]
        return push(src, rc.at[j, k], cs.at[j, k], cr.at[j, k], {"ws": core})

    def to_cross(k):
        return push(sx.at[k], rx.at[k], xs.at[k], xr.at[k], {"ws": cross})

    def to_home(k):
        peer = {"ep": (e + k) % n}
        return (
            push(st.at[k], o.at[e], ps.at[k], pr.at[k], peer),
            push(dgs.at[(e + k) % n], dgo.at[e], hs.at[k], hr.at[k], peer),
        )

    @pl.loop(0, n)
    def _(i):
        to_core((i + 1) % n, 0).start()
        to_core((i + 1) % n, 1).start()

    loads = []
    for i, (src, dst) in enumerate(((act_h, act), (down_h, down))):
        copy = pltpu.make_async_copy(src, dst, ls.at[i])
        copy.start()
        loads.append(copy)
    gates = []
    for j, peer in enumerate((core, cross, diag)):
        copy = push(dg, dgr.at[j], gs.at[j], gr.at[j], {"ws": peer})
        copy.start()
        gates.append(copy)

    @pl.loop(0, n)
    def _(i):
        k = (i + 1) % n
        to_core(k, 0).wait_recv()
        mine = p[(e + k) % n, :, columns((1 - x) * 2 + c, cols)]
        sx[k] = (mine.astype(F32) + rc[0, k].astype(F32)).astype(BF)
        to_cross(k).start()

    for copy in gates:
        copy.wait_recv()
    dgs[...] = dg[...] + dgr[0] + dgr[1] + dgr[2]
    for copy in loads:
        copy.wait()

    def out_copy(i):
        return pltpu.make_async_copy(stage.at[i % 2], part.at[:, columns(i, size)], os_.at[i % 2])

    @pl.loop(0, n)
    def _(i):
        k = (i + 1) % n
        terms = lax.dot_general(
            act[...],
            down[pl.ds(pl.multiple_of(i * size, size), size)],
            (((1,), (1,)), ((), ())),
            preferred_element_type=F32,
        )

        @pl.when(i > 1)
        def _():
            out_copy(i - 2).wait()

        stage[i % 2] = terms.astype(BF)
        out_copy(i).start()
        to_core(k, 1).wait_recv()
        mine = p[(e + k) % n, :, columns(x * 2 + c, cols)]
        near = mine.astype(F32) + rc[1, k].astype(F32)
        to_cross(k).wait_recv()
        st[k] = (near + rx[k].astype(F32)).astype(BF)

        @pl.when(i < n - 1)
        def _():
            for copy in to_home(k):
                copy.start()

    last = [
        pltpu.make_async_copy(st.at[0], o.at[e], own.at[0]),
        pltpu.make_async_copy(dgs.at[e], dgo.at[e], own.at[1]),
    ]
    for copy in last:
        copy.start()
    for i in range(n - 2, n):
        out_copy(i).wait()
    for copy in last:
        copy.wait()
    for copy in gates:
        copy.wait_send()

    @pl.loop(0, n)
    def _(k):
        to_core(k, 0).wait_send()
        to_core(k, 1).wait_send()
        to_cross(k).wait_send()

    @pl.loop(1, n)
    def _(k):
        for copy in to_home(k):
            copy.wait()


def give_back_part(p, dg, act, down, cid):
    n, cap, cols = p.shape[0], p.shape[1], p.shape[2] // 4
    dma = pltpu.SemaphoreType.DMA
    vm = lambda a: pltpu.VMEM(a.shape, a.dtype)
    count, width = act.shape[0], down.shape[0]
    return pl.pallas_call(
        functools.partial(return_part_kernel, n),
        out_shape=(
            jax.ShapeDtypeStruct((n, cap, cols), BF),
            jax.ShapeDtypeStruct(dg.shape, F32),
            jax.ShapeDtypeStruct((count, width), BF),
        ),
        in_specs=[vmem_spec(), vmem_spec(), any_spec(), any_spec()],
        out_specs=(any_spec(),) * 3,
        scratch_shapes=[
            pltpu.VMEM((2, n, cap, cols), BF),
            pltpu.VMEM((n, cap, cols), BF),
            pltpu.VMEM((n, cap, cols), BF),
            pltpu.VMEM((n, cap, cols), BF),
            pltpu.VMEM((3,) + dg.shape, F32),
            pltpu.VMEM(dg.shape, F32),
            vm(act),
            vm(down),
            pltpu.VMEM((2, count, width // n), BF),
            dma((2,)),
            dma((2, n)),
            dma((2, n)),
            dma((n,)),
            dma((n,)),
            dma((n,)),
            dma((n,)),
            dma((3,)),
            dma((3,)),
            dma((n,)),
            dma((n,)),
            dma((2,)),
            dma((2,)),
        ],
        compiler_params=params(cid),
        name=f"give_back_part_{cid}",
    )(p, dg, act, down)


def last_kernel(n, dq, dkv, xt, sel, wq, wkv, hm, dh, unit, extra, inv, gain, lo, gn2, ga, gm, *refs):
    grads_in, refs = refs[:5], refs[5:]
    all_dq, gkv, ha, gt_all, lo_all, gv_all, *grads_out = refs[:9]
    (wt, kwt, rows, pt, rc, sx, rx, near, kvs, kvr, stat, stats, gt, vs, vr,
     wl, own, qs, qr, ks, kr, cs, cr, xs, xr, ss, sr, ts, tr, vps, vpr, vws, vwr) = refs[9:42]
    held, (stage, gl, go, *dsems) = refs[42:47], refs[47:]
    e = lax.axis_index("ep")
    w, x, c, core, cross = ws_places()
    diag = (1 - x) * 2 + 1 - c
    mates = [{"ws": core}, {"ws": cross}, {"ws": diag}]
    pos = ring_pos(n)
    right = {"ep": ring_index((pos + 1) % n, n)}
    left = {"ep": ring_index((pos + n - 1) % n, n)}
    experts, cap, inner = dq.shape
    tokens, cols = dh.shape
    over_last = (((1,), (1,)), ((), ()))
    first = (((0,), (0,)), ((), ()))

    order = ((1 - x) * 2 + 1 - c, x * 2 + 1 - c, (1 - x) * 2 + c, x * 2 + c)

    def load(t):
        r = columns(order[t], cols)
        return (
            pltpu.make_async_copy(wq.at[:, r], wt.at[t % 2], wl.at[t % 2, 0]),
            pltpu.make_async_copy(wkv.at[:, r], kwt.at[t % 2], wl.at[t % 2, 1]),
        )

    for t in range(2):
        for copy in load(t):
            copy.start()
    meet([{"ep": (e + k) % n} for k in range(1, n)] + mates)

    each = experts // 4

    def dq_copy(f, s, fresh=False):
        peer, sign = (right, -1) if f % 2 == 0 else (left, 1)
        part = pl.ds((f % 2 * 2 + f // 2) * each, each)
        dst = all_dq.at[ring_index((pos + n + sign * s) % n, n), part]
        return push(dq.at[part] if fresh else dst, dst, qs.at[f, s], qr.at[f, s], peer)

    for f in range(4):
        dq_copy(f, 0, True).start()
    mine = pltpu.make_async_copy(dq, all_dq.at[e], own.at[0])
    mine.start()

    def dq_step(s):
        for f in range(4):
            dq_copy(f, s - 1).wait_recv()

            @pl.when(s < n - 1)
            def _():
                dq_copy(f, s).start()

    def kv_copy(k, s):
        return push(kvs.at[k, s], kvr.at[k, s], ks.at[k, s], kr.at[k, s], left if k else right)

    def kv_step(s, begin=False):
        for k in range(2):
            ahead = s + 1 if k else n - 1 - s
            block = ring_index((pos + ahead) % n, n)
            value = jnp.dot(xt[block], dkv[k], preferred_element_type=F32)
            if not begin:
                kv_copy(k, s - 1).wait_recv()
                value = value + kvr[k, s - 1].astype(F32)

            @pl.when(s < n - 1)
            def _():
                kvs[k, s] = value.astype(BF)
                kv_copy(k, s).start()

            @pl.when(s == n - 1)
            def _():
                gkv[k] = value

    def share(src, dst, j):
        place = dst.at[:, columns(w, cols)]
        local = pltpu.make_async_copy(src, place, own.at[1 + j])
        over = push(src, place, xs.at[1 + j], xr.at[1 + j], {"ws": cross})
        beside = push(src, place, ts.at[j, 0], tr.at[j, 0], {"ws": core})
        for copy in (local, over, beside):
            copy.start()
        return local, over, beside

    def hand_on(dst, j, over):
        over.wait_recv()
        block = dst.at[:, columns(cross, cols)]
        copy = push(block, block, ts.at[j, 1], tr.at[j, 1], {"ws": core})
        copy.start()
        return copy

    kv_step(0, True)
    spread = Dispatch(n, (0,), (hm,), (ha,), *dsems)
    spread.start()

    def tile(t):
        for copy in load(t):
            copy.wait()

        @pl.loop(0, experts)
        def _(i):
            part = lax.dot_general(dq[i], wt[t % 2, i], over_last, preferred_element_type=F32)
            rows[pl.ds(pl.multiple_of(i * cap, cap), cap)] = part.astype(BF)

        total = lax.dot_general(sel[...], rows[...], first, preferred_element_type=F32)
        for k in range(2):
            total += lax.dot_general(dkv[k], kwt[t % 2, k], over_last, preferred_element_type=F32)
        if t < 2:
            for copy in load(t + 2):
                copy.start()
        return total

    coring = []
    for j in range(2):
        pt[j] = tile(j).astype(BF)
        copy = push(pt.at[j], rc.at[j], cs.at[j], cr.at[j], {"ws": core})
        copy.start()
        coring.append(copy)
    kv_step(1)
    dq_step(1)
    total = tile(2)
    coring[0].wait_recv()
    sx[...] = (total + rc[0].astype(F32)).astype(BF)
    crossing = push(sx, rx, xs.at[0], xr.at[0], {"ws": cross})
    crossing.start()
    total = tile(3)
    coring[1].wait_recv()
    near[...] = total + rc[1].astype(F32)
    kv_step(2)
    dq_step(2)
    loads = []
    for i in range(5):
        copy = pltpu.make_async_copy(grads_in[i], held[i], gl.at[i])
        copy.start()
        loads.append(copy)
    crossing.wait_recv()
    d_xn = near[...] + rx[...].astype(F32) + extra[...]
    u = unit[...]
    row = lax.broadcasted_iota(jnp.int32, gn2.shape, 0)
    vs[:8] = jnp.where(row == 0, jnp.sum(d_xn * u, axis=0, keepdims=True), gn2[...])
    vs[8 : 8 + ga.shape[0]] = ga[...]
    vs[8 + ga.shape[0] :] = gm[...]
    weighted = d_xn * gain[...]
    near[...] = weighted
    across = jnp.sum(weighted * u, axis=1, keepdims=True)
    stat[...] = jnp.broadcast_to(across, (tokens, 128)).T[:8]
    sums = []
    for j, peer in enumerate(mates):
        copy = push(stat, stats.at[j], ss.at[j], sr.at[j], peer)
        copy.start()
        sums.append(copy)
    gains = []
    for k in range(1, n):
        copy = push(vs, vr.at[k - 1], vps.at[k], vpr.at[k], {"ep": (e + k) % n})
        copy.start()
        gains.append(copy)
    for copy in sums:
        copy.wait_recv()
    mean = (stat[...] + stats[0] + stats[1] + stats[2]) / (4 * cols)
    mean = jnp.broadcast_to(mean[:1], (128, tokens)).T[:, :1]
    gt[...] = (dh[...] + inv[...] * (near[...] - u * mean)).astype(BF)
    gt_copies = share(gt, gt_all, 1)
    lo_copies = share(lo, lo_all, 0)
    kv_step(3)
    dq_step(3)
    spread.hand_on()
    for copy in loads:
        copy.wait()

    size = grads_out[0].shape[0] // 8
    rows_in, dy_in, dgate_in, dup_in, down_in = held

    def out_copy(i, j):
        dst = grads_out[j].at[pl.ds(pl.multiple_of(i * size, size), size)]
        return pltpu.make_async_copy(stage.at[j], dst, go.at[j])

    @pl.loop(4, n)
    def _(s):
        kv_step(s)
        dq_step(s)

        @pl.loop(0, 2)
        def _(h):
            i = (s - 4) * 2 + h
            for j, (a, b) in enumerate(((rows_in, dgate_in), (rows_in, dup_in), (dy_in, down_in))):
                grad = lax.dot_general(
                    a[:, columns(i, size)], b[...], first, preferred_element_type=F32
                )

                @pl.when(i > 0)
                def _():
                    out_copy(i - 1, j).wait()

                stage[j] = grad.astype(BF)
                out_copy(i, j).start()

    gt_core = hand_on(gt_all, 1, gt_copies[1])
    lo_core = hand_on(lo_all, 0, lo_copies[1])
    spread.onward()
    for copy in gains:
        copy.wait_recv()
    vs_total = vs[...]
    for k in range(n - 1):
        vs_total += vr[k]
    for copy in gains:
        copy.wait_send()
    vs[...] = vs_total
    place = gv_all.at[:, columns(w, cols)]
    gv_copies = [pltpu.make_async_copy(vs, place, own.at[3])]
    for j, peer in enumerate(mates):
        gv_copies.append(push(vs, place, vws.at[j], vwr.at[j], peer))
    for copy in gv_copies:
        copy.start()
    for j in range(3):
        out_copy(7, j).wait()
    mine.wait()
    for copy in gv_copies + [lo_copies[0], lo_copies[2], gt_copies[0], gt_copies[2], lo_core, gt_core]:
        copy.wait()
    for copy in coring + sums + [crossing, lo_copies[1], gt_copies[1]]:
        copy.wait_send()
    for f in range(4):
        dq_copy(f, 0, True).wait_send()

    @pl.loop(1, n - 1)
    def _(s):
        for f in range(4):
            dq_copy(f, s).wait_send()

    @pl.loop(0, n - 1)
    def _(s):
        for k in range(2):
            kv_copy(k, s).wait_send()

    spread.finish()


def last_stage(cid, dq, dkv, xt, sel, wq, wkv, hm, dh, unit, extra, inv, gain, lo, gn2, ga, gm, *grads):
    n = xt.shape[0]
    experts, cap, inner = dq.shape
    tokens, cols = dh.shape
    block = xt.shape[1]
    dma = pltpu.SemaphoreType.DMA
    vm, hbm = vmem_spec(), any_spec()
    small = (8 + ga.shape[0] + gm.shape[0], cols)
    width, f = grads[0].shape[1], grads[2].shape[1]
    wide = jax.ShapeDtypeStruct((tokens, 4 * cols), BF)
    return pl.pallas_call(
        functools.partial(last_kernel, n),
        out_shape=[
            jax.ShapeDtypeStruct((n,) + dq.shape, BF),
            jax.ShapeDtypeStruct((2, block, inner), F32),
            dispatched(hm, 0),
            wide,
            wide,
            jax.ShapeDtypeStruct((small[0], 4 * cols), F32),
        ]
        + [jax.ShapeDtypeStruct((width, f), BF)] * 3,
        in_specs=[vm] * 4 + [hbm] * 3 + [vm] * 9 + [hbm] * 5,
        out_specs=[hbm, vm] + [hbm] * 7,
        scratch_shapes=[
            pltpu.VMEM((2, experts, cols, inner), BF),
            pltpu.VMEM((2, 2, cols, inner), BF),
            pltpu.VMEM((experts * cap, cols), BF),
            pltpu.VMEM((2, tokens, cols), BF),
            pltpu.VMEM((2, tokens, cols), BF),
            pltpu.VMEM((tokens, cols), BF),
            pltpu.VMEM((tokens, cols), BF),
            pltpu.VMEM((tokens, cols), F32),
            pltpu.VMEM((2, n - 1, block, inner), BF),
            pltpu.VMEM((2, n - 1, block, inner), BF),
            pltpu.VMEM((8, tokens), F32),
            pltpu.VMEM((3, 8, tokens), F32),
            pltpu.VMEM((tokens, cols), BF),
            pltpu.VMEM(small, F32),
            pltpu.VMEM((n - 1,) + small, F32),
            dma((2, 2)),
            dma((4,)),
            dma((4, n)),
            dma((4, n)),
            dma((2, n)),
            dma((2, n)),
            dma((2,)),
            dma((2,)),
            dma((3,)),
            dma((3,)),
            dma((3,)),
            dma((3,)),
            dma((2, 2)),
            dma((2, 2)),
            dma((n,)),
            dma((n,)),
            dma((3,)),
            dma((3,)),
        ]
        + [pltpu.VMEM(a.shape, a.dtype) for a in grads]
        + [pltpu.VMEM((3, width // 8, f), BF), dma((5,)), dma((3,))]
        + dispatch_sems(1, n),
        compiler_params=params(cid),
        name=f"last_{cid}",
    )(dq, dkv, xt, sel, wq, wkv, hm, dh, unit, extra, inv, gain, lo, gn2, ga, gm, *grads)


def grad_slots_kernel(n, dest, x, y, o, picked, ys):
    e = pl.program_id(0)
    cap = y.shape[2]
    index = e * cap + lax.broadcasted_iota(jnp.int32, (cap, x.shape[1]), 0)
    for g in range(n):
        hit = (dest[g, 0:1, :] == index) | (dest[g, 1:2, :] == index)
        sel = jnp.where(hit, 1.0, 0.0).astype(BF)
        r = pl.ds(g * cap, cap)
        picked[r] = jnp.dot(sel, x[g], preferred_element_type=F32).astype(BF)
        ys[r] = y[g, 0]
    o[0] = lax.dot_general(
        picked[...], ys[...], (((0,), (0,)), ((), ())), preferred_element_type=F32
    )


def grad_slots(dest, x, y):
    n, tokens, block = x.shape
    experts, cap, cols = y.shape[1:]
    return pl.pallas_call(
        functools.partial(grad_slots_kernel, n),
        grid=(experts,),
        out_shape=jax.ShapeDtypeStruct((experts, block, cols), F32),
        in_specs=[
            pl.BlockSpec(dest.shape, lambda i: (0, 0, 0)),
            pl.BlockSpec(x.shape, lambda i: (0, 0, 0)),
            pl.BlockSpec((n, 1, cap, cols), lambda i: (0, i, 0, 0)),
        ],
        out_specs=pl.BlockSpec((1, block, cols), lambda i: (i, 0, 0)),
        scratch_shapes=[pltpu.VMEM((n * cap, block), BF), pltpu.VMEM((n * cap, cols), BF)],
        compiler_params=pltpu.CompilerParams(vmem_limit_bytes=VMEM_CAP),
        cost_estimate=pl.CostEstimate(
            flops=2 * experts * n * cap * block * (tokens + cols),
            bytes_accessed=2 * (x.size + y.size) + 4 * experts * block * cols,
            transcendentals=0,
        ),
        name="grad_slots",
    )(dest, x, y)


def collect_kernel(n, v, o, got, part, own, ps, pr, ws, wr):
    e, w = lax.axis_index("ep"), lax.axis_index("ws")
    cols = v.shape[1]
    peers = [{"ep": (e + k) % n} for k in range(1, n)]
    mates = [{"ws": (w + k) % 4} for k in range(1, 4)]
    meet(peers + mates)
    first = []
    for k in range(1, n):
        copy = push(v, got.at[k - 1], ps.at[k], pr.at[k], peers[k - 1])
        copy.start()
        first.append(copy)
    total = v[...]
    for k in range(1, n):
        first[k - 1].wait_recv()
        total += got[k - 1]
    part[...] = total
    mine = o.at[:, columns(w, cols)]
    local = pltpu.make_async_copy(part, mine, own)
    local.start()
    second = []
    for k in range(3):
        copy = push(part, mine, ws.at[k], wr.at[k], mates[k])
        copy.start()
        second.append(copy)
    local.wait()
    for copy in second:
        copy.wait()
    for copy in first:
        copy.wait_send()


def collect(v, cid):
    n = lax.axis_size("ep")
    rows, cols = v.shape
    dma = pltpu.SemaphoreType.DMA
    return pl.pallas_call(
        functools.partial(collect_kernel, n),
        out_shape=jax.ShapeDtypeStruct((rows, 4 * cols), F32),
        in_specs=[vmem_spec()],
        out_specs=vmem_spec(),
        scratch_shapes=[
            pltpu.VMEM((n - 1, rows, cols), F32),
            pltpu.VMEM((rows, cols), F32),
            dma,
            dma((n,)),
            dma((n,)),
            dma((3,)),
            dma((3,)),
        ],
        compiler_params=params(cid),
        name=f"collect_{cid}",
    )(v)


def ring_kernel(n, m, splits, axes, *refs):
    p = len(axes)
    xs, qs, refs = refs[:m], refs[m : m + p], refs[m + p :]
    os, qos, refs = refs[:m], refs[m : m + p], refs[m + p :]
    own, send, recv, *sems = refs
    pos, me = ring_pos(n), lax.axis_index("ep")
    right = {"ep": ring_index((pos + 1) % n, n)}
    left = {"ep": ring_index((pos + n - 1) % n, n)}
    _, _, _, core, cross = ws_places()
    meet([{"ep": (me + k) % n} for k in range(1, n)] + [{"ws": core}, {"ws": cross}])
    flows = []
    for i in range(m):
        part = xs[i].shape[0] // (2 * splits[i])
        for k in range(splits[i]):
            flows.append((i, k * part, part, right, -1))
            flows.append((i, (splits[i] + k) * part, part, left, 1))

    def window(i, first, part, owner):
        size = xs[i].shape[1]
        return os[i].at[pl.ds(first, part), pl.ds(pl.multiple_of(owner * size, size), size)]

    def start(f, s):
        i, first, part, peer, sign = flows[f]
        owner = ring_index((pos + n + sign * s) % n, n)
        dst = window(i, first, part, owner)
        src = xs[i].at[pl.ds(first, part)] if s == 0 else dst
        copy = push(src, dst, send.at[f, s], recv.at[f, s], peer)
        copy.start()
        return copy

    live = [start(f, 0) for f in range(len(flows))]
    work = Dispatch(n, axes, qs, qos, *sems)
    work.start()
    locals_ = []
    for i in range(m):
        copy = pltpu.make_async_copy(xs[i], window(i, 0, xs[i].shape[0], me), own.at[i])
        copy.start()
        locals_.append(copy)
    done = []
    for s in range(1, n):
        for f in range(len(flows)):
            live[f].wait_recv()
            done.append(live[f])
            if s < n - 1:
                live[f] = start(f, s)
        if s == 1:
            work.run()
    work.finish()
    for copy in locals_:
        copy.wait()
    for copy in done:
        copy.wait_send()


def ring_kernel_gather(cid, splits, xs, payloads):
    n, m = lax.axis_size("ep"), len(xs)
    dma = pltpu.SemaphoreType.DMA
    flows = 2 * sum(splits)
    out = pl.pallas_call(
        functools.partial(ring_kernel, n, m, splits, [axis for _, axis in payloads]),
        out_shape=[jax.ShapeDtypeStruct((x.shape[0], n * x.shape[1], x.shape[2]), x.dtype) for x in xs]
        + [dispatched(*payload) for payload in payloads],
        in_specs=[any_spec()] * (m + len(payloads)),
        out_specs=[any_spec()] * (m + len(payloads)),
        scratch_shapes=[dma((m,)), dma((flows, n)), dma((flows, n))] + dispatch_sems(len(payloads), n),
        compiler_params=params(cid),
        name=f"ring_{cid}",
    )(*xs, *[q for q, _ in payloads])
    return out[:m], out[m:]


def project_kernel(experts, parts, extra, sel, y, *rest):
    weights, rest = rest[:parts], rest[parts:]
    if extra:
        kv, kv_weight, o, rows = rest
    else:
        o, rows = rest
    each = experts // parts
    cap = y.shape[1]
    over_last = (((1,), (1,)), ((), ()))
    for i in range(experts):
        weight = weights[i // each][i % each]
        part = lax.dot_general(y[i], weight, over_last, preferred_element_type=F32)
        rows[pl.ds(i * cap, cap)] = part.astype(BF)
    total = lax.dot_general(sel[...], rows[...], (((0,), (0,)), ((), ())), preferred_element_type=F32)
    if extra:
        for i in range(2):
            total += lax.dot_general(kv[i], kv_weight[i], over_last, preferred_element_type=F32)
    o[...] = total.astype(BF)


def project_back(sel, y, weight, kv=None, kv_weight=None, tile=512):
    experts, cap, inner = y.shape
    width, tokens = weight[0].shape[1], sel.shape[1]
    whole = lambda a: pl.BlockSpec(a.shape, lambda i: (0,) * a.ndim)
    tiled = lambda a: pl.BlockSpec((a.shape[0], tile, a.shape[2]), lambda i: (0, i, 0))
    args, specs = [sel, y, *weight], [whole(sel), whole(y), *map(tiled, weight)]
    if kv is not None:
        args += [kv, kv_weight]
        specs += [whole(kv), tiled(kv_weight)]
    flops = 2 * experts * cap * inner * width + 2 * tokens * experts * cap * width
    return pl.pallas_call(
        functools.partial(project_kernel, experts, len(weight), kv is not None),
        grid=(width // tile,),
        out_shape=jax.ShapeDtypeStruct((tokens, width), BF),
        in_specs=specs,
        out_specs=pl.BlockSpec((tokens, tile), lambda i: (0, i)),
        scratch_shapes=[pltpu.VMEM((experts * cap, tile), BF)],
        compiler_params=pltpu.CompilerParams(vmem_limit_bytes=VMEM_CAP),
        cost_estimate=pl.CostEstimate(
            flops=flops, bytes_accessed=2 * (sum(a.size for a in weight) + sel.size + y.size), transcendentals=0
        ),
        name="project_back",
    )(*args)


def beside(n, axes, qs, os, sems):
    step, last = pl.program_id(0), pl.num_programs(0) - 1

    @pl.when(step == 0)
    def _():
        meet(dispatch_peers(n))
        Dispatch(n, axes, qs, os, *sems).start()

    @pl.when(step == last)
    def _():
        Dispatch(n, axes, qs, os, *sems).hand_on()

    def finish():
        @pl.when(step == last)
        def _():
            work = Dispatch(n, axes, qs, os, *sems)
            work.onward()
            work.finish()

    return finish


def expert_kernel(owners, n, axes, rows, other, dy_down, router, wg, wu, *refs):
    m = len(axes)
    qs, refs = refs[:m], refs[m:]
    d_gate, d_up, act_o, down_o, part, dg = refs[:6]
    finish = beside(n, axes, qs, refs[6 : 6 + m], refs[6 + m :]) if m else None
    expert = lax.axis_index("ep") // owners
    tile, cap = rows.shape[0], dg.shape[2]
    x = rows[...]
    logits = jnp.dot(x, router[...], preferred_element_type=F32)
    index = lax.broadcasted_iota(jnp.int32, logits.shape, 1)
    own = jnp.sum(jnp.where(index == expert, logits, 0.0), axis=1, keepdims=True)
    oth = jnp.sum(jnp.where(index == other[...], logits, 0.0), axis=1, keepdims=True)
    top = jnp.maximum(own, oth)
    own, oth = jnp.exp(own - top), jnp.exp(oth - top)
    gate = own / (own + oth)
    gate_pre = jnp.dot(x, wg[...], preferred_element_type=F32)
    up_pre = jnp.dot(x, wu[...], preferred_element_type=F32)
    sig = 1.0 / (1.0 + jnp.exp(-gate_pre))
    silu = gate_pre * sig
    act = silu * up_pre
    dy = dy_down[...]
    act_o[...] = act.astype(BF)
    down_o[...] = (act * gate).astype(BF)
    dgate = jnp.sum(act * dy, axis=1, keepdims=True)
    d_act = dy * gate
    dgb = (d_act * up_pre * sig * (1.0 + gate_pre * (1.0 - sig))).astype(BF)
    dub = (d_act * silu).astype(BF)
    d_gate[...] = dgb
    d_up[...] = dub
    over_last = (((1,), (1,)), ((), ()))
    total = lax.dot_general(dgb, wg[...], over_last, preferred_element_type=F32)
    total += lax.dot_general(dub, wu[...], over_last, preferred_element_type=F32)
    part[...] = total.astype(BF)
    lane = lax.broadcasted_iota(jnp.int32, (tile, 128), 1)
    both = jnp.where(lane < 4, dgate, 0.25 * gate).T[:8]
    for j in range(tile // cap):
        dg[j] = both[:, j * cap : (j + 1) * cap]
    if m:
        finish()


def expert_pass(rows, other, dy_down, router, wg, wu, owners, cap, payloads, cid, tile=256):
    n, m = lax.axis_size("ep"), len(payloads)
    count, width = rows.shape
    f = wg.shape[1]
    by_row = lambda c: pl.BlockSpec((tile, c), lambda i: (i, 0))
    once = lambda a: pl.BlockSpec(a.shape, lambda i: (0, 0), pipeline_mode=pl.Buffered(1))
    wide = jax.ShapeDtypeStruct((count, f), BF)
    return pl.pallas_call(
        functools.partial(expert_kernel, owners, n, [axis for _, axis in payloads]),
        grid=(count // tile,),
        out_shape=(wide,) * 4
        + (
            jax.ShapeDtypeStruct((count, width), BF),
            jax.ShapeDtypeStruct((count // cap, 8, cap), F32),
            *[dispatched(*payload) for payload in payloads],
        ),
        in_specs=[by_row(width), by_row(1), by_row(f), once(router), once(wg), once(wu)]
        + [any_spec()] * m,
        out_specs=(by_row(f),) * 4
        + (by_row(width), pl.BlockSpec((tile // cap, 8, cap), lambda i: (i, 0, 0)))
        + (any_spec(),) * m,
        scratch_shapes=dispatch_sems(m, n) if m else [],
        compiler_params=params(cid) if m else pltpu.CompilerParams(vmem_limit_bytes=VMEM_CAP),
        cost_estimate=pl.CostEstimate(
            flops=8 * count * width * f, bytes_accessed=4 * width * f + 12 * count * f, transcendentals=count * f
        ),
        name="expert_pass",
    )(rows, other, dy_down, router, wg, wu, *[q for q, _ in payloads])


def turn(v, cos, sin, sign):
    return v * cos + sign * (pltpu.roll(v, HD // 2, 1) * sin)


def masked_scores(q, k, token):
    raw = lax.dot_general(q, k, (((1,), (1,)), ((), ())), preferred_element_type=F32)
    key = lax.broadcasted_iota(jnp.int32, (1, k.shape[0]), 1)
    _, key_segment = place_of(key)
    _, segment = place_of(token)
    allowed = (key <= token) & ((key_segment == 0) | (key_segment == segment))
    return jnp.where(allowed, raw * (1.0 / math.sqrt(HD)), MASKED)


ROWS = 256


def attend_kernel(q_pre, k_pre, v_pre, q_cos, q_sin, cos, sin, token, gate, q, k, v, o, gated, lse):
    k[...] = turn(k_pre[...], cos[...], sin[...], 1).astype(BF)
    v[...] = v_pre[...].astype(BF)
    for i in range(q.shape[0] // ROWS):
        r = pl.ds(i * ROWS, ROWS)
        q[r] = turn(q_pre[r], q_cos[r], q_sin[r], 1).astype(BF)
        scores = masked_scores(q[r], k[...], token[r])
        peak = jnp.max(scores, axis=1, keepdims=True)
        exponent = jnp.exp(scores - peak)
        total = jnp.sum(exponent, axis=1, keepdims=True)
        lse[0, r] = peak + jnp.log(total)
        probs = (exponent / total).astype(BF)
        out = jnp.dot(probs, v[...], preferred_element_type=F32)
        o[r] = out.astype(BF)
        gated[r] = (out * gate[r]).astype(BF)


def attend_specs(slots, tokens):
    head = lambda rows: pl.BlockSpec((rows, HD), lambda h: (0, h))
    table = lambda rows: pl.BlockSpec((rows, HD), lambda h: (0, 0))
    column = pl.BlockSpec((slots, 1), lambda h: (0, 0))
    line = pl.BlockSpec((1, slots, 1), lambda h: (h, 0, 0))
    return head, table, column, line


def attend(q_pre, k_pre, v_pre, q_cos, q_sin, cos, sin, token, gate):
    slots, inner = q_pre.shape
    tokens = k_pre.shape[0]
    head, table, column, line = attend_specs(slots, tokens)
    wide, narrow = jax.ShapeDtypeStruct((slots, inner), BF), jax.ShapeDtypeStruct((tokens, inner), BF)
    return pl.pallas_call(
        attend_kernel,
        grid=(inner // HD,),
        out_shape=(wide, narrow, narrow, wide, wide, jax.ShapeDtypeStruct((inner // HD, slots, 1), F32)),
        in_specs=[head(slots), head(tokens), head(tokens), table(slots), table(slots), table(tokens), table(tokens)]
        + [column] * 2,
        out_specs=(head(slots), head(tokens), head(tokens), head(slots), head(slots), line),
        compiler_params=pltpu.CompilerParams(vmem_limit_bytes=VMEM_CAP),
        cost_estimate=pl.CostEstimate(
            flops=4 * slots * tokens * inner, bytes_accessed=16 * slots * inner, transcendentals=slots * tokens
        ),
        name="attend",
    )(q_pre, k_pre, v_pre, q_cos, q_sin, cos, sin, token, gate)


def attend_back_kernel(n, axes, raw, o, gate, q, k, v, lse, q_cos, q_sin, cos, sin, token, *refs):
    m = len(axes)
    qs, refs = refs[:m], refs[m:]
    dq, dkv, dgate = refs[:3]
    finish = beside(n, axes, qs, refs[3 : 3 + m], refs[3 + m :]) if m else None
    scale = 1.0 / math.sqrt(HD)
    first = (((0,), (0,)), ((), ()))
    over_last = (((1,), (1,)), ((), ()))
    dk, dv = None, None
    for i in range(q.shape[0] // ROWS):
        r = pl.ds(i * ROWS, ROWS)
        across = jnp.sum(raw[r] * o[r].astype(F32), axis=1, keepdims=True)
        line = jnp.broadcast_to(across, (ROWS, 128)).T[:8]
        lanes = pl.ds(i * ROWS, ROWS)

        @pl.when(pl.program_id(0) == 0)
        def _():
            dgate[:, lanes] = line

        @pl.when(pl.program_id(0) > 0)
        def _():
            dgate[:, lanes] += line

        d_o = (raw[r] * gate[r]).astype(BF)
        probs = jnp.exp(masked_scores(q[r], k[...], token[r]) - lse[0, r])
        d_probs = lax.dot_general(d_o, v[...], over_last, preferred_element_type=F32)
        inside = jnp.sum(probs * d_probs, axis=1, keepdims=True)
        d_scores = (probs * (d_probs - inside)).astype(BF)
        part = jnp.dot(d_scores, k[...], preferred_element_type=F32) * scale
        dq[r] = turn(part, q_cos[r], q_sin[r], -1).astype(BF)
        dk_part = lax.dot_general(d_scores, q[r], first, preferred_element_type=F32)
        dv_part = lax.dot_general(probs.astype(BF), d_o, first, preferred_element_type=F32)
        dk = dk_part if dk is None else dk + dk_part
        dv = dv_part if dv is None else dv + dv_part
    dkv[0] = turn(dk * scale, cos[...], sin[...], -1).astype(BF)
    dkv[1] = dv.astype(BF)
    if m:
        finish()


def attend_back(raw, o, gate, q, k, v, lse, q_cos, q_sin, cos, sin, token, payloads, cid):
    n, m = lax.axis_size("ep"), len(payloads)
    slots, inner = q.shape
    tokens = k.shape[0]
    head, table, column, line = attend_specs(slots, tokens)
    return pl.pallas_call(
        functools.partial(attend_back_kernel, n, [axis for _, axis in payloads]),
        grid=(inner // HD,),
        out_shape=(
            jax.ShapeDtypeStruct((slots, inner), BF),
            jax.ShapeDtypeStruct((2, tokens, inner), BF),
            jax.ShapeDtypeStruct((8, slots), F32),
            *[dispatched(*payload) for payload in payloads],
        ),
        in_specs=[head(slots), head(slots), column, head(slots), head(tokens), head(tokens), line]
        + [table(slots), table(slots), table(tokens), table(tokens), column]
        + [any_spec()] * m,
        out_specs=(
            head(slots),
            pl.BlockSpec((2, tokens, HD), lambda h: (0, 0, h)),
            pl.BlockSpec((8, slots), lambda h: (0, 0)),
        )
        + (any_spec(),) * m,
        scratch_shapes=dispatch_sems(m, n) if m else [],
        compiler_params=params(cid) if m else pltpu.CompilerParams(vmem_limit_bytes=VMEM_CAP),
        cost_estimate=pl.CostEstimate(
            flops=10 * slots * tokens * inner, bytes_accessed=16 * slots * inner, transcendentals=slots * tokens
        ),
        name="attend_back",
    )(raw, o, gate, q, k, v, lse, q_cos, q_sin, cos, sin, token, *[v for v, _ in payloads])


def arrivals(rings, n):
    args, specs = [], []
    for p, got in enumerate([got for ring in rings for got in ring.got]):
        each = got[0].shape[0]
        for v in got:
            args.append(v)
            specs.append(
                pl.BlockSpec(
                    (1,) + v.shape[1:],
                    lambda i, p=p, each=each: (jnp.clip(i - p * each, 0, each - 1), 0, 0),
                )
            )
    return args, specs


def out_kernel(n, each, sel, y, *refs):
    blocks, (o, rows) = refs[:-2], refs[-2:]
    e, pos = pl.program_id(0), ring_pos(n)
    cap = y.shape[1]
    size = blocks[0].shape[1]
    here = pl.ds(pl.multiple_of(e * cap, cap), cap)

    def project(p):
        for s in range(n):
            g = ring_index((pos + n + (2 * (p % 2) - 1) * s) % n, n)
            part = lax.dot_general(
                y[0], blocks[p * n + s][0], (((1,), (1,)), ((), ())), preferred_element_type=F32
            )
            rows[here, columns(g, size)] = part.astype(BF)

    for p in range(len(blocks) // n):
        pl.when(e // each == p)(functools.partial(project, p))

    @pl.when(e == pl.num_programs(0) - 1)
    def _():
        tile = o.shape[1] // 4
        for t in range(4):
            c = pl.ds(t * tile, tile)
            o[:, c] = lax.dot_general(
                sel[...], rows[:, c], (((0,), (0,)), ((), ())), preferred_element_type=F32
            ).astype(BF)


def out_project(sel, y, rings, width):
    n = lax.axis_size("ep")
    experts, cap, inner = y.shape
    tokens = sel.shape[1]
    args, specs = arrivals(rings, n)
    return pl.pallas_call(
        functools.partial(out_kernel, n, args[0].shape[0]),
        grid=(experts,),
        out_shape=jax.ShapeDtypeStruct((tokens, width), BF),
        in_specs=[
            pl.BlockSpec(sel.shape, lambda i: (0, 0)),
            pl.BlockSpec((1, cap, inner), lambda i: (i, 0, 0)),
        ]
        + specs,
        out_specs=pl.BlockSpec((tokens, width), lambda i: (0, 0)),
        scratch_shapes=[pltpu.VMEM((experts * cap, width), BF)],
        compiler_params=pltpu.CompilerParams(vmem_limit_bytes=VMEM_CAP),
        cost_estimate=pl.CostEstimate(
            flops=2 * experts * cap * width * (inner + tokens),
            bytes_accessed=2 * experts * inner * width,
            transcendentals=0,
        ),
        name="out_project",
    )(sel, y, *args)


def back_kernel(n, each, sel, d, *refs):
    blocks, (o, rows) = refs[:-2], refs[-2:]
    e, pos = pl.program_id(0), ring_pos(n)
    size = blocks[0].shape[1]
    rows[...] = jnp.dot(sel[...], d[...], preferred_element_type=F32).astype(BF)

    def project(p):
        total = None
        for s in range(n):
            g = ring_index((pos + n + (2 * (p % 2) - 1) * s) % n, n)
            part = jnp.dot(
                rows[:, columns(g, size)], blocks[p * n + s][0], preferred_element_type=F32
            )
            total = part if total is None else total + part
        o[0] = total

    for p in range(len(blocks) // n):
        pl.when(e // each == p)(functools.partial(project, p))


def out_back(sel, d, rings, experts):
    n = lax.axis_size("ep")
    tokens, width = d.shape
    cap = sel.shape[0] // experts
    args, specs = arrivals(rings, n)
    inner = args[0].shape[2]
    return pl.pallas_call(
        functools.partial(back_kernel, n, args[0].shape[0]),
        grid=(experts,),
        out_shape=jax.ShapeDtypeStruct((experts, cap, inner), F32),
        in_specs=[
            pl.BlockSpec((cap, tokens), lambda i: (i, 0)),
            pl.BlockSpec((tokens, width), lambda i: (0, 0)),
        ]
        + specs,
        out_specs=pl.BlockSpec((1, cap, inner), lambda i: (i, 0, 0)),
        scratch_shapes=[pltpu.VMEM((cap, width), BF)],
        compiler_params=pltpu.CompilerParams(vmem_limit_bytes=VMEM_CAP),
        cost_estimate=pl.CostEstimate(
            flops=2 * experts * cap * width * (inner + tokens),
            bytes_accessed=2 * experts * inner * width,
            transcendentals=0,
        ),
        name="out_back",
    )(sel, d, *args)


def grad_rows_kernel(n, half, dest, x, *refs):
    low, high = refs[:n], refs[n : 2 * n]
    o, picked, y = refs[2 * n :]
    e = pl.program_id(0)
    pos = ring_pos(n)
    cap = low[0].shape[1]
    index = e * cap + lax.broadcasted_iota(jnp.int32, (cap, x.shape[1]), 0)

    def gather(sources, sign):
        for s in range(n):
            g = ring_index((pos + n + sign * s) % n, n)
            hit = (dest[g, 0:1, :] == index) | (dest[g, 1:2, :] == index)
            sel = jnp.where(hit, 1.0, 0.0).astype(BF)
            r = pl.ds(s * cap, cap)
            picked[r] = jnp.dot(sel, x[g], preferred_element_type=F32).astype(BF)
            y[r] = sources[s][0]

    pl.when(e < half)(lambda: gather(low, -1))
    pl.when(e >= half)(lambda: gather(high, 1))
    o[0] = lax.dot_general(
        picked[...], y[...], (((0,), (0,)), ((), ())), preferred_element_type=F32
    )


def grad_rows(dest, x, got):
    n, tokens, block = x.shape
    half, cap, cols = got[0][0].shape
    experts = 2 * half
    low = pl.BlockSpec((1, cap, cols), lambda i: (jnp.minimum(i, half - 1), 0, 0))
    high = pl.BlockSpec((1, cap, cols), lambda i: (jnp.maximum(i - half, 0), 0, 0))
    return pl.pallas_call(
        functools.partial(grad_rows_kernel, n, half),
        grid=(experts,),
        out_shape=jax.ShapeDtypeStruct((experts, block, cols), F32),
        in_specs=[
            pl.BlockSpec(dest.shape, lambda i: (0, 0, 0)),
            pl.BlockSpec(x.shape, lambda i: (0, 0, 0)),
        ]
        + [low] * n
        + [high] * n,
        out_specs=pl.BlockSpec((1, block, cols), lambda i: (i, 0, 0)),
        scratch_shapes=[pltpu.VMEM((n * cap, block), BF), pltpu.VMEM((n * cap, cols), BF)],
        compiler_params=pltpu.CompilerParams(vmem_limit_bytes=VMEM_CAP),
        cost_estimate=pl.CostEstimate(
            flops=2 * experts * n * cap * block * (tokens + cols),
            bytes_accessed=2 * (x.size + experts * n * cap * cols) + 4 * experts * block * cols,
            transcendentals=0,
        ),
        name="grad_rows",
    )(dest, x, *got[0], *got[1])


def slot_dest(routes, order, experts, capacity):
    pairs = routes.shape[0] * 2
    expert = routes.reshape(pairs)
    index = jnp.arange(pairs, dtype=jnp.int32)
    place = jnp.sum(
        jnp.where(order.reshape(1, pairs) == index[:, None], index[None, :], 0), axis=1
    )
    ahead = (place[None, :] < place[:, None]) & (expert[None, :] == expert[:, None])
    slot = jnp.sum(ahead.astype(jnp.int32), axis=1)
    dest = jnp.where(slot < capacity, expert * capacity + slot, -1)
    return dest.reshape(-1, 2)


def slot_onehot(dest, slots):
    index = jnp.arange(slots, dtype=jnp.int32)[:, None]
    return ((dest[None, :, 0] == index) | (dest[None, :, 1] == index)).astype(BF)


def slot_values(dest, values, slots):
    index = jnp.arange(slots, dtype=jnp.int32)[:, None]
    zero = jnp.zeros((), values.dtype)
    return jnp.sum(
        jnp.where(dest[None, :, 0] == index, values[None, :, 0], zero)
        + jnp.where(dest[None, :, 1] == index, values[None, :, 1], zero),
        axis=1,
    )


def router_gates(logits, hot):
    top = jnp.max(jnp.where(hot, logits, MASKED), axis=1, keepdims=True)
    e = jnp.where(hot, jnp.exp(logits - top), 0.0)
    return e / jnp.sum(e, axis=1, keepdims=True)


def chosen(gates, routes):
    index = jnp.arange(gates.shape[1], dtype=jnp.int32)
    return jnp.sum(jnp.where(routes[:, :, None] == index, gates[:, None, :], 0.0), axis=2)


def angles(positions):
    half = HD // 2
    freq = ROPE_BASE ** (-(jnp.arange(half, dtype=F32) * 2.0) / HD)
    a = positions.astype(F32)[:, None] * freq[None, :]
    return jnp.tile(jnp.cos(a), (1, 2)), jnp.concatenate([-jnp.sin(a), jnp.sin(a)], axis=1)


def place_of(index):
    tail = jnp.maximum(index - PROMPT, 0)
    position = jnp.where(index < PROMPT, index, PROMPT + tail % CLEN)
    segment = jnp.where(index < PROMPT, 0, 1 + tail // CLEN)
    return position, segment


def per_device(
    tokens,
    grad_out,
    norm1_gain,
    attn_router,
    attn_routes,
    attn_order,
    w_query,
    w_kv,
    w_attn_out,
    norm2_gain,
    mlp_router,
    mlp_routes,
    mlp_order,
    w_gate,
    w_up,
    w_down,
):
    glen, width = tokens.shape
    n = lax.axis_size("ep")
    nw = lax.axis_size("ws")
    ep, ws = lax.axis_index("ep"), lax.axis_index("ws")
    ea, em = attn_router.shape[1], mlp_router.shape[1]
    acap, mcap = 2 * glen // ea, 2 * glen // em
    owners = n // em
    slots, mslots = ea * acap, em * mcap
    heads = w_query.shape[2] // HD
    block = w_query.shape[1]
    quarter = width // nw
    cut = lambda v: lax.dynamic_slice_in_dim(v, ws * quarter, quarter, v.ndim - 1)
    cut0 = lambda v: lax.dynamic_slice_in_dim(v, ws * quarter, quarter, 0)

    on_ring = n <= RING_MAX
    ring_a = [GatherRing(w_attn_out[: ea // 2])] if on_ring else []
    hop(ring_a)

    a_dest = slot_dest(attn_routes, attn_order, ea, acap)
    m_dest = slot_dest(mlp_routes, mlp_order, em, mcap)
    a_dest, m_dest = lock(ring_a, a_dest, m_dest)
    hop(ring_a)
    a_sel = slot_onehot(a_dest, slots)
    m_sel = slot_onehot(m_dest, mslots)
    a_hot = jnp.any(attn_routes[:, :, None] == jnp.arange(ea, dtype=jnp.int32), axis=1)
    m_hot = jnp.any(mlp_routes[:, :, None] == jnp.arange(em, dtype=jnp.int32), axis=1)
    token_index = jnp.arange(glen, dtype=jnp.int32)
    a_token = slot_values(a_dest, jnp.stack([token_index, token_index], 1), slots)
    other = slot_values(m_dest, mlp_routes[:, ::-1], mslots).reshape(em, mcap)
    x = tokens.astype(F32)
    inv1 = lax.rsqrt(jnp.mean(x * x, axis=1, keepdims=True) + EPS)
    xn = (x * inv1 * norm1_gain).astype(BF)
    a_sel, m_sel, a_token, xn, other = lock(ring_a, a_sel, m_sel, a_token, xn, other)
    hop(ring_a)
    slot_in = mm("st,td->sd", a_sel, xn).astype(BF).reshape(ea, acap, width)
    xn_turned = jnp.transpose(xn.reshape(glen, n, block), (1, 2, 0))
    part_w = glen // nw
    x_mine = lax.dynamic_slice_in_dim(xn, ws * part_w, part_w, 0)
    x_mine = jnp.transpose(x_mine.reshape(part_w, n, block), (1, 0, 2))
    dest_mine = lax.dynamic_slice_in_dim(a_dest.T, ws * part_w, part_w, 1)
    dest_mine = jnp.broadcast_to(jnp.tile(dest_mine, (4, 1))[None], (n, 8, part_w))
    slot_in, xn_turned, x_mine, dest_mine = lock(ring_a, slot_in, xn_turned, x_mine, dest_mine)
    hop(ring_a)
    q_cos, q_sin = angles(place_of(a_token)[0])
    cos, sin = angles(place_of(token_index)[0])
    q_cos, q_sin, cos, sin = lock(ring_a, q_cos, q_sin, cos, sin)
    hop(ring_a)
    a_logits = mm("td,de->te", xn, attn_router)
    a_gate = router_gates(a_logits, a_hot)
    a_slot_gate = slot_values(a_dest, chosen(a_gate, attn_routes), slots)
    dy_q = cut(grad_out)
    dy_slots = mm("st,td->sd", m_sel, dy_q).astype(BF)
    a_column, gate_column = a_token[:, None], a_slot_gate[:, None]
    a_column, gate_column, dy_slots, a_gate = lock(ring_a, a_column, gate_column, dy_slots, a_gate)
    hop(ring_a)
    hop(ring_a)
    w_kv, w_query = lock(ring_a, w_kv, w_query)
    dy_send = jnp.repeat(dy_slots.reshape(em, mcap, quarter), owners, axis=0)
    other = jnp.broadcast_to(jnp.repeat(other, owners, axis=0)[:, None], (n, 8, mcap))
    payloads = ((dy_send, 1), (other, 0), (x_mine, 0), (dest_mine, 1))
    if on_ring:
        (full_kv, full_query), (dy_rows, other, x_all, all_dest) = ring_kernel_gather(8, (1, 2), (w_kv, w_query), payloads)
        ring_b = [GatherRing(after(w_attn_out[ea // 2 :], full_query))]
    else:
        gather = lambda v: lax.all_gather(v, "ep", axis=1, tiled=True)
        full_kv, full_query, full_out = gather(w_kv), gather(w_query), gather(w_attn_out)
        dy_rows, other = dispatch(8, *payloads[:2])
        ring_b = []
    dy_rows, other = dy_rows.reshape(n * mcap, width), other[:, 0].reshape(-1)
    hop(ring_b)
    q_pre = mm("ecd,edj->ecj", slot_in, full_query)
    (q_pre,) = lock(ring_b, q_pre)
    hop(ring_b)
    k_pre = mm("td,dj->tj", xn, full_kv[0])
    v_pre = mm("td,dj->tj", xn, full_kv[1])
    k_pre, v_pre = lock(ring_b, k_pre, v_pre)
    hop(ring_b)
    q, k, v, attn_o, gated_o, lse = attend(
        q_pre.reshape(slots, -1), k_pre, v_pre, q_cos, q_sin, cos, sin, a_column, gate_column
    )
    (gated_o,) = lock(ring_b, gated_o)
    hop(ring_b)
    dy_down = mm("rd,df->rf", dy_rows, w_down)
    (dy_down,) = lock(ring_b, dy_down)
    for _ in range(3):
        hop(ring_b)
    gated_o = gated_o.reshape(ea, acap, heads * HD)
    slots_travel = n <= RING_MAX and n * slots <= ea * width
    ring_o = [GatherRing(gated_o)] if slots_travel else []
    hop(ring_o)
    if on_ring:
        branch = out_project(a_sel, gated_o, ring_a + ring_b, width)
    else:
        branch = project_back(a_sel, gated_o, (full_out,))
    (branch,) = lock(ring_o, branch)
    hop(ring_o)
    gain2 = cut0(norm2_gain)[None]
    hidden, inv2, hn, hn_slots = mix(branch, cut(tokens), gain2, m_sel, 0)
    hidden, inv2, hn, hn_slots = lock(ring_o, hidden, inv2, hn, hn_slots)
    x_q = cut(tokens).astype(F32)
    router_q = lax.dynamic_slice_in_dim(mlp_router, ws * quarter, quarter, 0)
    hn_slots = jnp.repeat(hn_slots.reshape(em, mcap, quarter), owners, axis=0)
    rows = dispatch(1, (hn_slots, 1))[0].reshape(n * mcap, width)
    (rows,) = lock(ring_o, rows)

    rows_w = glen // nw

    def mine(v):
        v = lax.dynamic_slice_in_dim(v, ws * rows_w, rows_w, 0)
        return jnp.transpose(v.reshape(rows_w, n, block), (1, 0, 2))

    hop(ring_o)
    d_gate, d_up, act_bf, down_bf, d_part, row_dgate, *spread = expert_pass(
        rows, other[:, None], dy_down, mlp_router, w_gate, w_up, owners, mcap,
        (), 6,
    )
    d_gate, d_up, act_bf, down_bf, d_part, row_dgate = lock(
        ring_o, d_gate, d_up, act_bf, down_bf, d_part, row_dgate
    )
    hop(ring_o)
    d_part = d_part.reshape(n, mcap, width)
    if on_ring:
        d_rows, m_dgate, part = give_back_part(d_part, row_dgate, act_bf, w_down, 2)
    else:
        d_rows, m_dgate = give_back(d_part, row_dgate, 2)
        part = mm("rf,df->rd", act_bf, w_down).astype(BF)
        grad_gate = mm("rd,rf->df", rows, d_gate)
        grad_up = mm("rd,rf->df", rows, d_up)
        grad_down = mm("rd,rf->df", dy_rows, down_bf)
    d_rows, m_dgate, part = lock(ring_o, d_rows, m_dgate, part)
    hop(ring_o)
    far, near = ws_to_core(part)
    m_slot_gate = m_dgate[:, 4].reshape(em, owners, mcap)[:, 0].reshape(mslots)
    m_dgate = jnp.sum(m_dgate[:, 0].reshape(em, owners, mcap), axis=1).reshape(mslots, 1)

    def by_owner(v):
        if owners > 1:
            v = jnp.sum(v.astype(F32).reshape(em, owners, mcap, quarter), axis=1).astype(BF)
        return v.reshape(mslots, quarter)

    d_rows = by_owner(d_rows)
    def per_expert(sel, values, experts):
        terms = sel.reshape(experts, -1, glen).astype(F32) * values.reshape(experts, -1, 1)
        return jnp.sum(terms, axis=1).T

    def router_back(dgate, gates):
        return (gates * (dgate - jnp.sum(gates * dgate, axis=1, keepdims=True))).astype(BF)

    m_gate = per_expert(m_sel, m_slot_gate, em)
    kept = jnp.sum(m_gate, axis=1, keepdims=True)
    m_gate = jnp.where(m_hot & (m_gate == 0.0), jnp.maximum(1.0 - kept, 0.0), m_gate)
    d_m_logits = router_back(per_expert(m_sel, m_dgate, em), m_gate)
    grad_mlp_router = mm("td,te->ed", hn, d_m_logits)
    d_hn = mm("te,de->td", d_m_logits, router_q)
    d_hidden, grad_norm2, d_hid = home(m_sel, d_rows, d_hn, hidden, inv2, gain2, dy_q, 3)
    d_hid, far, near = lock(ring_o, d_hid, far, near)
    hop(ring_o)
    part = ws_to_cross(far, near)

    if on_ring:
        raw_do = out_back(a_sel, d_hid, ring_a + ring_b, ea).reshape(slots, heads * HD)
    else:
        dh_slots = mm("st,td->sd", a_sel, d_hid).astype(BF).reshape(ea, acap, width)
        raw_do = mm("ecd,edj->ecj", dh_slots, full_out).reshape(slots, heads * HD)
    raw_do, part = lock(ring_o, raw_do, part)
    hop(ring_o)
    part = lax.all_to_all(part.astype(BF).reshape(n, mcap, quarter), "ep", 0, 0, tiled=True)
    d_q, d_kv, a_dgate, *spread = attend_back(
        raw_do, attn_o, gate_column, q, k, v, lse, q_cos, q_sin, cos, sin, a_column,
        (), 7,
    )
    a_dgate = lax.psum(a_dgate[0], "ws")
    d_q = d_q.reshape(ea, acap, heads * HD)
    d_q, d_kv, part = lock(ring_o, d_q, d_kv, part)

    d_a_logits = router_back(per_expert(a_sel, a_dgate, ea), a_gate)
    arouter_q = lax.dynamic_slice_in_dim(attn_router, ws * quarter, quarter, 0)
    grad_attn_router = mm("td,te->ed", cut(xn), d_a_logits)
    d_xn_router = mm("te,de->td", d_a_logits, arouter_q)
    unit1 = x_q * inv1
    gain1 = cut0(norm1_gain)[None]
    expert_out = by_owner(part)
    mlp_branch = mm("st,sd->td", m_sel, (expert_out.astype(F32) * m_slot_gate[:, None]).astype(BF))
    layer_out = (hidden + mlp_branch).astype(BF)

    if slots_travel:
        all_dq, grad_kv, h_all, grad_tokens, layer_out, stats, *grads = last_stage(
            9, d_q, d_kv, xn_turned, a_sel, full_query, full_kv, mine(d_hid), d_hidden, unit1, d_xn_router, inv1, gain1, layer_out, grad_norm2, grad_attn_router, grad_mlp_router,
            rows, dy_rows, d_gate, d_up, down_bf,
        )
        grad_gate, grad_up, grad_down = [g.astype(F32) for g in grads]
        grad_query = grad_slots(all_dest, x_all, all_dq)
        grad_attn_out = grad_rows(all_dest, h_all, ring_o[0].got)
    else:
        d_xn = ws_reduce(project_back(a_sel, d_q, (full_query,), d_kv, full_kv), 4) + d_xn_router
        grad_norm1 = jnp.sum(d_xn * unit1, axis=0, keepdims=True)
        w1 = d_xn * gain1
        mean1 = lax.psum(jnp.sum(w1 * unit1, axis=1, keepdims=True), "ws") / width
        grad_tokens = (d_hidden + inv1 * (w1 - unit1 * mean1)).astype(BF)
        grad_tokens = ws_spread(grad_tokens, 5)
        dh_slots = mm("st,td->sd", a_sel, d_hid).astype(BF).reshape(ea, acap, width)
        scatter = lambda g: lax.psum_scatter(g.astype(BF), "ep", scatter_dimension=1, tiled=True)
        grad_query = scatter(mm("ecd,ecj->edj", slot_in, d_q)).astype(F32)
        grad_attn_out = scatter(mm("ecd,ecj->edj", dh_slots, gated_o)).astype(F32)
        grad_kv = scatter(mm("td,ktj->kdj", xn, d_kv)).astype(F32)
        layer_out = ws_gather(layer_out)
        norms = jnp.where(jnp.arange(8)[:, None] == 0, grad_norm1, grad_norm2)
        stats = collect(jnp.concatenate([norms, grad_attn_router, grad_mlp_router]), 10)
    grad_tokens = grad_tokens.astype(F32)

    grad_norm1, grad_norm2 = stats[0], stats[1]
    grad_attn_router, grad_mlp_router = stats[8 : 8 + ea].T, stats[8 + ea :].T
    return (
        layer_out,
        grad_tokens,
        grad_norm1,
        grad_attn_router,
        grad_query,
        grad_kv,
        grad_attn_out,
        grad_norm2,
        grad_mlp_router,
        grad_gate,
        grad_up,
        grad_down,
    )


def solution(mesh):
    rows, wide = P("ep", None), P(None, ("ep", "ws"))
    attn = P(None, "ep", "ws")
    return jax.shard_map(
        per_device,
        mesh=mesh,
        in_specs=(rows, rows, P(), P(), rows, rows, attn, attn, attn, P(), P(), rows, rows)
        + (wide,) * 3,
        out_specs=(rows, rows, P(), P(), attn, attn, attn, P(), P()) + (wide,) * 3,
        check_vma=False,
    )
```

```python
import functools
import math

import jax
import jax.numpy as jnp
from jax import lax
from jax.experimental import pallas as pl
from jax.experimental.pallas import tpu as pltpu
from jax.sharding import PartitionSpec as P

HD = 128
PROMPT = 256
CLEN = 128
EPS = 1e-06
ROPE_BASE = 10000.0
MASKED = -1e30
BF = jnp.bfloat16
F32 = jnp.float32
RING_MAX = 8


def mm(eq, a, b):
    return jnp.einsum(eq, a, b, preferred_element_type=F32)


def after(value, *deps):
    return lax.optimization_barrier((value,) + deps)[0]


def ring_index(p, n):
    h = p // (n // 2)
    return 2 * p * (1 - h) + h * (2 * (n - 1 - p) + 1)


def ring_pos(n):
    i = lax.axis_index("ep")
    h = i // 2
    return h + (i % 2) * (n - 1 - 2 * h)


def ring_perms(n):
    fw = [(ring_index(p, n), ring_index((p + 1) % n, n)) for p in range(n)]
    return fw, [(b, a) for a, b in fw]


def ring_gather(x, dim):
    n = lax.axis_size("ep")
    half = x.shape[0] // 2
    if n > RING_MAX:
        full = lax.all_gather(x, "ep", axis=dim, tiled=True)
        return (full[:half], full[half:]), (full,)
    fw, bw = ring_perms(n)
    pos = ring_pos(n)
    a, b = x[:half], x[half:]
    shape = list(a.shape)
    size = shape[dim]
    shape[dim] = size * n
    out_a, out_b = jnp.zeros(shape, x.dtype), jnp.zeros(shape, x.dtype)
    me = lax.axis_index("ep")
    out_a = lax.dynamic_update_slice_in_dim(out_a, a, me * size, dim)
    out_b = lax.dynamic_update_slice_in_dim(out_b, b, me * size, dim)
    for s in range(1, n):
        a = lax.ppermute(a, "ep", fw)
        b = lax.ppermute(b, "ep", bw)
        src_a = ring_index((pos + n - s) % n, n)
        src_b = ring_index((pos + s) % n, n)
        out_a = lax.dynamic_update_slice_in_dim(out_a, a, src_a * size, dim)
        out_b = lax.dynamic_update_slice_in_dim(out_b, b, src_b * size, dim)
    return (out_a, out_b), (a, b)


class GatherRing:
    def __init__(self, x):
        half = x.shape[0] // 2
        self.moving = [x[:half], x[half:]]
        self.got = [[self.moving[0]], [self.moving[1]]]

    def hop(self):
        perms = ring_perms(lax.axis_size("ep"))
        self.moving = [lax.ppermute(v, "ep", p) for v, p in zip(self.moving, perms)]
        for k in range(2):
            self.got[k].append(self.moving[k])

    def settle(self, values):
        self.moving = list(values)
        for k in range(2):
            self.got[k][-1] = self.moving[k]


def lock(rings, *values):
    flat = [m for r in rings for m in r.moving] + list(values)
    flat = list(lax.optimization_barrier(tuple(flat))) if flat else []
    for r in rings:
        r.settle([flat.pop(0), flat.pop(0)])
    return flat


def hop(rings):
    for r in rings:
        r.hop()


CORE = [(0, 1), (1, 0), (2, 3), (3, 2)]
CROSS = [(0, 2), (2, 0), (1, 3), (3, 1)]


def ws_stack(q):
    w = lax.axis_index("ws")
    x, c = w // 2, w % 2
    other = lax.ppermute(q, "ws", CROSS)
    mine = jnp.where(x == 0, jnp.stack([q, other]), jnp.stack([other, q]))
    peer = lax.ppermute(mine, "ws", CORE)
    both = jnp.where(c == 0, jnp.stack([mine, peer], 1), jnp.stack([peer, mine], 1))
    return both.reshape((4,) + q.shape)


def ws_gather(q):
    rows, cols = q.shape
    return jnp.transpose(ws_stack(q), (1, 0, 2)).reshape(rows, 4 * cols)


def quarters(p):
    w = lax.axis_index("ws")
    x, c = w // 2, w % 2
    cols = p.shape[1] // 4
    take = lambda q: lax.dynamic_slice_in_dim(p, q * cols, cols, 1)
    return [take((1 - x) * 2 + 1 - c), take(x * 2 + 1 - c), take((1 - x) * 2 + c), take(x * 2 + c)]


MESH_ID = pl.DeviceIdType.MESH
VMEM_CAP = 60 * 1024 * 1024


def any_spec():
    return pl.BlockSpec(memory_space=pl.ANY)


def vmem_spec():
    return pl.BlockSpec(memory_space=pltpu.VMEM)


def ws_places():
    w = lax.axis_index("ws")
    x, c = w // 2, w % 2
    return w, x, c, x * 2 + 1 - c, (1 - x) * 2 + c


def meet(peers):
    barrier = pltpu.get_barrier_semaphore()
    for peer in peers:
        pl.semaphore_signal(barrier, inc=1, device_id=peer, device_id_type=MESH_ID)
    pl.semaphore_wait(barrier, len(peers))


def push(src, dst, send, recv, peer):
    return pltpu.make_async_remote_copy(
        src_ref=src, dst_ref=dst, send_sem=send, recv_sem=recv, device_id=peer, device_id_type=MESH_ID
    )


def columns(q, cols):
    return pl.ds(pl.multiple_of(q * cols, cols), cols)


def params(cid):
    return pltpu.CompilerParams(
        collective_id=cid, has_side_effects=True, vmem_limit_bytes=VMEM_CAP
    )


def reduce_kernel(chunks, p, o, rc, sx, rx, cs, cr, xs, xr):
    w, x, c, core, cross = ws_places()
    rows, cols = o.shape
    step = rows // chunks
    meet([{"ws": core}, {"ws": cross}])
    sent = []
    for k in range(chunks):
        r = pl.ds(k * step, step)
        for j, far in enumerate((1 - x, x)):
            src = p.at[r, columns(far * 2 + 1 - c, cols)]
            copy = push(src, rc.at[j, r], cs.at[j, k], cr.at[j, k], {"ws": core})
            copy.start()
            sent.append(copy)
    cross_sent = []
    for k in range(chunks):
        r = pl.ds(k * step, step)
        sent[2 * k].wait_recv()
        total = p[r, columns((1 - x) * 2 + c, cols)].astype(F32) + rc[0, r].astype(F32)
        sx[r] = total.astype(BF)
        copy = push(sx.at[r], rx.at[r], xs.at[k], xr.at[k], {"ws": cross})
        copy.start()
        cross_sent.append(copy)
    for k in range(chunks):
        r = pl.ds(k * step, step)
        sent[2 * k + 1].wait_recv()
        near = p[r, columns(x * 2 + c, cols)].astype(F32) + rc[1, r].astype(F32)
        cross_sent[k].wait_recv()
        o[r] = near + rx[r].astype(F32)
    for copy in sent + cross_sent:
        copy.wait_send()


def ws_reduce(p, cid, chunks=4):
    rows, cols = p.shape[0], p.shape[1] // 4
    dma = pltpu.SemaphoreType.DMA
    return pl.pallas_call(
        functools.partial(reduce_kernel, chunks),
        out_shape=jax.ShapeDtypeStruct((rows, cols), F32),
        in_specs=[vmem_spec()],
        out_specs=vmem_spec(),
        scratch_shapes=[
            pltpu.VMEM((2, rows, cols), BF),
            pltpu.VMEM((rows, cols), BF),
            pltpu.VMEM((rows, cols), BF),
            dma((2, chunks)),
            dma((2, chunks)),
            dma((chunks,)),
            dma((chunks,)),
        ],
        compiler_params=params(cid),
        name=f"ws_reduce_{cid}",
    )(p)


def to_lanes(column):
    return jnp.broadcast_to(column, (column.shape[0], 128)).T[:8]


def to_column(lanes):
    return jnp.broadcast_to(lanes[:1], (128, lanes.shape[1])).T[:, :1]


def sum_over_ws(stat, stats, send, recv, mates):
    copies = []
    for j, peer in enumerate(mates):
        copy = push(stat, stats.at[j], send.at[j], recv.at[j], peer)
        copy.start()
        copies.append(copy)
    for copy in copies:
        copy.wait()
    return stat[...] + stats[0] + stats[1] + stats[2]


def mix_kernel(chunks, p, xq, gain, sel, o, inv, hn, picked, rc, sx, rx, stat, stats, cs, cr, xs, xr, ss, sr):
    w, x, c, core, cross = ws_places()
    mates = [{"ws": core}, {"ws": cross}, {"ws": (1 - x) * 2 + 1 - c}]
    rows, cols = o.shape
    step = rows // chunks
    meet(mates)
    sent = []
    for k in range(chunks):
        r = pl.ds(k * step, step)
        for j, far in enumerate((1 - x, x)):
            src = p.at[r, columns(far * 2 + 1 - c, cols)]
            copy = push(src, rc.at[j, r], cs.at[j, k], cr.at[j, k], {"ws": core})
            copy.start()
            sent.append(copy)
    cross_sent = []
    for k in range(chunks):
        r = pl.ds(k * step, step)
        sent[2 * k].wait_recv()
        total = p[r, columns((1 - x) * 2 + c, cols)].astype(F32) + rc[0, r].astype(F32)
        sx[r] = total.astype(BF)
        copy = push(sx.at[r], rx.at[r], xs.at[k], xr.at[k], {"ws": cross})
        copy.start()
        cross_sent.append(copy)
    for k in range(chunks):
        r = pl.ds(k * step, step)
        sent[2 * k + 1].wait_recv()
        near = p[r, columns(x * 2 + c, cols)].astype(F32) + rc[1, r].astype(F32)
        cross_sent[k].wait_recv()
        total = near + rx[r].astype(F32) + xq[r].astype(F32)
        o[r] = total
        stat[:, k * step : (k + 1) * step] = to_lanes(jnp.sum(total * total, axis=1, keepdims=True))
    total = sum_over_ws(stat, stats, ss, sr, mates)
    inverse = lax.rsqrt(to_column(total) / (4 * cols) + EPS)
    inv[...] = inverse
    hn[...] = (o[...] * inverse * gain[...]).astype(BF)
    picked[...] = jnp.dot(sel[...], hn[...], preferred_element_type=F32).astype(BF)
    for copy in sent + cross_sent:
        copy.wait_send()


def mix(p, xq, gain, sel, cid, chunks=4):
    rows, cols = xq.shape
    slots = sel.shape[0]
    dma = pltpu.SemaphoreType.DMA
    return pl.pallas_call(
        functools.partial(mix_kernel, chunks),
        out_shape=(
            jax.ShapeDtypeStruct((rows, cols), F32),
            jax.ShapeDtypeStruct((rows, 1), F32),
            jax.ShapeDtypeStruct((rows, cols), BF),
            jax.ShapeDtypeStruct((slots, cols), BF),
        ),
        in_specs=[vmem_spec()] * 4,
        out_specs=(vmem_spec(),) * 4,
        scratch_shapes=[
            pltpu.VMEM((2, rows, cols), BF),
            pltpu.VMEM((rows, cols), BF),
            pltpu.VMEM((rows, cols), BF),
            pltpu.VMEM((8, rows), F32),
            pltpu.VMEM((3, 8, rows), F32),
            dma((2, chunks)),
            dma((2, chunks)),
            dma((chunks,)),
            dma((chunks,)),
            dma((3,)),
            dma((3,)),
        ],
        compiler_params=params(cid),
        name=f"mix_{cid}",
    )(p, xq, gain, sel)


def home_kernel(sel, d, extra, hidden, inv, gain, dy, dh, gn, o, stat, stats, mine, own, ss, sr, xs, xr, cs, cr):
    w, x, c, core, cross = ws_places()
    mates = [{"ws": core}, {"ws": cross}, {"ws": (1 - x) * 2 + 1 - c}]
    rows, cols = hidden.shape
    meet(mates)
    total = lax.dot_general(sel[...], d[...], (((0,), (0,)), ((), ())), preferred_element_type=F32)
    total += extra[...]
    unit = hidden[...] * inv[...]
    gn[...] = jnp.broadcast_to(jnp.sum(total * unit, axis=0, keepdims=True), gn.shape)
    weighted = total * gain[...]
    stat[...] = to_lanes(jnp.sum(weighted * unit, axis=1, keepdims=True))
    mean = to_column(sum_over_ws(stat, stats, ss, sr, mates)) / (4 * cols)
    result = dy[...].astype(F32) + inv[...] * (weighted - unit * mean)
    dh[...] = result
    mine[...] = result.astype(BF)
    place = o.at[:, columns(w, cols)]
    local = pltpu.make_async_copy(mine, place, own)
    over = push(mine, place, xs, xr, {"ws": cross})
    beside_ = push(mine, place, cs.at[0], cr.at[0], {"ws": core})
    for copy in (local, over, beside_):
        copy.start()
    over.wait_recv()
    block = o.at[:, columns(cross, cols)]
    onward = push(block, block, cs.at[1], cr.at[1], {"ws": core})
    onward.start()
    for copy in (local, beside_, onward):
        copy.wait()
    over.wait_send()


def home(sel, d, extra, hidden, inv, gain, dy, cid):
    rows, cols = hidden.shape
    dma = pltpu.SemaphoreType.DMA
    return pl.pallas_call(
        home_kernel,
        out_shape=(
            jax.ShapeDtypeStruct((rows, cols), F32),
            jax.ShapeDtypeStruct((8, cols), F32),
            jax.ShapeDtypeStruct((rows, 4 * cols), BF),
        ),
        in_specs=[vmem_spec()] * 7,
        out_specs=(vmem_spec(), vmem_spec(), any_spec()),
        scratch_shapes=[
            pltpu.VMEM((8, rows), F32),
            pltpu.VMEM((3, 8, rows), F32),
            pltpu.VMEM((rows, cols), BF),
            dma,
            dma((3,)),
            dma((3,)),
            dma,
            dma,
            dma((2,)),
            dma((2,)),
        ],
        compiler_params=params(cid),
        name=f"home_{cid}",
    )(sel, d, extra, hidden, inv, gain, dy)


def spread_kernel(chunks, q, o, own, cs, cr, xs, xr):
    w, x, c, core, cross = ws_places()
    rows, cols = q.shape
    step = rows // chunks
    meet([{"ws": core}, {"ws": cross}])
    local = pltpu.make_async_copy(q, o.at[:, columns(w, cols)], own)
    local.start()
    crossing, coring = [], []
    for k in range(chunks):
        r = pl.ds(k * step, step)
        dst = o.at[r, columns(w, cols)]
        copy = push(q.at[r], dst, xs.at[k], xr.at[k], {"ws": cross})
        copy.start()
        crossing.append(copy)
        copy = push(q.at[r], dst, cs.at[0, k], cr.at[0, k], {"ws": core})
        copy.start()
        coring.append(copy)
    for k in range(chunks):
        r = pl.ds(k * step, step)
        crossing[k].wait_recv()
        block = o.at[r, columns(cross, cols)]
        copy = push(block, block, cs.at[1, k], cr.at[1, k], {"ws": core})
        copy.start()
        coring.append(copy)
    local.wait()
    for copy in coring:
        copy.wait()
    for copy in crossing:
        copy.wait_send()


def ws_spread(q, cid, chunks=4):
    rows, cols = q.shape
    dma = pltpu.SemaphoreType.DMA
    return pl.pallas_call(
        functools.partial(spread_kernel, chunks),
        out_shape=jax.ShapeDtypeStruct((rows, 4 * cols), q.dtype),
        in_specs=[any_spec()],
        out_specs=any_spec(),
        scratch_shapes=[dma, dma((2, chunks)), dma((2, chunks)), dma((chunks,)), dma((chunks,))],
        compiler_params=params(cid),
        name=f"ws_spread_{cid}",
    )(q)


class Dispatch:
    def __init__(self, n, axes, qs, os, own, ps, pr, cs, cr, xs, xr):
        self.n, self.axes, self.qs, self.os = n, axes, qs, os
        self.own, self.ps, self.pr, self.cs, self.cr, self.xs, self.xr = own, ps, pr, cs, cr, xs, xr
        self.e = lax.axis_index("ep")
        self.w, _, _, self.core, self.cross = ws_places()
        self.steps = [(i, k) for k in range(n) for i in range(len(axes))]

    def window(self, i, g, q):
        rows, cols = self.qs[i].shape[1:]
        if self.axes[i] == 0:
            return self.os[i].at[g, pl.ds(pl.multiple_of(q * rows, rows), rows)]
        return self.os[i].at[g, :, columns(q, cols)]

    def local(self, i):
        return pltpu.make_async_copy(
            self.qs[i].at[self.e], self.window(i, self.e, self.w), self.own.at[i]
        )

    def sent(self, i, k):
        d = (self.e + k) % self.n
        dst = self.window(i, self.e, self.w)
        return push(self.qs[i].at[d], dst, self.ps.at[i, k], self.pr.at[i, k], {"ep": d})

    def to_cross(self, i, k):
        block = self.window(i, (self.e + self.n - k) % self.n, self.w)
        return push(block, block, self.xs.at[i, k], self.xr.at[i, k], {"ws": self.cross})

    def to_core(self, i, j, k):
        block = self.window(i, (self.e + self.n - k) % self.n, self.cross if j else self.w)
        return push(block, block, self.cs.at[i, j, k], self.cr.at[i, j, k], {"ws": self.core})

    def start(self):
        for i, k in self.steps:
            (self.local(i) if k == 0 else self.sent(i, k)).start()

    def hand_on(self):
        for i, k in self.steps:
            if k == 0:
                self.local(i).wait()
            else:
                self.sent(i, k).wait_recv()
            self.to_cross(i, k).start()
            self.to_core(i, 0, k).start()

    def onward(self):
        for i, k in self.steps:
            self.to_cross(i, k).wait_recv()
            self.to_core(i, 1, k).start()

    def run(self):
        self.hand_on()
        self.onward()

    def finish(self):
        for i, k in self.steps:
            if k > 0:
                self.sent(i, k).wait_send()
            self.to_cross(i, k).wait_send()
            self.to_core(i, 0, k).wait()
            self.to_core(i, 1, k).wait()


def dispatch_peers(n):
    e = lax.axis_index("ep")
    _, _, _, core, cross = ws_places()
    return [{"ep": (e + k) % n} for k in range(1, n)] + [{"ws": core}, {"ws": cross}]


def dispatch_sems(m, n):
    dma = pltpu.SemaphoreType.DMA
    return [dma((m,))] + [dma((m, n))] * 2 + [dma((m, 2, n))] * 2 + [dma((m, n))] * 2


def dispatched(q, axis):
    n, rows, cols = q.shape
    shape = (n, 4 * rows, cols) if axis == 0 else (n, rows, 4 * cols)
    return jax.ShapeDtypeStruct(shape, q.dtype)


def dispatch_kernel(n, axes, *refs):
    m = len(axes)
    meet(dispatch_peers(n))
    work = Dispatch(n, axes, refs[:m], refs[m : 2 * m], *refs[2 * m :])
    work.start()
    work.run()
    work.finish()


def dispatch(cid, *payloads):
    n = payloads[0][0].shape[0]
    m = len(payloads)
    return pl.pallas_call(
        functools.partial(dispatch_kernel, n, [axis for _, axis in payloads]),
        out_shape=[dispatched(*payload) for payload in payloads],
        in_specs=[any_spec()] * m,
        out_specs=[any_spec()] * m,
        scratch_shapes=dispatch_sems(m, n),
        compiler_params=params(cid),
        name=f"dispatch_{cid}",
    )(*[q for q, _ in payloads])


def return_kernel(n, p, dg, o, dgo, rc, sx, rx, st, dgr, dgs, own, cs, cr, xs, xr, ps, pr, gs, gr, hs, hr):
    e = lax.axis_index("ep")
    w, x, c, core, cross = ws_places()
    diag = (1 - x) * 2 + 1 - c
    cols = o.shape[2]
    peers = [{"ep": (e + k) % n} for k in range(1, n)]
    meet(peers + [{"ws": core}, {"ws": cross}, {"ws": diag}])
    order = list(range(1, n)) + [0]
    coring = {}
    for k in order:
        g = (e + k) % n
        for j, far in enumerate((1 - x, x)):
            src = p.at[g, :, columns(far * 2 + 1 - c, cols)]
            copy = push(src, rc.at[j, k], cs.at[j, k], cr.at[j, k], {"ws": core})
            copy.start()
            coring[j, k] = copy
    gates = []
    for j, peer in enumerate((core, cross, diag)):
        copy = push(dg, dgr.at[j], gs.at[j], gr.at[j], {"ws": peer})
        copy.start()
        gates.append(copy)
    crossing = {}
    for k in order:
        g = (e + k) % n
        coring[0, k].wait_recv()
        total = p[g, :, columns((1 - x) * 2 + c, cols)].astype(F32) + rc[0, k].astype(F32)
        sx[k] = total.astype(BF)
        crossing[k] = push(sx.at[k], rx.at[k], xs.at[k], xr.at[k], {"ws": cross})
        crossing[k].start()
    for copy in gates:
        copy.wait_recv()
    dgs[...] = dg[...] + dgr[0] + dgr[1] + dgr[2]
    home = []
    for k in order:
        g = (e + k) % n
        coring[1, k].wait_recv()
        near = p[g, :, columns(x * 2 + c, cols)].astype(F32) + rc[1, k].astype(F32)
        crossing[k].wait_recv()
        st[k] = (near + rx[k].astype(F32)).astype(BF)
        if k > 0:
            copy = push(st.at[k], o.at[e], ps.at[k], pr.at[k], peers[k - 1])
            copy.start()
            home.append(copy)
            copy = push(dgs.at[g], dgo.at[e], hs.at[k], hr.at[k], peers[k - 1])
            copy.start()
            home.append(copy)
        else:
            copy = pltpu.make_async_copy(st.at[0], o.at[e], own.at[0])
            copy.start()
            home.append(copy)
            copy = pltpu.make_async_copy(dgs.at[g], dgo.at[e], own.at[1])
            copy.start()
            home.append(copy)
    for copy in home:
        copy.wait()
    for copy in gates + list(coring.values()) + list(crossing.values()):
        copy.wait_send()


def give_back(p, dg, cid):
    n, rows, cols = p.shape[0], p.shape[1], p.shape[2] // 4
    dma = pltpu.SemaphoreType.DMA
    return pl.pallas_call(
        functools.partial(return_kernel, n),
        out_shape=(jax.ShapeDtypeStruct((n, rows, cols), BF), jax.ShapeDtypeStruct(dg.shape, F32)),
        in_specs=[vmem_spec(), vmem_spec()],
        out_specs=(any_spec(), any_spec()),
        scratch_shapes=[
            pltpu.VMEM((2, n, rows, cols), BF),
            pltpu.VMEM((n, rows, cols), BF),
            pltpu.VMEM((n, rows, cols), BF),
            pltpu.VMEM((n, rows, cols), BF),
            pltpu.VMEM((3,) + dg.shape, F32),
            pltpu.VMEM(dg.shape, F32),
            dma((2,)),
            dma((2, n)),
            dma((2, n)),
            dma((n,)),
            dma((n,)),
            dma((n,)),
            dma((n,)),
            dma((3,)),
            dma((3,)),
            dma((n,)),
            dma((n,)),
        ],
        compiler_params=params(cid),
        name=f"give_back_{cid}",
    )(p, dg)


def return_part_kernel(n, p, dg, act_h, down_h, o, dgo, part0, part1, part2, part3, rc, sx, rx, st, dgr, dgs,
                       act, down, stage, own, cs, cr, xs, xr, ps, pr, gs, gr, hs, hr, ls, os_):
    e = lax.axis_index("ep")
    w, x, c, core, cross = ws_places()
    diag = (1 - x) * 2 + 1 - c
    cols = o.shape[2]
    size = down.shape[0] // n
    meet([{"ep": (e + k) % n} for k in range(1, n)] + [{"ws": core}, {"ws": cross}, {"ws": diag}])

    def to_core(k, j):
        far = (1 - x) if j == 0 else x
        src = p.at[(e + k) % n, :, columns(far * 2 + 1 - c, cols)]
        return push(src, rc.at[j, k], cs.at[j, k], cr.at[j, k], {"ws": core})

    def to_cross(k):
        return push(sx.at[k], rx.at[k], xs.at[k], xr.at[k], {"ws": cross})

    def to_home(k):
        peer = {"ep": (e + k) % n}
        return (
            push(st.at[k], o.at[e], ps.at[k], pr.at[k], peer),
            push(dgs.at[(e + k) % n], dgo.at[e], hs.at[k], hr.at[k], peer),
        )

    @pl.loop(0, n)
    def _(i):
        to_core((i + 1) % n, 0).start()
        to_core((i + 1) % n, 1).start()

    loads = []
    for i, (src, dst) in enumerate(((act_h, act), (down_h, down))):
        copy = pltpu.make_async_copy(src, dst, ls.at[i])
        copy.start()
        loads.append(copy)
    gates = []
    for j, peer in enumerate((core, cross, diag)):
        copy = push(dg, dgr.at[j], gs.at[j], gr.at[j], {"ws": peer})
        copy.start()
        gates.append(copy)

    @pl.loop(0, n)
    def _(i):
        k = (i + 1) % n
        to_core(k, 0).wait_recv()
        mine = p[(e + k) % n, :, columns((1 - x) * 2 + c, cols)]
        sx[k] = (mine.astype(F32) + rc[0, k].astype(F32)).astype(BF)
        to_cross(k).start()

    for copy in gates:
        copy.wait_recv()
    dgs[...] = dg[...] + dgr[0] + dgr[1] + dgr[2]
    for copy in loads:
        copy.wait()

    per = n // 4

    def out_start(i):
        for j, part in enumerate((part0, part1, part2, part3)):

            @pl.when(i // per == j)
            def _():
                dst = part.at[:, columns(i % per, size)]
                pltpu.make_async_copy(stage.at[i % 2], dst, os_.at[i % 2]).start()

    def out_wait(i):
        pltpu.make_async_copy(stage.at[i % 2], part0.at[:, pl.ds(0, size)], os_.at[i % 2]).wait()

    def tile_of(i):
        r = i // per
        far, other = 1 - r % 2, 1 - r // 2
        quarter = (x + far * (1 - 2 * x)) * 2 + c + other * (1 - 2 * c)
        return quarter * per + i % per

    @pl.loop(0, n)
    def _(i):
        k = (i + 1) % n
        terms = lax.dot_general(
            act[...],
            down[pl.ds(pl.multiple_of(tile_of(i) * size, size), size)],
            (((1,), (1,)), ((), ())),
            preferred_element_type=F32,
        )

        @pl.when(i > 1)
        def _():
            out_wait(i - 2)

        stage[i % 2] = terms.astype(BF)
        out_start(i)
        to_core(k, 1).wait_recv()
        mine = p[(e + k) % n, :, columns(x * 2 + c, cols)]
        near = mine.astype(F32) + rc[1, k].astype(F32)
        to_cross(k).wait_recv()
        st[k] = (near + rx[k].astype(F32)).astype(BF)

        @pl.when(i < n - 1)
        def _():
            for copy in to_home(k):
                copy.start()

    last = [
        pltpu.make_async_copy(st.at[0], o.at[e], own.at[0]),
        pltpu.make_async_copy(dgs.at[e], dgo.at[e], own.at[1]),
    ]
    for copy in last:
        copy.start()
    for i in range(n - 2, n):
        out_wait(i)
    for copy in last:
        copy.wait()
    for copy in gates:
        copy.wait_send()

    @pl.loop(0, n)
    def _(k):
        to_core(k, 0).wait_send()
        to_core(k, 1).wait_send()
        to_cross(k).wait_send()

    @pl.loop(1, n)
    def _(k):
        for copy in to_home(k):
            copy.wait()


def give_back_part(p, dg, act, down, cid):
    n, cap, cols = p.shape[0], p.shape[1], p.shape[2] // 4
    dma = pltpu.SemaphoreType.DMA
    vm = lambda a: pltpu.VMEM(a.shape, a.dtype)
    count, width = act.shape[0], down.shape[0]
    return pl.pallas_call(
        functools.partial(return_part_kernel, n),
        out_shape=(
            jax.ShapeDtypeStruct((n, cap, cols), BF),
            jax.ShapeDtypeStruct(dg.shape, F32),
        )
        + (jax.ShapeDtypeStruct((count, width // 4), BF),) * 4,
        in_specs=[vmem_spec(), vmem_spec(), any_spec(), any_spec()],
        out_specs=(any_spec(),) * 6,
        scratch_shapes=[
            pltpu.VMEM((2, n, cap, cols), BF),
            pltpu.VMEM((n, cap, cols), BF),
            pltpu.VMEM((n, cap, cols), BF),
            pltpu.VMEM((n, cap, cols), BF),
            pltpu.VMEM((3,) + dg.shape, F32),
            pltpu.VMEM(dg.shape, F32),
            vm(act),
            vm(down),
            pltpu.VMEM((2, count, width // n), BF),
            dma((2,)),
            dma((2, n)),
            dma((2, n)),
            dma((n,)),
            dma((n,)),
            dma((n,)),
            dma((n,)),
            dma((3,)),
            dma((3,)),
            dma((n,)),
            dma((n,)),
            dma((2,)),
            dma((2,)),
        ],
        compiler_params=params(cid),
        name=f"give_back_part_{cid}",
    )(p, dg, act, down)


def last_kernel(n, dq, dkv, xt, sel, wq, wkv, hm, dh, unit, inv, gain, lo, gn2, gm, dg, gates, router, xq, *refs):
    grads_in, refs = refs[:5], refs[5:]
    all_dq, gkv, ha, gt_all, lo_all, gv_all, *grads_out = refs[:9]
    (wt, kwt, rows, pt, rc, sx, rx, near, kvs, kvr, stat, stats, gt, vs, vr,
     wl, own, qs, qr, ks, kr, cs, cr, xs, xr, ss, sr, ts, tr, vps, vpr, vws, vwr) = refs[9:42]
    held, (stage, gl, go, dgr, gs, gr, *dsems) = refs[42:47], refs[47:]
    e = lax.axis_index("ep")
    w, x, c, core, cross = ws_places()
    diag = (1 - x) * 2 + 1 - c
    mates = [{"ws": core}, {"ws": cross}, {"ws": diag}]
    pos = ring_pos(n)
    right = {"ep": ring_index((pos + 1) % n, n)}
    left = {"ep": ring_index((pos + n - 1) % n, n)}
    experts, cap, inner = dq.shape
    tokens, cols = dh.shape
    over_last = (((1,), (1,)), ((), ()))
    first = (((0,), (0,)), ((), ()))

    order = ((1 - x) * 2 + 1 - c, x * 2 + 1 - c, (1 - x) * 2 + c, x * 2 + c)

    def load(t):
        r = columns(order[t], cols)
        return (
            pltpu.make_async_copy(wq.at[:, r], wt.at[t % 2], wl.at[t % 2, 0]),
            pltpu.make_async_copy(wkv.at[:, r], kwt.at[t % 2], wl.at[t % 2, 1]),
        )

    for t in range(2):
        for copy in load(t):
            copy.start()
    meet([{"ep": (e + k) % n} for k in range(1, n)] + mates)

    terms = []
    for j, peer in enumerate(mates):
        copy = push(dg, dgr.at[j], gs.at[j], gr.at[j], peer)
        copy.start()
        terms.append(copy)

    each = experts // 4

    def dq_copy(f, s, fresh=False):
        peer, sign = (right, -1) if f % 2 == 0 else (left, 1)
        part = pl.ds((f % 2 * 2 + f // 2) * each, each)
        dst = all_dq.at[ring_index((pos + n + sign * s) % n, n), part]
        return push(dq.at[part] if fresh else dst, dst, qs.at[f, s], qr.at[f, s], peer)

    for f in range(4):
        dq_copy(f, 0, True).start()
    mine = pltpu.make_async_copy(dq, all_dq.at[e], own.at[0])
    mine.start()

    def dq_step(s):
        for f in range(4):
            dq_copy(f, s - 1).wait_recv()

            @pl.when(s < n - 1)
            def _():
                dq_copy(f, s).start()

    def kv_copy(k, s):
        return push(kvs.at[k, s], kvr.at[k, s], ks.at[k, s], kr.at[k, s], left if k else right)

    def kv_step(s, begin=False):
        for k in range(2):
            ahead = s + 1 if k else n - 1 - s
            block = ring_index((pos + ahead) % n, n)
            value = jnp.dot(xt[block], dkv[k], preferred_element_type=F32)
            if not begin:
                kv_copy(k, s - 1).wait_recv()
                value = value + kvr[k, s - 1].astype(F32)

            @pl.when(s < n - 1)
            def _():
                kvs[k, s] = value.astype(BF)
                kv_copy(k, s).start()

            @pl.when(s == n - 1)
            def _():
                gkv[k] = value

    def share(src, dst, j):
        place = dst.at[:, columns(w, cols)]
        local = pltpu.make_async_copy(src, place, own.at[1 + j])
        over = push(src, place, xs.at[1 + j], xr.at[1 + j], {"ws": cross})
        beside = push(src, place, ts.at[j, 0], tr.at[j, 0], {"ws": core})
        for copy in (local, over, beside):
            copy.start()
        return local, over, beside

    def hand_on(dst, j, over):
        over.wait_recv()
        block = dst.at[:, columns(cross, cols)]
        copy = push(block, block, ts.at[j, 1], tr.at[j, 1], {"ws": core})
        copy.start()
        return copy

    kv_step(0, True)
    spread = Dispatch(n, (0,), (hm,), (ha,), *dsems)
    spread.start()

    def tile(t):
        for copy in load(t):
            copy.wait()

        @pl.loop(0, experts)
        def _(i):
            part = lax.dot_general(dq[i], wt[t % 2, i], over_last, preferred_element_type=F32)
            rows[pl.ds(pl.multiple_of(i * cap, cap), cap)] = part.astype(BF)

        total = lax.dot_general(sel[...], rows[...], first, preferred_element_type=F32)
        for k in range(2):
            total += lax.dot_general(dkv[k], kwt[t % 2, k], over_last, preferred_element_type=F32)
        if t < 2:
            for copy in load(t + 2):
                copy.start()
        return total

    coring = []
    for j in range(2):
        pt[j] = tile(j).astype(BF)
        copy = push(pt.at[j], rc.at[j], cs.at[j], cr.at[j], {"ws": core})
        copy.start()
        coring.append(copy)
    kv_step(1)
    dq_step(1)
    total = tile(2)
    coring[0].wait_recv()
    sx[...] = (total + rc[0].astype(F32)).astype(BF)
    crossing = push(sx, rx, xs.at[0], xr.at[0], {"ws": cross})
    crossing.start()
    total = tile(3)
    coring[1].wait_recv()
    near[...] = total + rc[1].astype(F32)
    kv_step(2)
    dq_step(2)
    loads = []
    for i in range(5):
        copy = pltpu.make_async_copy(grads_in[i], held[i], gl.at[i])
        copy.start()
        loads.append(copy)
    for copy in terms:
        copy.wait()
    line = dg[...] + dgr[0] + dgr[1] + dgr[2]
    picks = (gates.shape[0], experts * cap)
    owner = lax.broadcasted_iota(jnp.int32, picks, 1) // cap
    line = jnp.where(
        lax.broadcasted_iota(jnp.int32, picks, 0) == owner, jnp.broadcast_to(line[:1], picks), 0.0
    )
    dgate = None
    for _ in range(3):
        high = line.astype(BF)
        line = line - high.astype(F32)
        part = jnp.dot(high, sel[...], preferred_element_type=F32)
        dgate = part if dgate is None else dgate + part
    g = gates[...]
    d_logits = (g * (dgate - jnp.sum(g * dgate, axis=0, keepdims=True))).astype(BF)
    ga = jnp.dot(d_logits, xq[...], preferred_element_type=F32)[:experts]
    extra = lax.dot_general(d_logits, router[...], first, preferred_element_type=F32)
    crossing.wait_recv()
    d_xn = near[...] + rx[...].astype(F32) + extra
    u = unit[...]
    row = lax.broadcasted_iota(jnp.int32, gn2.shape, 0)
    vs[:8] = jnp.where(row == 0, jnp.sum(d_xn * u, axis=0, keepdims=True), gn2[...])
    vs[8 : 8 + experts] = ga
    vs[8 + experts :] = gm[...]
    weighted = d_xn * gain[...]
    near[...] = weighted
    across = jnp.sum(weighted * u, axis=1, keepdims=True)
    stat[...] = jnp.broadcast_to(across, (tokens, 128)).T[:8]
    sums = []
    for j, peer in enumerate(mates):
        copy = push(stat, stats.at[j], ss.at[j], sr.at[j], peer)
        copy.start()
        sums.append(copy)
    gains = []
    for k in range(1, n):
        copy = push(vs, vr.at[k - 1], vps.at[k], vpr.at[k], {"ep": (e + k) % n})
        copy.start()
        gains.append(copy)
    for copy in sums:
        copy.wait_recv()
    mean = (stat[...] + stats[0] + stats[1] + stats[2]) / (4 * cols)
    mean = jnp.broadcast_to(mean[:1], (128, tokens)).T[:, :1]
    gt[...] = (dh[...] + inv[...] * (near[...] - u * mean)).astype(BF)
    gt_copies = share(gt, gt_all, 1)
    lo_copies = share(lo, lo_all, 0)
    kv_step(3)
    dq_step(3)
    spread.hand_on()
    for copy in loads:
        copy.wait()

    size = grads_out[0].shape[0] // 8
    rows_in, dy_in, dgate_in, dup_in, down_in = held

    def out_copy(i, j):
        dst = grads_out[j].at[pl.ds(pl.multiple_of(i * size, size), size)]
        return pltpu.make_async_copy(stage.at[j], dst, go.at[j])

    @pl.loop(4, n)
    def _(s):
        kv_step(s)
        dq_step(s)

        @pl.loop(0, 2)
        def _(h):
            i = (s - 4) * 2 + h
            for j, (a, b) in enumerate(((rows_in, dgate_in), (rows_in, dup_in), (dy_in, down_in))):
                grad = lax.dot_general(
                    a[:, columns(i, size)], b[...], first, preferred_element_type=F32
                )

                @pl.when(i > 0)
                def _():
                    out_copy(i - 1, j).wait()

                stage[j] = grad.astype(BF)
                out_copy(i, j).start()

    gt_core = hand_on(gt_all, 1, gt_copies[1])
    lo_core = hand_on(lo_all, 0, lo_copies[1])
    spread.onward()
    for copy in gains:
        copy.wait_recv()
    vs_total = vs[...]
    for k in range(n - 1):
        vs_total += vr[k]
    for copy in gains:
        copy.wait_send()
    vs[...] = vs_total
    place = gv_all.at[:, columns(w, cols)]
    gv_copies = [pltpu.make_async_copy(vs, place, own.at[3])]
    for j, peer in enumerate(mates):
        gv_copies.append(push(vs, place, vws.at[j], vwr.at[j], peer))
    for copy in gv_copies:
        copy.start()
    for j in range(3):
        out_copy(7, j).wait()
    mine.wait()
    for copy in gv_copies + [lo_copies[0], lo_copies[2], gt_copies[0], gt_copies[2], lo_core, gt_core]:
        copy.wait()
    for copy in coring + sums + [crossing, lo_copies[1], gt_copies[1]]:
        copy.wait_send()
    for f in range(4):
        dq_copy(f, 0, True).wait_send()

    @pl.loop(1, n - 1)
    def _(s):
        for f in range(4):
            dq_copy(f, s).wait_send()

    @pl.loop(0, n - 1)
    def _(s):
        for k in range(2):
            kv_copy(k, s).wait_send()

    spread.finish()


def last_stage(cid, dq, dkv, xt, sel, wq, wkv, hm, dh, unit, inv, gain, lo, gn2, gm, dg, gates, router, xq, *grads):
    n = xt.shape[0]
    experts, cap, inner = dq.shape
    tokens, cols = dh.shape
    block = xt.shape[1]
    dma = pltpu.SemaphoreType.DMA
    vm, hbm = vmem_spec(), any_spec()
    small = (8 + experts + gm.shape[0], cols)
    width, f = grads[0].shape[1], grads[2].shape[1]
    wide = jax.ShapeDtypeStruct((tokens, 4 * cols), BF)
    return pl.pallas_call(
        functools.partial(last_kernel, n),
        out_shape=[
            jax.ShapeDtypeStruct((n,) + dq.shape, BF),
            jax.ShapeDtypeStruct((2, block, inner), F32),
            dispatched(hm, 0),
            wide,
            wide,
            jax.ShapeDtypeStruct((small[0], 4 * cols), F32),
        ]
        + [jax.ShapeDtypeStruct((width, f), BF)] * 3,
        in_specs=[vm] * 4 + [hbm] * 3 + [vm] * 11 + [hbm] * 5,
        out_specs=[hbm, vm] + [hbm] * 7,
        scratch_shapes=[
            pltpu.VMEM((2, experts, cols, inner), BF),
            pltpu.VMEM((2, 2, cols, inner), BF),
            pltpu.VMEM((experts * cap, cols), BF),
            pltpu.VMEM((2, tokens, cols), BF),
            pltpu.VMEM((2, tokens, cols), BF),
            pltpu.VMEM((tokens, cols), BF),
            pltpu.VMEM((tokens, cols), BF),
            pltpu.VMEM((tokens, cols), F32),
            pltpu.VMEM((2, n - 1, block, inner), BF),
            pltpu.VMEM((2, n - 1, block, inner), BF),
            pltpu.VMEM((8, tokens), F32),
            pltpu.VMEM((3, 8, tokens), F32),
            pltpu.VMEM((tokens, cols), BF),
            pltpu.VMEM(small, F32),
            pltpu.VMEM((n - 1,) + small, F32),
            dma((2, 2)),
            dma((4,)),
            dma((4, n)),
            dma((4, n)),
            dma((2, n)),
            dma((2, n)),
            dma((2,)),
            dma((2,)),
            dma((3,)),
            dma((3,)),
            dma((3,)),
            dma((3,)),
            dma((2, 2)),
            dma((2, 2)),
            dma((n,)),
            dma((n,)),
            dma((3,)),
            dma((3,)),
        ]
        + [pltpu.VMEM(a.shape, a.dtype) for a in grads]
        + [pltpu.VMEM((3, width // 8, f), BF), dma((5,)), dma((3,))]
        + [pltpu.VMEM((3,) + dg.shape, F32), dma((3,)), dma((3,))]
        + dispatch_sems(1, n),
        compiler_params=params(cid),
        name=f"last_{cid}",
    )(dq, dkv, xt, sel, wq, wkv, hm, dh, unit, inv, gain, lo, gn2, gm, dg, gates, router, xq, *grads)


def grad_slots_kernel(n, dest, x, y, o, picked, ys):
    e = pl.program_id(0)
    cap = y.shape[2]
    index = e * cap + lax.broadcasted_iota(jnp.int32, (cap, x.shape[1]), 0)
    for g in range(n):
        hit = (dest[g, 0:1, :] == index) | (dest[g, 1:2, :] == index)
        sel = jnp.where(hit, 1.0, 0.0).astype(BF)
        r = pl.ds(g * cap, cap)
        picked[r] = jnp.dot(sel, x[g], preferred_element_type=F32).astype(BF)
        ys[r] = y[g, 0]
    o[0] = lax.dot_general(
        picked[...], ys[...], (((0,), (0,)), ((), ())), preferred_element_type=F32
    )


def grad_slots(dest, x, y):
    n, tokens, block = x.shape
    experts, cap, cols = y.shape[1:]
    return pl.pallas_call(
        functools.partial(grad_slots_kernel, n),
        grid=(experts,),
        out_shape=jax.ShapeDtypeStruct((experts, block, cols), F32),
        in_specs=[
            pl.BlockSpec(dest.shape, lambda i: (0, 0, 0)),
            pl.BlockSpec(x.shape, lambda i: (0, 0, 0)),
            pl.BlockSpec((n, 1, cap, cols), lambda i: (0, i, 0, 0)),
        ],
        out_specs=pl.BlockSpec((1, block, cols), lambda i: (i, 0, 0)),
        scratch_shapes=[pltpu.VMEM((n * cap, block), BF), pltpu.VMEM((n * cap, cols), BF)],
        compiler_params=pltpu.CompilerParams(vmem_limit_bytes=VMEM_CAP),
        cost_estimate=pl.CostEstimate(
            flops=2 * experts * n * cap * block * (tokens + cols),
            bytes_accessed=2 * (x.size + y.size) + 4 * experts * block * cols,
            transcendentals=0,
        ),
        name="grad_slots",
    )(dest, x, y)


def collect_kernel(n, v, o, got, part, own, ps, pr, ws, wr):
    e, w = lax.axis_index("ep"), lax.axis_index("ws")
    cols = v.shape[1]
    peers = [{"ep": (e + k) % n} for k in range(1, n)]
    mates = [{"ws": (w + k) % 4} for k in range(1, 4)]
    meet(peers + mates)
    first = []
    for k in range(1, n):
        copy = push(v, got.at[k - 1], ps.at[k], pr.at[k], peers[k - 1])
        copy.start()
        first.append(copy)
    total = v[...]
    for k in range(1, n):
        first[k - 1].wait_recv()
        total += got[k - 1]
    part[...] = total
    mine = o.at[:, columns(w, cols)]
    local = pltpu.make_async_copy(part, mine, own)
    local.start()
    second = []
    for k in range(3):
        copy = push(part, mine, ws.at[k], wr.at[k], mates[k])
        copy.start()
        second.append(copy)
    local.wait()
    for copy in second:
        copy.wait()
    for copy in first:
        copy.wait_send()


def collect(v, cid):
    n = lax.axis_size("ep")
    rows, cols = v.shape
    dma = pltpu.SemaphoreType.DMA
    return pl.pallas_call(
        functools.partial(collect_kernel, n),
        out_shape=jax.ShapeDtypeStruct((rows, 4 * cols), F32),
        in_specs=[vmem_spec()],
        out_specs=vmem_spec(),
        scratch_shapes=[
            pltpu.VMEM((n - 1, rows, cols), F32),
            pltpu.VMEM((rows, cols), F32),
            dma,
            dma((n,)),
            dma((n,)),
            dma((3,)),
            dma((3,)),
        ],
        compiler_params=params(cid),
        name=f"collect_{cid}",
    )(v)


def ring_kernel(n, m, splits, axes, *refs):
    p = len(axes)
    xs, qs, refs = refs[:m], refs[m : m + p], refs[m + p :]
    os, qos, refs = refs[:m], refs[m : m + p], refs[m + p :]
    own, send, recv, *sems = refs
    pos, me = ring_pos(n), lax.axis_index("ep")
    right = {"ep": ring_index((pos + 1) % n, n)}
    left = {"ep": ring_index((pos + n - 1) % n, n)}
    _, _, _, core, cross = ws_places()
    meet([{"ep": (me + k) % n} for k in range(1, n)] + [{"ws": core}, {"ws": cross}])
    flows = []
    for i in range(m):
        part = xs[i].shape[0] // (2 * splits[i])
        for k in range(splits[i]):
            flows.append((i, k * part, part, right, -1))
            flows.append((i, (splits[i] + k) * part, part, left, 1))

    def window(i, first, part, owner):
        size = xs[i].shape[1]
        return os[i].at[pl.ds(first, part), pl.ds(pl.multiple_of(owner * size, size), size)]

    def start(f, s):
        i, first, part, peer, sign = flows[f]
        owner = ring_index((pos + n + sign * s) % n, n)
        dst = window(i, first, part, owner)
        src = xs[i].at[pl.ds(first, part)] if s == 0 else dst
        copy = push(src, dst, send.at[f, s], recv.at[f, s], peer)
        copy.start()
        return copy

    live = [start(f, 0) for f in range(len(flows))]
    work = Dispatch(n, axes, qs, qos, *sems)
    work.start()
    locals_ = []
    for i in range(m):
        copy = pltpu.make_async_copy(xs[i], window(i, 0, xs[i].shape[0], me), own.at[i])
        copy.start()
        locals_.append(copy)
    done = []
    for s in range(1, n):
        for f in range(len(flows)):
            live[f].wait_recv()
            done.append(live[f])
            if s < n - 1:
                live[f] = start(f, s)
        if s == 1:
            work.run()
    work.finish()
    for copy in locals_:
        copy.wait()
    for copy in done:
        copy.wait_send()


def ring_kernel_gather(cid, splits, xs, payloads):
    n, m = lax.axis_size("ep"), len(xs)
    dma = pltpu.SemaphoreType.DMA
    flows = 2 * sum(splits)
    out = pl.pallas_call(
        functools.partial(ring_kernel, n, m, splits, [axis for _, axis in payloads]),
        out_shape=[jax.ShapeDtypeStruct((x.shape[0], n * x.shape[1], x.shape[2]), x.dtype) for x in xs]
        + [dispatched(*payload) for payload in payloads],
        in_specs=[any_spec()] * (m + len(payloads)),
        out_specs=[any_spec()] * (m + len(payloads)),
        scratch_shapes=[dma((m,)), dma((flows, n)), dma((flows, n))] + dispatch_sems(len(payloads), n),
        compiler_params=params(cid),
        name=f"ring_{cid}",
    )(*xs, *[q for q, _ in payloads])
    return out[:m], out[m:]


def project_kernel(experts, parts, extra, sel, y, *rest):
    weights, rest = rest[:parts], rest[parts:]
    if extra:
        kv, kv_weight, o, rows = rest
    else:
        o, rows = rest
    each = experts // parts
    cap = y.shape[1]
    over_last = (((1,), (1,)), ((), ()))
    for i in range(experts):
        weight = weights[i // each][i % each]
        part = lax.dot_general(y[i], weight, over_last, preferred_element_type=F32)
        rows[pl.ds(i * cap, cap)] = part.astype(BF)
    total = lax.dot_general(sel[...], rows[...], (((0,), (0,)), ((), ())), preferred_element_type=F32)
    if extra:
        for i in range(2):
            total += lax.dot_general(kv[i], kv_weight[i], over_last, preferred_element_type=F32)
    o[...] = total.astype(BF)


def project_back(sel, y, weight, kv=None, kv_weight=None, tile=512):
    experts, cap, inner = y.shape
    width, tokens = weight[0].shape[1], sel.shape[1]
    whole = lambda a: pl.BlockSpec(a.shape, lambda i: (0,) * a.ndim)
    tiled = lambda a: pl.BlockSpec((a.shape[0], tile, a.shape[2]), lambda i: (0, i, 0))
    args, specs = [sel, y, *weight], [whole(sel), whole(y), *map(tiled, weight)]
    if kv is not None:
        args += [kv, kv_weight]
        specs += [whole(kv), tiled(kv_weight)]
    flops = 2 * experts * cap * inner * width + 2 * tokens * experts * cap * width
    return pl.pallas_call(
        functools.partial(project_kernel, experts, len(weight), kv is not None),
        grid=(width // tile,),
        out_shape=jax.ShapeDtypeStruct((tokens, width), BF),
        in_specs=specs,
        out_specs=pl.BlockSpec((tokens, tile), lambda i: (0, i)),
        scratch_shapes=[pltpu.VMEM((experts * cap, tile), BF)],
        compiler_params=pltpu.CompilerParams(vmem_limit_bytes=VMEM_CAP),
        cost_estimate=pl.CostEstimate(
            flops=flops, bytes_accessed=2 * (sum(a.size for a in weight) + sel.size + y.size), transcendentals=0
        ),
        name="project_back",
    )(*args)


def beside(n, axes, qs, os, sems):
    step, last = pl.program_id(0), pl.num_programs(0) - 1

    @pl.when(step == 0)
    def _():
        meet(dispatch_peers(n))
        Dispatch(n, axes, qs, os, *sems).start()

    @pl.when(step == last)
    def _():
        Dispatch(n, axes, qs, os, *sems).hand_on()

    def finish():
        @pl.when(step == last)
        def _():
            work = Dispatch(n, axes, qs, os, *sems)
            work.onward()
            work.finish()

    return finish


def expert_kernel(owners, n, axes, rows, other, dy_down, router, wg, wu, *refs):
    m = len(axes)
    qs, refs = refs[:m], refs[m:]
    d_gate, d_up, act_o, down_o, part, dg = refs[:6]
    finish = beside(n, axes, qs, refs[6 : 6 + m], refs[6 + m :]) if m else None
    expert = lax.axis_index("ep") // owners
    tile, cap = rows.shape[0], dg.shape[2]
    x = rows[...]
    logits = jnp.dot(x, router[...], preferred_element_type=F32)
    index = lax.broadcasted_iota(jnp.int32, logits.shape, 1)
    own = jnp.sum(jnp.where(index == expert, logits, 0.0), axis=1, keepdims=True)
    oth = jnp.sum(jnp.where(index == other[...], logits, 0.0), axis=1, keepdims=True)
    top = jnp.maximum(own, oth)
    own, oth = jnp.exp(own - top), jnp.exp(oth - top)
    gate = own / (own + oth)
    gate_pre = jnp.dot(x, wg[...], preferred_element_type=F32)
    up_pre = jnp.dot(x, wu[...], preferred_element_type=F32)
    sig = 1.0 / (1.0 + jnp.exp(-gate_pre))
    silu = gate_pre * sig
    act = silu * up_pre
    dy = dy_down[...]
    act_o[...] = act.astype(BF)
    down_o[...] = (act * gate).astype(BF)
    dgate = jnp.sum(act * dy, axis=1, keepdims=True)
    d_act = dy * gate
    dgb = (d_act * up_pre * sig * (1.0 + gate_pre * (1.0 - sig))).astype(BF)
    dub = (d_act * silu).astype(BF)
    d_gate[...] = dgb
    d_up[...] = dub
    over_last = (((1,), (1,)), ((), ()))
    total = lax.dot_general(dgb, wg[...], over_last, preferred_element_type=F32)
    total += lax.dot_general(dub, wu[...], over_last, preferred_element_type=F32)
    part[...] = total.astype(BF)
    lane = lax.broadcasted_iota(jnp.int32, (tile, 128), 1)
    both = jnp.where(lane < 4, dgate, 0.25 * gate).T[:8]
    for j in range(tile // cap):
        dg[j] = both[:, j * cap : (j + 1) * cap]
    if m:
        finish()


def expert_pass(rows, other, dy_down, router, wg, wu, owners, cap, payloads, cid, tile=256):
    n, m = lax.axis_size("ep"), len(payloads)
    count, width = rows.shape
    f = wg.shape[1]
    by_row = lambda c: pl.BlockSpec((tile, c), lambda i: (i, 0))
    once = lambda a: pl.BlockSpec(a.shape, lambda i: (0, 0), pipeline_mode=pl.Buffered(1))
    wide = jax.ShapeDtypeStruct((count, f), BF)
    return pl.pallas_call(
        functools.partial(expert_kernel, owners, n, [axis for _, axis in payloads]),
        grid=(count // tile,),
        out_shape=(wide,) * 4
        + (
            jax.ShapeDtypeStruct((count, width), BF),
            jax.ShapeDtypeStruct((count // cap, 8, cap), F32),
            *[dispatched(*payload) for payload in payloads],
        ),
        in_specs=[by_row(width), by_row(1), by_row(f), once(router), once(wg), once(wu)]
        + [any_spec()] * m,
        out_specs=(by_row(f),) * 4
        + (by_row(width), pl.BlockSpec((tile // cap, 8, cap), lambda i: (i, 0, 0)))
        + (any_spec(),) * m,
        scratch_shapes=dispatch_sems(m, n) if m else [],
        compiler_params=params(cid) if m else pltpu.CompilerParams(vmem_limit_bytes=VMEM_CAP),
        cost_estimate=pl.CostEstimate(
            flops=8 * count * width * f, bytes_accessed=4 * width * f + 12 * count * f, transcendentals=count * f
        ),
        name="expert_pass",
    )(rows, other, dy_down, router, wg, wu, *[q for q, _ in payloads])


def turn(v, cos, sin, sign):
    return v * cos + sign * (pltpu.roll(v, HD // 2, 1) * sin)


def masked_scores(q, k, token):
    raw = lax.dot_general(q, k, (((1,), (1,)), ((), ())), preferred_element_type=F32)
    key = lax.broadcasted_iota(jnp.int32, (1, k.shape[0]), 1)
    _, key_segment = place_of(key)
    _, segment = place_of(token)
    allowed = (key <= token) & ((key_segment == 0) | (key_segment == segment))
    return jnp.where(allowed, raw * (1.0 / math.sqrt(HD)), MASKED)


ROWS = 256


def attend_kernel(q_pre, k_pre, v_pre, q_cos, q_sin, cos, sin, token, gate, q, k, v, o, gated, lse):
    k[...] = turn(k_pre[...], cos[...], sin[...], 1).astype(BF)
    v[...] = v_pre[...].astype(BF)
    for i in range(q.shape[0] // ROWS):
        r = pl.ds(i * ROWS, ROWS)
        q[r] = turn(q_pre[r], q_cos[r], q_sin[r], 1).astype(BF)
        scores = masked_scores(q[r], k[...], token[r])
        peak = jnp.max(scores, axis=1, keepdims=True)
        exponent = jnp.exp(scores - peak)
        total = jnp.sum(exponent, axis=1, keepdims=True)
        lse[0, r] = peak + jnp.log(total)
        probs = (exponent / total).astype(BF)
        out = jnp.dot(probs, v[...], preferred_element_type=F32)
        o[r] = out.astype(BF)
        gated[r] = (out * gate[r]).astype(BF)


def attend_specs(slots, tokens):
    head = lambda rows: pl.BlockSpec((rows, HD), lambda h: (0, h))
    table = lambda rows: pl.BlockSpec((rows, HD), lambda h: (0, 0))
    column = pl.BlockSpec((slots, 1), lambda h: (0, 0))
    line = pl.BlockSpec((1, slots, 1), lambda h: (h, 0, 0))
    return head, table, column, line


def attend(q_pre, k_pre, v_pre, q_cos, q_sin, cos, sin, token, gate):
    slots, inner = q_pre.shape
    tokens = k_pre.shape[0]
    head, table, column, line = attend_specs(slots, tokens)
    wide, narrow = jax.ShapeDtypeStruct((slots, inner), BF), jax.ShapeDtypeStruct((tokens, inner), BF)
    return pl.pallas_call(
        attend_kernel,
        grid=(inner // HD,),
        out_shape=(wide, narrow, narrow, wide, wide, jax.ShapeDtypeStruct((inner // HD, slots, 1), F32)),
        in_specs=[head(slots), head(tokens), head(tokens), table(slots), table(slots), table(tokens), table(tokens)]
        + [column] * 2,
        out_specs=(head(slots), head(tokens), head(tokens), head(slots), head(slots), line),
        compiler_params=pltpu.CompilerParams(vmem_limit_bytes=VMEM_CAP),
        cost_estimate=pl.CostEstimate(
            flops=4 * slots * tokens * inner, bytes_accessed=16 * slots * inner, transcendentals=slots * tokens
        ),
        name="attend",
    )(q_pre, k_pre, v_pre, q_cos, q_sin, cos, sin, token, gate)


def attend_back_kernel(n, axes, raw, o, gate, q, k, v, lse, q_cos, q_sin, cos, sin, token, *refs):
    m = len(axes)
    qs, refs = refs[:m], refs[m:]
    dq, dkv, dgate = refs[:3]
    finish = beside(n, axes, qs, refs[3 : 3 + m], refs[3 + m :]) if m else None
    scale = 1.0 / math.sqrt(HD)
    first = (((0,), (0,)), ((), ()))
    over_last = (((1,), (1,)), ((), ()))
    dk, dv = None, None
    for i in range(q.shape[0] // ROWS):
        r = pl.ds(i * ROWS, ROWS)
        across = jnp.sum(raw[r] * o[r].astype(F32), axis=1, keepdims=True)
        line = jnp.broadcast_to(across, (ROWS, 128)).T[:8]
        lanes = pl.ds(i * ROWS, ROWS)

        @pl.when(pl.program_id(0) == 0)
        def _():
            dgate[:, lanes] = line

        @pl.when(pl.program_id(0) > 0)
        def _():
            dgate[:, lanes] += line

        d_o = (raw[r] * gate[r]).astype(BF)
        probs = jnp.exp(masked_scores(q[r], k[...], token[r]) - lse[0, r])
        d_probs = lax.dot_general(d_o, v[...], over_last, preferred_element_type=F32)
        inside = jnp.sum(probs * d_probs, axis=1, keepdims=True)
        d_scores = (probs * (d_probs - inside)).astype(BF)
        part = jnp.dot(d_scores, k[...], preferred_element_type=F32) * scale
        dq[r] = turn(part, q_cos[r], q_sin[r], -1).astype(BF)
        dk_part = lax.dot_general(d_scores, q[r], first, preferred_element_type=F32)
        dv_part = lax.dot_general(probs.astype(BF), d_o, first, preferred_element_type=F32)
        dk = dk_part if dk is None else dk + dk_part
        dv = dv_part if dv is None else dv + dv_part
    dkv[0] = turn(dk * scale, cos[...], sin[...], -1).astype(BF)
    dkv[1] = dv.astype(BF)
    if m:
        finish()


def attend_back(raw, o, gate, q, k, v, lse, q_cos, q_sin, cos, sin, token, payloads, cid):
    n, m = lax.axis_size("ep"), len(payloads)
    slots, inner = q.shape
    tokens = k.shape[0]
    head, table, column, line = attend_specs(slots, tokens)
    return pl.pallas_call(
        functools.partial(attend_back_kernel, n, [axis for _, axis in payloads]),
        grid=(inner // HD,),
        out_shape=(
            jax.ShapeDtypeStruct((slots, inner), BF),
            jax.ShapeDtypeStruct((2, tokens, inner), BF),
            jax.ShapeDtypeStruct((8, slots), F32),
            *[dispatched(*payload) for payload in payloads],
        ),
        in_specs=[head(slots), head(slots), column, head(slots), head(tokens), head(tokens), line]
        + [table(slots), table(slots), table(tokens), table(tokens), column]
        + [any_spec()] * m,
        out_specs=(
            head(slots),
            pl.BlockSpec((2, tokens, HD), lambda h: (0, 0, h)),
            pl.BlockSpec((8, slots), lambda h: (0, 0)),
        )
        + (any_spec(),) * m,
        scratch_shapes=dispatch_sems(m, n) if m else [],
        compiler_params=params(cid) if m else pltpu.CompilerParams(vmem_limit_bytes=VMEM_CAP),
        cost_estimate=pl.CostEstimate(
            flops=10 * slots * tokens * inner, bytes_accessed=16 * slots * inner, transcendentals=slots * tokens
        ),
        name="attend_back",
    )(raw, o, gate, q, k, v, lse, q_cos, q_sin, cos, sin, token, *[v for v, _ in payloads])


def arrivals(rings, n):
    args, specs = [], []
    for p, got in enumerate([got for ring in rings for got in ring.got]):
        each = got[0].shape[0]
        for v in got:
            args.append(v)
            specs.append(
                pl.BlockSpec(
                    (1,) + v.shape[1:],
                    lambda i, p=p, each=each: (jnp.clip(i - p * each, 0, each - 1), 0, 0),
                )
            )
    return args, specs


def out_kernel(n, each, sel, y, *refs):
    blocks, (o, rows) = refs[:-2], refs[-2:]
    e, pos = pl.program_id(0), ring_pos(n)
    cap = y.shape[1]
    size = blocks[0].shape[1]
    here = pl.ds(pl.multiple_of(e * cap, cap), cap)

    def project(p):
        for s in range(n):
            g = ring_index((pos + n + (2 * (p % 2) - 1) * s) % n, n)
            part = lax.dot_general(
                y[0], blocks[p * n + s][0], (((1,), (1,)), ((), ())), preferred_element_type=F32
            )
            rows[here, columns(g, size)] = part.astype(BF)

    for p in range(len(blocks) // n):
        pl.when(e // each == p)(functools.partial(project, p))

    @pl.when(e == pl.num_programs(0) - 1)
    def _():
        tile = o.shape[1] // 4
        for t in range(4):
            c = pl.ds(t * tile, tile)
            o[:, c] = lax.dot_general(
                sel[...], rows[:, c], (((0,), (0,)), ((), ())), preferred_element_type=F32
            ).astype(BF)


def out_project(sel, y, rings, width):
    n = lax.axis_size("ep")
    experts, cap, inner = y.shape
    tokens = sel.shape[1]
    args, specs = arrivals(rings, n)
    return pl.pallas_call(
        functools.partial(out_kernel, n, args[0].shape[0]),
        grid=(experts,),
        out_shape=jax.ShapeDtypeStruct((tokens, width), BF),
        in_specs=[
            pl.BlockSpec(sel.shape, lambda i: (0, 0)),
            pl.BlockSpec((1, cap, inner), lambda i: (i, 0, 0)),
        ]
        + specs,
        out_specs=pl.BlockSpec((tokens, width), lambda i: (0, 0)),
        scratch_shapes=[pltpu.VMEM((experts * cap, width), BF)],
        compiler_params=pltpu.CompilerParams(vmem_limit_bytes=VMEM_CAP),
        cost_estimate=pl.CostEstimate(
            flops=2 * experts * cap * width * (inner + tokens),
            bytes_accessed=2 * experts * inner * width,
            transcendentals=0,
        ),
        name="out_project",
    )(sel, y, *args)


def back_kernel(n, each, sel, d, *refs):
    blocks, (o, rows) = refs[:-2], refs[-2:]
    e, pos = pl.program_id(0), ring_pos(n)
    size = blocks[0].shape[1]
    rows[...] = jnp.dot(sel[...], d[...], preferred_element_type=F32).astype(BF)

    def project(p):
        total = None
        for s in range(n):
            g = ring_index((pos + n + (2 * (p % 2) - 1) * s) % n, n)
            part = jnp.dot(
                rows[:, columns(g, size)], blocks[p * n + s][0], preferred_element_type=F32
            )
            total = part if total is None else total + part
        o[0] = total

    for p in range(len(blocks) // n):
        pl.when(e // each == p)(functools.partial(project, p))


def out_back(sel, d, rings, experts):
    n = lax.axis_size("ep")
    tokens, width = d.shape
    cap = sel.shape[0] // experts
    args, specs = arrivals(rings, n)
    inner = args[0].shape[2]
    return pl.pallas_call(
        functools.partial(back_kernel, n, args[0].shape[0]),
        grid=(experts,),
        out_shape=jax.ShapeDtypeStruct((experts, cap, inner), F32),
        in_specs=[
            pl.BlockSpec((cap, tokens), lambda i: (i, 0)),
            pl.BlockSpec((tokens, width), lambda i: (0, 0)),
        ]
        + specs,
        out_specs=pl.BlockSpec((1, cap, inner), lambda i: (i, 0, 0)),
        scratch_shapes=[pltpu.VMEM((cap, width), BF)],
        compiler_params=pltpu.CompilerParams(vmem_limit_bytes=VMEM_CAP),
        cost_estimate=pl.CostEstimate(
            flops=2 * experts * cap * width * (inner + tokens),
            bytes_accessed=2 * experts * inner * width,
            transcendentals=0,
        ),
        name="out_back",
    )(sel, d, *args)


def grad_rows_kernel(n, half, dest, x, *refs):
    low, high = refs[:n], refs[n : 2 * n]
    o, picked, y = refs[2 * n :]
    e = pl.program_id(0)
    pos = ring_pos(n)
    cap = low[0].shape[1]
    index = e * cap + lax.broadcasted_iota(jnp.int32, (cap, x.shape[1]), 0)

    def gather(sources, sign):
        for s in range(n):
            g = ring_index((pos + n + sign * s) % n, n)
            hit = (dest[g, 0:1, :] == index) | (dest[g, 1:2, :] == index)
            sel = jnp.where(hit, 1.0, 0.0).astype(BF)
            r = pl.ds(s * cap, cap)
            picked[r] = jnp.dot(sel, x[g], preferred_element_type=F32).astype(BF)
            y[r] = sources[s][0]

    pl.when(e < half)(lambda: gather(low, -1))
    pl.when(e >= half)(lambda: gather(high, 1))
    o[0] = lax.dot_general(
        picked[...], y[...], (((0,), (0,)), ((), ())), preferred_element_type=F32
    )


def grad_rows(dest, x, got):
    n, tokens, block = x.shape
    half, cap, cols = got[0][0].shape
    experts = 2 * half
    low = pl.BlockSpec((1, cap, cols), lambda i: (jnp.minimum(i, half - 1), 0, 0))
    high = pl.BlockSpec((1, cap, cols), lambda i: (jnp.maximum(i - half, 0), 0, 0))
    return pl.pallas_call(
        functools.partial(grad_rows_kernel, n, half),
        grid=(experts,),
        out_shape=jax.ShapeDtypeStruct((experts, block, cols), F32),
        in_specs=[
            pl.BlockSpec(dest.shape, lambda i: (0, 0, 0)),
            pl.BlockSpec(x.shape, lambda i: (0, 0, 0)),
        ]
        + [low] * n
        + [high] * n,
        out_specs=pl.BlockSpec((1, block, cols), lambda i: (i, 0, 0)),
        scratch_shapes=[pltpu.VMEM((n * cap, block), BF), pltpu.VMEM((n * cap, cols), BF)],
        compiler_params=pltpu.CompilerParams(vmem_limit_bytes=VMEM_CAP),
        cost_estimate=pl.CostEstimate(
            flops=2 * experts * n * cap * block * (tokens + cols),
            bytes_accessed=2 * (x.size + experts * n * cap * cols) + 4 * experts * block * cols,
            transcendentals=0,
        ),
        name="grad_rows",
    )(dest, x, *got[0], *got[1])


def slot_dest(routes, order, experts, capacity):
    pairs = routes.shape[0] * 2
    expert = routes.reshape(pairs)
    index = jnp.arange(pairs, dtype=jnp.int32)
    place = jnp.sum(
        jnp.where(order.reshape(1, pairs) == index[:, None], index[None, :], 0), axis=1
    )
    ahead = (place[None, :] < place[:, None]) & (expert[None, :] == expert[:, None])
    slot = jnp.sum(ahead.astype(jnp.int32), axis=1)
    dest = jnp.where(slot < capacity, expert * capacity + slot, -1)
    return dest.reshape(-1, 2)


def slot_onehot(dest, slots):
    index = jnp.arange(slots, dtype=jnp.int32)[:, None]
    return ((dest[None, :, 0] == index) | (dest[None, :, 1] == index)).astype(BF)


def slot_values(dest, values, slots):
    index = jnp.arange(slots, dtype=jnp.int32)[:, None]
    zero = jnp.zeros((), values.dtype)
    return jnp.sum(
        jnp.where(dest[None, :, 0] == index, values[None, :, 0], zero)
        + jnp.where(dest[None, :, 1] == index, values[None, :, 1], zero),
        axis=1,
    )


def router_gates(logits, hot):
    top = jnp.max(jnp.where(hot, logits, MASKED), axis=1, keepdims=True)
    e = jnp.where(hot, jnp.exp(logits - top), 0.0)
    return e / jnp.sum(e, axis=1, keepdims=True)


def chosen(gates, routes):
    index = jnp.arange(gates.shape[1], dtype=jnp.int32)
    return jnp.sum(jnp.where(routes[:, :, None] == index, gates[:, None, :], 0.0), axis=2)


def angles(positions):
    half = HD // 2
    freq = ROPE_BASE ** (-(jnp.arange(half, dtype=F32) * 2.0) / HD)
    a = positions.astype(F32)[:, None] * freq[None, :]
    return jnp.tile(jnp.cos(a), (1, 2)), jnp.concatenate([-jnp.sin(a), jnp.sin(a)], axis=1)


def place_of(index):
    tail = jnp.maximum(index - PROMPT, 0)
    position = jnp.where(index < PROMPT, index, PROMPT + tail % CLEN)
    segment = jnp.where(index < PROMPT, 0, 1 + tail // CLEN)
    return position, segment


def per_device(
    tokens,
    grad_out,
    norm1_gain,
    attn_router,
    attn_routes,
    attn_order,
    w_query,
    w_kv,
    w_attn_out,
    norm2_gain,
    mlp_router,
    mlp_routes,
    mlp_order,
    w_gate,
    w_up,
    w_down,
):
    glen, width = tokens.shape
    n = lax.axis_size("ep")
    nw = lax.axis_size("ws")
    ep, ws = lax.axis_index("ep"), lax.axis_index("ws")
    ea, em = attn_router.shape[1], mlp_router.shape[1]
    acap, mcap = 2 * glen // ea, 2 * glen // em
    owners = n // em
    slots, mslots = ea * acap, em * mcap
    heads = w_query.shape[2] // HD
    block = w_query.shape[1]
    quarter = width // nw
    cut = lambda v: lax.dynamic_slice_in_dim(v, ws * quarter, quarter, v.ndim - 1)
    cut0 = lambda v: lax.dynamic_slice_in_dim(v, ws * quarter, quarter, 0)

    on_ring = n <= RING_MAX
    ring_a = [GatherRing(w_attn_out[: ea // 2])] if on_ring else []
    hop(ring_a)

    a_dest = slot_dest(attn_routes, attn_order, ea, acap)
    m_dest = slot_dest(mlp_routes, mlp_order, em, mcap)
    lock(ring_a)
    hop(ring_a)
    a_dest, m_dest = lock(ring_a, a_dest, m_dest)
    hop(ring_a)
    a_sel = slot_onehot(a_dest, slots)
    m_sel = slot_onehot(m_dest, mslots)
    a_hot = jnp.any(attn_routes[:, :, None] == jnp.arange(ea, dtype=jnp.int32), axis=1)
    m_hot = jnp.any(mlp_routes[:, :, None] == jnp.arange(em, dtype=jnp.int32), axis=1)
    token_index = jnp.arange(glen, dtype=jnp.int32)
    a_token = slot_values(a_dest, jnp.stack([token_index, token_index], 1), slots)
    other = slot_values(m_dest, mlp_routes[:, ::-1], mslots).reshape(em, mcap)
    x = tokens.astype(F32)
    inv1 = lax.rsqrt(jnp.mean(x * x, axis=1, keepdims=True) + EPS)
    xn = (x * inv1 * norm1_gain).astype(BF)
    a_sel, m_sel, a_token, xn, other = lock(ring_a, a_sel, m_sel, a_token, xn, other)
    hop(ring_a)
    slot_in = mm("st,td->sd", a_sel, xn).astype(BF).reshape(ea, acap, width)
    xn_turned = jnp.transpose(xn.reshape(glen, n, block), (1, 2, 0))
    part_w = glen // nw
    x_mine = lax.dynamic_slice_in_dim(xn, ws * part_w, part_w, 0)
    x_mine = jnp.transpose(x_mine.reshape(part_w, n, block), (1, 0, 2))
    dest_mine = lax.dynamic_slice_in_dim(a_dest.T, ws * part_w, part_w, 1)
    dest_mine = jnp.broadcast_to(jnp.tile(dest_mine, (4, 1))[None], (n, 8, part_w))
    slot_in, xn_turned, x_mine, dest_mine = lock(ring_a, slot_in, xn_turned, x_mine, dest_mine)
    hop(ring_a)
    q_cos, q_sin = angles(place_of(a_token)[0])
    cos, sin = angles(place_of(token_index)[0])
    q_cos, q_sin, cos, sin = lock(ring_a, q_cos, q_sin, cos, sin)
    hop(ring_a)
    a_logits = mm("td,de->te", xn, attn_router)
    a_gate = router_gates(a_logits, a_hot)
    a_slot_gate = slot_values(a_dest, chosen(a_gate, attn_routes), slots)
    dy_q = cut(grad_out)
    dy_slots = mm("st,td->sd", m_sel, dy_q).astype(BF)
    a_column, gate_column = a_token[:, None], a_slot_gate[:, None]
    a_column, gate_column, dy_slots, a_gate = lock(ring_a, a_column, gate_column, dy_slots, a_gate)
    hop(ring_a)
    w_kv, w_query = lock(ring_a, w_kv, w_query)
    dy_send = jnp.repeat(dy_slots.reshape(em, mcap, quarter), owners, axis=0)
    other = jnp.broadcast_to(jnp.repeat(other, owners, axis=0)[:, None], (n, 8, mcap))
    payloads = ((dy_send, 1), (other, 0), (x_mine, 0), (dest_mine, 1))
    if on_ring:
        (full_kv, full_query), (dy_rows, other, x_all, all_dest) = ring_kernel_gather(8, (1, 2), (w_kv, w_query), payloads)
        ring_b = [GatherRing(after(w_attn_out[ea // 2 :], full_query))]
    else:
        gather = lambda v: lax.all_gather(v, "ep", axis=1, tiled=True)
        full_kv, full_query, full_out = gather(w_kv), gather(w_query), gather(w_attn_out)
        dy_rows, other = dispatch(8, *payloads[:2])
        ring_b = []
    dy_rows, other = dy_rows.reshape(n * mcap, width), other[:, 0].reshape(-1)
    hop(ring_b)
    q_pre = mm("ecd,edj->ecj", slot_in, full_query)
    (q_pre,) = lock(ring_b, q_pre)
    hop(ring_b)
    k_pre = mm("td,dj->tj", xn, full_kv[0])
    v_pre = mm("td,dj->tj", xn, full_kv[1])
    k_pre, v_pre = lock(ring_b, k_pre, v_pre)
    hop(ring_b)
    q, k, v, attn_o, gated_o, lse = attend(
        q_pre.reshape(slots, -1), k_pre, v_pre, q_cos, q_sin, cos, sin, a_column, gate_column
    )
    (gated_o,) = lock(ring_b, gated_o)
    hop(ring_b)
    dy_down = mm("rd,df->rf", dy_rows, w_down)
    (dy_down,) = lock(ring_b, dy_down)
    for _ in range(3):
        hop(ring_b)
    gated_o = gated_o.reshape(ea, acap, heads * HD)
    slots_travel = n <= RING_MAX and n * slots <= ea * width
    ring_o = [GatherRing(gated_o)] if slots_travel else []
    hop(ring_o)
    if on_ring:
        branch = out_project(a_sel, gated_o, ring_a + ring_b, width)
    else:
        branch = project_back(a_sel, gated_o, (full_out,))
    (branch,) = lock(ring_o, branch)
    hop(ring_o)
    gain2 = cut0(norm2_gain)[None]
    hidden, inv2, hn, hn_slots = mix(branch, cut(tokens), gain2, m_sel, 0)
    hidden, inv2, hn, hn_slots = lock(ring_o, hidden, inv2, hn, hn_slots)
    x_q = cut(tokens).astype(F32)
    router_q = lax.dynamic_slice_in_dim(mlp_router, ws * quarter, quarter, 0)
    hn_slots = jnp.repeat(hn_slots.reshape(em, mcap, quarter), owners, axis=0)
    rows = dispatch(1, (hn_slots, 1))[0].reshape(n * mcap, width)
    (rows,) = lock(ring_o, rows)

    rows_w = glen // nw

    def mine(v):
        v = lax.dynamic_slice_in_dim(v, ws * rows_w, rows_w, 0)
        return jnp.transpose(v.reshape(rows_w, n, block), (1, 0, 2))

    hop(ring_o)
    d_gate, d_up, act_bf, down_bf, d_part, row_dgate, *spread = expert_pass(
        rows, other[:, None], dy_down, mlp_router, w_gate, w_up, owners, mcap,
        (), 6,
    )
    d_gate, d_up, act_bf, down_bf, d_part, row_dgate = lock(
        ring_o, d_gate, d_up, act_bf, down_bf, d_part, row_dgate
    )
    hop(ring_o)
    d_part = d_part.reshape(n, mcap, width)
    if on_ring:
        d_rows, m_dgate, *part = give_back_part(d_part, row_dgate, act_bf, w_down, 2)
    else:
        d_rows, m_dgate = give_back(d_part, row_dgate, 2)
        part = quarters(mm("rf,df->rd", act_bf, w_down).astype(BF))
        grad_gate = mm("rd,rf->df", rows, d_gate)
        grad_up = mm("rd,rf->df", rows, d_up)
        grad_down = mm("rd,rf->df", dy_rows, down_bf)
    d_rows, m_dgate, *part = lock(ring_o, d_rows, m_dgate, *part)
    hop(ring_o)
    far, near = lax.ppermute(part[0], "ws", CORE), lax.ppermute(part[1], "ws", CORE)
    far = (part[2].astype(F32) + far.astype(F32)).astype(BF)
    m_slot_gate = m_dgate[:, 4].reshape(em, owners, mcap)[:, 0].reshape(mslots)
    m_dgate = jnp.sum(m_dgate[:, 0].reshape(em, owners, mcap), axis=1).reshape(mslots, 1)

    def by_owner(v):
        if owners > 1:
            v = jnp.sum(v.astype(F32).reshape(em, owners, mcap, quarter), axis=1).astype(BF)
        return v.reshape(mslots, quarter)

    d_rows = by_owner(d_rows)
    def per_expert(sel, values, experts):
        terms = sel.reshape(experts, -1, glen).astype(F32) * values.reshape(experts, -1, 1)
        return jnp.sum(terms, axis=1).T

    def router_back(dgate, gates):
        return (gates * (dgate - jnp.sum(gates * dgate, axis=1, keepdims=True))).astype(BF)

    m_gate = per_expert(m_sel, m_slot_gate, em)
    kept = jnp.sum(m_gate, axis=1, keepdims=True)
    m_gate = jnp.where(m_hot & (m_gate == 0.0), jnp.maximum(1.0 - kept, 0.0), m_gate)
    d_m_logits = router_back(per_expert(m_sel, m_dgate, em), m_gate)
    grad_mlp_router = mm("td,te->ed", hn, d_m_logits)
    d_hn = mm("te,de->td", d_m_logits, router_q)
    d_hidden, grad_norm2, d_hid = home(m_sel, d_rows, d_hn, hidden, inv2, gain2, dy_q, 3)
    d_hid, far, near = lock(ring_o, d_hid, far, near)
    hop(ring_o)
    far = lax.ppermute(far, "ws", CROSS)

    if on_ring:
        raw_do = out_back(a_sel, d_hid, ring_a + ring_b, ea).reshape(slots, heads * HD)
    else:
        dh_slots = mm("st,td->sd", a_sel, d_hid).astype(BF).reshape(ea, acap, width)
        raw_do = mm("ecd,edj->ecj", dh_slots, full_out).reshape(slots, heads * HD)
    raw_do, far, near = lock(ring_o, raw_do, far, near)
    hop(ring_o)
    part = (part[3].astype(F32) + near.astype(F32) + far.astype(F32)).astype(BF)
    part = lax.all_to_all(part.reshape(n, mcap, quarter), "ep", 0, 0, tiled=True)
    d_q, d_kv, a_dgate, *spread = attend_back(
        raw_do, attn_o, gate_column, q, k, v, lse, q_cos, q_sin, cos, sin, a_column,
        (), 7,
    )
    d_q = d_q.reshape(ea, acap, heads * HD)
    d_q, d_kv, part = lock(ring_o, d_q, d_kv, part)

    arouter_q = lax.dynamic_slice_in_dim(attn_router, ws * quarter, quarter, 0)
    xn_q = cut(xn)
    unit1 = x_q * inv1
    gain1 = cut0(norm1_gain)[None]
    expert_out = by_owner(part)
    mlp_branch = mm("st,sd->td", m_sel, (expert_out.astype(F32) * m_slot_gate[:, None]).astype(BF))
    layer_out = (hidden + mlp_branch).astype(BF)

    if slots_travel:
        pad = lambda v: jnp.pad(v, ((0, 16 - ea), (0, 0)))
        all_dq, grad_kv, h_all, grad_tokens, layer_out, stats, *grads = last_stage(
            9, d_q, d_kv, xn_turned, a_sel, full_query, full_kv, mine(d_hid), d_hidden, unit1, inv1, gain1, layer_out, grad_norm2, grad_mlp_router, a_dgate, pad(a_gate.T),
            pad(arouter_q.T), xn_q,
            rows, dy_rows, d_gate, d_up, down_bf,
        )
        grad_gate, grad_up, grad_down = [g.astype(F32) for g in grads]
        grad_query = grad_slots(all_dest, x_all, all_dq)
        grad_attn_out = grad_rows(all_dest, h_all, ring_o[0].got)
    else:
        a_dgate = lax.psum(a_dgate[0], "ws")
        d_a_logits = router_back(per_expert(a_sel, a_dgate, ea), a_gate)
        grad_attn_router = mm("td,te->ed", xn_q, d_a_logits)
        d_xn = ws_reduce(project_back(a_sel, d_q, (full_query,), d_kv, full_kv), 4)
        d_xn = d_xn + mm("te,de->td", d_a_logits, arouter_q)
        grad_norm1 = jnp.sum(d_xn * unit1, axis=0, keepdims=True)
        w1 = d_xn * gain1
        mean1 = lax.psum(jnp.sum(w1 * unit1, axis=1, keepdims=True), "ws") / width
        grad_tokens = (d_hidden + inv1 * (w1 - unit1 * mean1)).astype(BF)
        grad_tokens = ws_spread(grad_tokens, 5)
        dh_slots = mm("st,td->sd", a_sel, d_hid).astype(BF).reshape(ea, acap, width)
        scatter = lambda g: lax.psum_scatter(g.astype(BF), "ep", scatter_dimension=1, tiled=True)
        grad_query = scatter(mm("ecd,ecj->edj", slot_in, d_q)).astype(F32)
        grad_attn_out = scatter(mm("ecd,ecj->edj", dh_slots, gated_o)).astype(F32)
        grad_kv = scatter(mm("td,ktj->kdj", xn, d_kv)).astype(F32)
        layer_out = ws_gather(layer_out)
        norms = jnp.where(jnp.arange(8)[:, None] == 0, grad_norm1, grad_norm2)
        stats = collect(jnp.concatenate([norms, grad_attn_router, grad_mlp_router]), 10)
    grad_tokens = grad_tokens.astype(F32)

    grad_norm1, grad_norm2 = stats[0], stats[1]
    grad_attn_router, grad_mlp_router = stats[8 : 8 + ea].T, stats[8 + ea :].T
    return (
        layer_out,
        grad_tokens,
        grad_norm1,
        grad_attn_router,
        grad_query,
        grad_kv,
        grad_attn_out,
        grad_norm2,
        grad_mlp_router,
        grad_gate,
        grad_up,
        grad_down,
    )


def solution(mesh):
    rows, wide = P("ep", None), P(None, ("ep", "ws"))
    attn = P(None, "ep", "ws")
    return jax.shard_map(
        per_device,
        mesh=mesh,
        in_specs=(rows, rows, P(), P(), rows, rows, attn, attn, attn, P(), P(), rows, rows)
        + (wide,) * 3,
        out_specs=(rows, rows, P(), P(), attn, attn, attn, P(), P()) + (wide,) * 3,
        check_vma=False,
    )
```

```python
import functools
import math

import jax
import jax.numpy as jnp
from jax import lax
from jax.experimental import pallas as pl
from jax.experimental.pallas import tpu as pltpu
from jax.sharding import PartitionSpec as P

HD = 128
PROMPT = 256
CLEN = 128
EPS = 1e-06
ROPE_BASE = 10000.0
MASKED = -1e30
BF = jnp.bfloat16
F32 = jnp.float32
RING_MAX = 8


def mm(eq, a, b):
    return jnp.einsum(eq, a, b, preferred_element_type=F32)


def after(value, *deps):
    return lax.optimization_barrier((value,) + deps)[0]


def ring_index(p, n):
    h = p // (n // 2)
    return 2 * p * (1 - h) + h * (2 * (n - 1 - p) + 1)


def ring_pos(n):
    i = lax.axis_index("ep")
    h = i // 2
    return h + (i % 2) * (n - 1 - 2 * h)


def ring_perms(n):
    fw = [(ring_index(p, n), ring_index((p + 1) % n, n)) for p in range(n)]
    return fw, [(b, a) for a, b in fw]


def ring_gather(x, dim):
    n = lax.axis_size("ep")
    half = x.shape[0] // 2
    if n > RING_MAX:
        full = lax.all_gather(x, "ep", axis=dim, tiled=True)
        return (full[:half], full[half:]), (full,)
    fw, bw = ring_perms(n)
    pos = ring_pos(n)
    a, b = x[:half], x[half:]
    shape = list(a.shape)
    size = shape[dim]
    shape[dim] = size * n
    out_a, out_b = jnp.zeros(shape, x.dtype), jnp.zeros(shape, x.dtype)
    me = lax.axis_index("ep")
    out_a = lax.dynamic_update_slice_in_dim(out_a, a, me * size, dim)
    out_b = lax.dynamic_update_slice_in_dim(out_b, b, me * size, dim)
    for s in range(1, n):
        a = lax.ppermute(a, "ep", fw)
        b = lax.ppermute(b, "ep", bw)
        src_a = ring_index((pos + n - s) % n, n)
        src_b = ring_index((pos + s) % n, n)
        out_a = lax.dynamic_update_slice_in_dim(out_a, a, src_a * size, dim)
        out_b = lax.dynamic_update_slice_in_dim(out_b, b, src_b * size, dim)
    return (out_a, out_b), (a, b)


class GatherRing:
    def __init__(self, x):
        half = x.shape[0] // 2
        self.moving = [x[:half], x[half:]]
        self.got = [[self.moving[0]], [self.moving[1]]]

    def hop(self):
        perms = ring_perms(lax.axis_size("ep"))
        self.moving = [lax.ppermute(v, "ep", p) for v, p in zip(self.moving, perms)]
        for k in range(2):
            self.got[k].append(self.moving[k])

    def settle(self, values):
        self.moving = list(values)
        for k in range(2):
            self.got[k][-1] = self.moving[k]


def lock(rings, *values):
    flat = [m for r in rings for m in r.moving] + list(values)
    flat = list(lax.optimization_barrier(tuple(flat))) if flat else []
    for r in rings:
        r.settle([flat.pop(0), flat.pop(0)])
    return flat


def hop(rings):
    for r in rings:
        r.hop()


CORE = [(0, 1), (1, 0), (2, 3), (3, 2)]
CROSS = [(0, 2), (2, 0), (1, 3), (3, 1)]


def ws_stack(q):
    w = lax.axis_index("ws")
    x, c = w // 2, w % 2
    other = lax.ppermute(q, "ws", CROSS)
    mine = jnp.where(x == 0, jnp.stack([q, other]), jnp.stack([other, q]))
    peer = lax.ppermute(mine, "ws", CORE)
    both = jnp.where(c == 0, jnp.stack([mine, peer], 1), jnp.stack([peer, mine], 1))
    return both.reshape((4,) + q.shape)


def ws_gather(q):
    rows, cols = q.shape
    return jnp.transpose(ws_stack(q), (1, 0, 2)).reshape(rows, 4 * cols)


def quarters(p):
    w = lax.axis_index("ws")
    x, c = w // 2, w % 2
    cols = p.shape[1] // 4
    take = lambda q: lax.dynamic_slice_in_dim(p, q * cols, cols, 1)
    return [take((1 - x) * 2 + 1 - c), take(x * 2 + 1 - c), take((1 - x) * 2 + c), take(x * 2 + c)]


MESH_ID = pl.DeviceIdType.MESH
VMEM_CAP = 60 * 1024 * 1024


def any_spec():
    return pl.BlockSpec(memory_space=pl.ANY)


def vmem_spec():
    return pl.BlockSpec(memory_space=pltpu.VMEM)


def ws_places():
    w = lax.axis_index("ws")
    x, c = w // 2, w % 2
    return w, x, c, x * 2 + 1 - c, (1 - x) * 2 + c


def meet(peers):
    barrier = pltpu.get_barrier_semaphore()
    for peer in peers:
        pl.semaphore_signal(barrier, inc=1, device_id=peer, device_id_type=MESH_ID)
    pl.semaphore_wait(barrier, len(peers))


def push(src, dst, send, recv, peer):
    return pltpu.make_async_remote_copy(
        src_ref=src, dst_ref=dst, send_sem=send, recv_sem=recv, device_id=peer, device_id_type=MESH_ID
    )


def columns(q, cols):
    return pl.ds(pl.multiple_of(q * cols, cols), cols)


def params(cid):
    return pltpu.CompilerParams(
        collective_id=cid, has_side_effects=True, vmem_limit_bytes=VMEM_CAP
    )


def reduce_kernel(chunks, p, o, rc, sx, rx, cs, cr, xs, xr):
    w, x, c, core, cross = ws_places()
    rows, cols = o.shape
    step = rows // chunks
    meet([{"ws": core}, {"ws": cross}])
    sent = []
    for k in range(chunks):
        r = pl.ds(k * step, step)
        for j, far in enumerate((1 - x, x)):
            src = p.at[r, columns(far * 2 + 1 - c, cols)]
            copy = push(src, rc.at[j, r], cs.at[j, k], cr.at[j, k], {"ws": core})
            copy.start()
            sent.append(copy)
    cross_sent = []
    for k in range(chunks):
        r = pl.ds(k * step, step)
        sent[2 * k].wait_recv()
        total = p[r, columns((1 - x) * 2 + c, cols)].astype(F32) + rc[0, r].astype(F32)
        sx[r] = total.astype(BF)
        copy = push(sx.at[r], rx.at[r], xs.at[k], xr.at[k], {"ws": cross})
        copy.start()
        cross_sent.append(copy)
    for k in range(chunks):
        r = pl.ds(k * step, step)
        sent[2 * k + 1].wait_recv()
        near = p[r, columns(x * 2 + c, cols)].astype(F32) + rc[1, r].astype(F32)
        cross_sent[k].wait_recv()
        o[r] = near + rx[r].astype(F32)
    for copy in sent + cross_sent:
        copy.wait_send()


def ws_reduce(p, cid, chunks=4):
    rows, cols = p.shape[0], p.shape[1] // 4
    dma = pltpu.SemaphoreType.DMA
    return pl.pallas_call(
        functools.partial(reduce_kernel, chunks),
        out_shape=jax.ShapeDtypeStruct((rows, cols), F32),
        in_specs=[vmem_spec()],
        out_specs=vmem_spec(),
        scratch_shapes=[
            pltpu.VMEM((2, rows, cols), BF),
            pltpu.VMEM((rows, cols), BF),
            pltpu.VMEM((rows, cols), BF),
            dma((2, chunks)),
            dma((2, chunks)),
            dma((chunks,)),
            dma((chunks,)),
        ],
        compiler_params=params(cid),
        name=f"ws_reduce_{cid}",
    )(p)


def to_lanes(column):
    return jnp.broadcast_to(column, (column.shape[0], 128)).T[:8]


def to_column(lanes):
    return jnp.broadcast_to(lanes[:1], (128, lanes.shape[1])).T[:, :1]


def sum_over_ws(stat, stats, send, recv, mates):
    copies = []
    for j, peer in enumerate(mates):
        copy = push(stat, stats.at[j], send.at[j], recv.at[j], peer)
        copy.start()
        copies.append(copy)
    for copy in copies:
        copy.wait()
    return stat[...] + stats[0] + stats[1] + stats[2]


def mix_kernel(chunks, p, xq, gain, sel, o, inv, hn, picked, rc, sx, rx, stat, stats, cs, cr, xs, xr, ss, sr):
    w, x, c, core, cross = ws_places()
    mates = [{"ws": core}, {"ws": cross}, {"ws": (1 - x) * 2 + 1 - c}]
    rows, cols = o.shape
    step = rows // chunks
    meet(mates)
    sent = []
    for k in range(chunks):
        r = pl.ds(k * step, step)
        for j, far in enumerate((1 - x, x)):
            src = p.at[r, columns(far * 2 + 1 - c, cols)]
            copy = push(src, rc.at[j, r], cs.at[j, k], cr.at[j, k], {"ws": core})
            copy.start()
            sent.append(copy)
    cross_sent = []
    for k in range(chunks):
        r = pl.ds(k * step, step)
        sent[2 * k].wait_recv()
        total = p[r, columns((1 - x) * 2 + c, cols)].astype(F32) + rc[0, r].astype(F32)
        sx[r] = total.astype(BF)
        copy = push(sx.at[r], rx.at[r], xs.at[k], xr.at[k], {"ws": cross})
        copy.start()
        cross_sent.append(copy)
    for k in range(chunks):
        r = pl.ds(k * step, step)
        sent[2 * k + 1].wait_recv()
        near = p[r, columns(x * 2 + c, cols)].astype(F32) + rc[1, r].astype(F32)
        cross_sent[k].wait_recv()
        total = near + rx[r].astype(F32) + xq[r].astype(F32)
        o[r] = total
        stat[:, k * step : (k + 1) * step] = to_lanes(jnp.sum(total * total, axis=1, keepdims=True))
    total = sum_over_ws(stat, stats, ss, sr, mates)
    inverse = lax.rsqrt(to_column(total) / (4 * cols) + EPS)
    inv[...] = inverse
    hn[...] = (o[...] * inverse * gain[...]).astype(BF)
    picked[...] = jnp.dot(sel[...], hn[...], preferred_element_type=F32).astype(BF)
    for copy in sent + cross_sent:
        copy.wait_send()


def mix(p, xq, gain, sel, cid, chunks=4):
    rows, cols = xq.shape
    slots = sel.shape[0]
    dma = pltpu.SemaphoreType.DMA
    return pl.pallas_call(
        functools.partial(mix_kernel, chunks),
        out_shape=(
            jax.ShapeDtypeStruct((rows, cols), F32),
            jax.ShapeDtypeStruct((rows, 1), F32),
            jax.ShapeDtypeStruct((rows, cols), BF),
            jax.ShapeDtypeStruct((slots, cols), BF),
        ),
        in_specs=[vmem_spec()] * 4,
        out_specs=(vmem_spec(),) * 4,
        scratch_shapes=[
            pltpu.VMEM((2, rows, cols), BF),
            pltpu.VMEM((rows, cols), BF),
            pltpu.VMEM((rows, cols), BF),
            pltpu.VMEM((8, rows), F32),
            pltpu.VMEM((3, 8, rows), F32),
            dma((2, chunks)),
            dma((2, chunks)),
            dma((chunks,)),
            dma((chunks,)),
            dma((3,)),
            dma((3,)),
        ],
        compiler_params=params(cid),
        name=f"mix_{cid}",
    )(p, xq, gain, sel)


def home_kernel(sel, d, extra, hidden, inv, gain, dy, dh, gn, o, stat, stats, mine, own, ss, sr, xs, xr, cs, cr):
    w, x, c, core, cross = ws_places()
    mates = [{"ws": core}, {"ws": cross}, {"ws": (1 - x) * 2 + 1 - c}]
    rows, cols = hidden.shape
    meet(mates)
    total = lax.dot_general(sel[...], d[...], (((0,), (0,)), ((), ())), preferred_element_type=F32)
    total += extra[...]
    unit = hidden[...] * inv[...]
    gn[...] = jnp.broadcast_to(jnp.sum(total * unit, axis=0, keepdims=True), gn.shape)
    weighted = total * gain[...]
    stat[...] = to_lanes(jnp.sum(weighted * unit, axis=1, keepdims=True))
    mean = to_column(sum_over_ws(stat, stats, ss, sr, mates)) / (4 * cols)
    result = dy[...].astype(F32) + inv[...] * (weighted - unit * mean)
    dh[...] = result
    mine[...] = result.astype(BF)
    place = o.at[:, columns(w, cols)]
    local = pltpu.make_async_copy(mine, place, own)
    over = push(mine, place, xs, xr, {"ws": cross})
    beside_ = push(mine, place, cs.at[0], cr.at[0], {"ws": core})
    for copy in (local, over, beside_):
        copy.start()
    over.wait_recv()
    block = o.at[:, columns(cross, cols)]
    onward = push(block, block, cs.at[1], cr.at[1], {"ws": core})
    onward.start()
    for copy in (local, beside_, onward):
        copy.wait()
    over.wait_send()


def home(sel, d, extra, hidden, inv, gain, dy, cid):
    rows, cols = hidden.shape
    dma = pltpu.SemaphoreType.DMA
    return pl.pallas_call(
        home_kernel,
        out_shape=(
            jax.ShapeDtypeStruct((rows, cols), F32),
            jax.ShapeDtypeStruct((8, cols), F32),
            jax.ShapeDtypeStruct((rows, 4 * cols), BF),
        ),
        in_specs=[vmem_spec()] * 7,
        out_specs=(vmem_spec(), vmem_spec(), any_spec()),
        scratch_shapes=[
            pltpu.VMEM((8, rows), F32),
            pltpu.VMEM((3, 8, rows), F32),
            pltpu.VMEM((rows, cols), BF),
            dma,
            dma((3,)),
            dma((3,)),
            dma,
            dma,
            dma((2,)),
            dma((2,)),
        ],
        compiler_params=params(cid),
        name=f"home_{cid}",
    )(sel, d, extra, hidden, inv, gain, dy)


def spread_kernel(chunks, q, o, own, cs, cr, xs, xr):
    w, x, c, core, cross = ws_places()
    rows, cols = q.shape
    step = rows // chunks
    meet([{"ws": core}, {"ws": cross}])
    local = pltpu.make_async_copy(q, o.at[:, columns(w, cols)], own)
    local.start()
    crossing, coring = [], []
    for k in range(chunks):
        r = pl.ds(k * step, step)
        dst = o.at[r, columns(w, cols)]
        copy = push(q.at[r], dst, xs.at[k], xr.at[k], {"ws": cross})
        copy.start()
        crossing.append(copy)
        copy = push(q.at[r], dst, cs.at[0, k], cr.at[0, k], {"ws": core})
        copy.start()
        coring.append(copy)
    for k in range(chunks):
        r = pl.ds(k * step, step)
        crossing[k].wait_recv()
        block = o.at[r, columns(cross, cols)]
        copy = push(block, block, cs.at[1, k], cr.at[1, k], {"ws": core})
        copy.start()
        coring.append(copy)
    local.wait()
    for copy in coring:
        copy.wait()
    for copy in crossing:
        copy.wait_send()


def ws_spread(q, cid, chunks=4):
    rows, cols = q.shape
    dma = pltpu.SemaphoreType.DMA
    return pl.pallas_call(
        functools.partial(spread_kernel, chunks),
        out_shape=jax.ShapeDtypeStruct((rows, 4 * cols), q.dtype),
        in_specs=[any_spec()],
        out_specs=any_spec(),
        scratch_shapes=[dma, dma((2, chunks)), dma((2, chunks)), dma((chunks,)), dma((chunks,))],
        compiler_params=params(cid),
        name=f"ws_spread_{cid}",
    )(q)


class Dispatch:
    def __init__(self, n, axes, qs, os, own, ps, pr, cs, cr, xs, xr):
        self.n, self.axes, self.qs, self.os = n, axes, qs, os
        self.own, self.ps, self.pr, self.cs, self.cr, self.xs, self.xr = own, ps, pr, cs, cr, xs, xr
        self.e = lax.axis_index("ep")
        self.w, _, _, self.core, self.cross = ws_places()
        self.steps = [(i, k) for k in range(n) for i in range(len(axes))]

    def window(self, i, g, q):
        rows, cols = self.qs[i].shape[1:]
        if self.axes[i] == 0:
            return self.os[i].at[g, pl.ds(pl.multiple_of(q * rows, rows), rows)]
        return self.os[i].at[g, :, columns(q, cols)]

    def local(self, i):
        return pltpu.make_async_copy(
            self.qs[i].at[self.e], self.window(i, self.e, self.w), self.own.at[i]
        )

    def sent(self, i, k):
        d = (self.e + k) % self.n
        dst = self.window(i, self.e, self.w)
        return push(self.qs[i].at[d], dst, self.ps.at[i, k], self.pr.at[i, k], {"ep": d})

    def to_cross(self, i, k):
        block = self.window(i, (self.e + self.n - k) % self.n, self.w)
        return push(block, block, self.xs.at[i, k], self.xr.at[i, k], {"ws": self.cross})

    def to_core(self, i, j, k):
        block = self.window(i, (self.e + self.n - k) % self.n, self.cross if j else self.w)
        return push(block, block, self.cs.at[i, j, k], self.cr.at[i, j, k], {"ws": self.core})

    def start(self):
        for i, k in self.steps:
            (self.local(i) if k == 0 else self.sent(i, k)).start()

    def hand_on(self):
        for i, k in self.steps:
            if k == 0:
                self.local(i).wait()
            else:
                self.sent(i, k).wait_recv()
            self.to_cross(i, k).start()
            self.to_core(i, 0, k).start()

    def onward(self):
        for i, k in self.steps:
            self.to_cross(i, k).wait_recv()
            self.to_core(i, 1, k).start()

    def run(self):
        self.hand_on()
        self.onward()

    def finish(self):
        for i, k in self.steps:
            if k > 0:
                self.sent(i, k).wait_send()
            self.to_cross(i, k).wait_send()
            self.to_core(i, 0, k).wait()
            self.to_core(i, 1, k).wait()


def dispatch_peers(n):
    e = lax.axis_index("ep")
    _, _, _, core, cross = ws_places()
    return [{"ep": (e + k) % n} for k in range(1, n)] + [{"ws": core}, {"ws": cross}]


def dispatch_sems(m, n):
    dma = pltpu.SemaphoreType.DMA
    return [dma((m,))] + [dma((m, n))] * 2 + [dma((m, 2, n))] * 2 + [dma((m, n))] * 2


def dispatched(q, axis):
    n, rows, cols = q.shape
    shape = (n, 4 * rows, cols) if axis == 0 else (n, rows, 4 * cols)
    return jax.ShapeDtypeStruct(shape, q.dtype)


def dispatch_kernel(n, axes, *refs):
    m = len(axes)
    meet(dispatch_peers(n))
    work = Dispatch(n, axes, refs[:m], refs[m : 2 * m], *refs[2 * m :])
    work.start()
    work.run()
    work.finish()


def dispatch(cid, *payloads):
    n = payloads[0][0].shape[0]
    m = len(payloads)
    return pl.pallas_call(
        functools.partial(dispatch_kernel, n, [axis for _, axis in payloads]),
        out_shape=[dispatched(*payload) for payload in payloads],
        in_specs=[any_spec()] * m,
        out_specs=[any_spec()] * m,
        scratch_shapes=dispatch_sems(m, n),
        compiler_params=params(cid),
        name=f"dispatch_{cid}",
    )(*[q for q, _ in payloads])


def return_kernel(n, p, dg, o, dgo, rc, sx, rx, st, dgr, dgs, own, cs, cr, xs, xr, ps, pr, gs, gr, hs, hr):
    e = lax.axis_index("ep")
    w, x, c, core, cross = ws_places()
    diag = (1 - x) * 2 + 1 - c
    cols = o.shape[2]
    peers = [{"ep": (e + k) % n} for k in range(1, n)]
    meet(peers + [{"ws": core}, {"ws": cross}, {"ws": diag}])
    order = list(range(1, n)) + [0]
    coring = {}
    for k in order:
        g = (e + k) % n
        for j, far in enumerate((1 - x, x)):
            src = p.at[g, :, columns(far * 2 + 1 - c, cols)]
            copy = push(src, rc.at[j, k], cs.at[j, k], cr.at[j, k], {"ws": core})
            copy.start()
            coring[j, k] = copy
    gates = []
    for j, peer in enumerate((core, cross, diag)):
        copy = push(dg, dgr.at[j], gs.at[j], gr.at[j], {"ws": peer})
        copy.start()
        gates.append(copy)
    crossing = {}
    for k in order:
        g = (e + k) % n
        coring[0, k].wait_recv()
        total = p[g, :, columns((1 - x) * 2 + c, cols)].astype(F32) + rc[0, k].astype(F32)
        sx[k] = total.astype(BF)
        crossing[k] = push(sx.at[k], rx.at[k], xs.at[k], xr.at[k], {"ws": cross})
        crossing[k].start()
    for copy in gates:
        copy.wait_recv()
    dgs[...] = dg[...] + dgr[0] + dgr[1] + dgr[2]
    home = []
    for k in order:
        g = (e + k) % n
        coring[1, k].wait_recv()
        near = p[g, :, columns(x * 2 + c, cols)].astype(F32) + rc[1, k].astype(F32)
        crossing[k].wait_recv()
        st[k] = (near + rx[k].astype(F32)).astype(BF)
        if k > 0:
            copy = push(st.at[k], o.at[e], ps.at[k], pr.at[k], peers[k - 1])
            copy.start()
            home.append(copy)
            copy = push(dgs.at[g], dgo.at[e], hs.at[k], hr.at[k], peers[k - 1])
            copy.start()
            home.append(copy)
        else:
            copy = pltpu.make_async_copy(st.at[0], o.at[e], own.at[0])
            copy.start()
            home.append(copy)
            copy = pltpu.make_async_copy(dgs.at[g], dgo.at[e], own.at[1])
            copy.start()
            home.append(copy)
    for copy in home:
        copy.wait()
    for copy in gates + list(coring.values()) + list(crossing.values()):
        copy.wait_send()


def give_back(p, dg, cid):
    n, rows, cols = p.shape[0], p.shape[1], p.shape[2] // 4
    dma = pltpu.SemaphoreType.DMA
    return pl.pallas_call(
        functools.partial(return_kernel, n),
        out_shape=(jax.ShapeDtypeStruct((n, rows, cols), BF), jax.ShapeDtypeStruct(dg.shape, F32)),
        in_specs=[vmem_spec(), vmem_spec()],
        out_specs=(any_spec(), any_spec()),
        scratch_shapes=[
            pltpu.VMEM((2, n, rows, cols), BF),
            pltpu.VMEM((n, rows, cols), BF),
            pltpu.VMEM((n, rows, cols), BF),
            pltpu.VMEM((n, rows, cols), BF),
            pltpu.VMEM((3,) + dg.shape, F32),
            pltpu.VMEM(dg.shape, F32),
            dma((2,)),
            dma((2, n)),
            dma((2, n)),
            dma((n,)),
            dma((n,)),
            dma((n,)),
            dma((n,)),
            dma((3,)),
            dma((3,)),
            dma((n,)),
            dma((n,)),
        ],
        compiler_params=params(cid),
        name=f"give_back_{cid}",
    )(p, dg)


def return_part_kernel(n, p, dg, act_h, down_h, o, dgo, part0, part1, part2, part3, rc, sx, rx, st, dgr, dgs,
                       act, down, stage, own, cs, cr, xs, xr, ps, pr, gs, gr, hs, hr, ls, os_):
    e = lax.axis_index("ep")
    w, x, c, core, cross = ws_places()
    diag = (1 - x) * 2 + 1 - c
    cols = o.shape[2]
    size = down.shape[0] // n
    meet([{"ep": (e + k) % n} for k in range(1, n)] + [{"ws": core}, {"ws": cross}, {"ws": diag}])

    def to_core(k, j):
        far = (1 - x) if j == 0 else x
        src = p.at[(e + k) % n, :, columns(far * 2 + 1 - c, cols)]
        return push(src, rc.at[j, k], cs.at[j, k], cr.at[j, k], {"ws": core})

    def to_cross(k):
        return push(sx.at[k], rx.at[k], xs.at[k], xr.at[k], {"ws": cross})

    def to_home(k):
        peer = {"ep": (e + k) % n}
        return (
            push(st.at[k], o.at[e], ps.at[k], pr.at[k], peer),
            push(dgs.at[(e + k) % n], dgo.at[e], hs.at[k], hr.at[k], peer),
        )

    @pl.loop(0, n)
    def _(i):
        to_core((i + 1) % n, 0).start()
        to_core((i + 1) % n, 1).start()

    loads = []
    for i, (src, dst) in enumerate(((act_h, act), (down_h, down))):
        copy = pltpu.make_async_copy(src, dst, ls.at[i])
        copy.start()
        loads.append(copy)
    gates = []
    for j, peer in enumerate((core, cross, diag)):
        copy = push(dg, dgr.at[j], gs.at[j], gr.at[j], {"ws": peer})
        copy.start()
        gates.append(copy)

    @pl.loop(0, n)
    def _(i):
        k = (i + 1) % n
        to_core(k, 0).wait_recv()
        mine = p[(e + k) % n, :, columns((1 - x) * 2 + c, cols)]
        sx[k] = (mine.astype(F32) + rc[0, k].astype(F32)).astype(BF)
        to_cross(k).start()

    for copy in gates:
        copy.wait_recv()
    dgs[...] = dg[...] + dgr[0] + dgr[1] + dgr[2]
    for copy in loads:
        copy.wait()

    per = n // 4

    def out_start(i):
        for j, part in enumerate((part0, part1, part2, part3)):

            @pl.when(i // per == j)
            def _():
                dst = part.at[:, columns(i % per, size)]
                pltpu.make_async_copy(stage.at[i % 2], dst, os_.at[i % 2]).start()

    def out_wait(i):
        pltpu.make_async_copy(stage.at[i % 2], part0.at[:, pl.ds(0, size)], os_.at[i % 2]).wait()

    def tile_of(i):
        r = i // per
        far, other = 1 - r % 2, 1 - r // 2
        quarter = (x + far * (1 - 2 * x)) * 2 + c + other * (1 - 2 * c)
        return quarter * per + i % per

    @pl.loop(0, n)
    def _(i):
        k = (i + 1) % n
        terms = lax.dot_general(
            act[...],
            down[pl.ds(pl.multiple_of(tile_of(i) * size, size), size)],
            (((1,), (1,)), ((), ())),
            preferred_element_type=F32,
        )

        @pl.when(i > 1)
        def _():
            out_wait(i - 2)

        stage[i % 2] = terms.astype(BF)
        out_start(i)
        to_core(k, 1).wait_recv()
        mine = p[(e + k) % n, :, columns(x * 2 + c, cols)]
        near = mine.astype(F32) + rc[1, k].astype(F32)
        to_cross(k).wait_recv()
        st[k] = (near + rx[k].astype(F32)).astype(BF)

        @pl.when(i < n - 1)
        def _():
            for copy in to_home(k):
                copy.start()

    last = [
        pltpu.make_async_copy(st.at[0], o.at[e], own.at[0]),
        pltpu.make_async_copy(dgs.at[e], dgo.at[e], own.at[1]),
    ]
    for copy in last:
        copy.start()
    for i in range(n - 2, n):
        out_wait(i)
    for copy in last:
        copy.wait()
    for copy in gates:
        copy.wait_send()

    @pl.loop(0, n)
    def _(k):
        to_core(k, 0).wait_send()
        to_core(k, 1).wait_send()
        to_cross(k).wait_send()

    @pl.loop(1, n)
    def _(k):
        for copy in to_home(k):
            copy.wait()


def give_back_part(p, dg, act, down, cid):
    n, cap, cols = p.shape[0], p.shape[1], p.shape[2] // 4
    dma = pltpu.SemaphoreType.DMA
    vm = lambda a: pltpu.VMEM(a.shape, a.dtype)
    count, width = act.shape[0], down.shape[0]
    return pl.pallas_call(
        functools.partial(return_part_kernel, n),
        out_shape=(
            jax.ShapeDtypeStruct((n, cap, cols), BF),
            jax.ShapeDtypeStruct(dg.shape, F32),
        )
        + (jax.ShapeDtypeStruct((count, width // 4), BF),) * 4,
        in_specs=[vmem_spec(), vmem_spec(), any_spec(), any_spec()],
        out_specs=(any_spec(),) * 6,
        scratch_shapes=[
            pltpu.VMEM((2, n, cap, cols), BF),
            pltpu.VMEM((n, cap, cols), BF),
            pltpu.VMEM((n, cap, cols), BF),
            pltpu.VMEM((n, cap, cols), BF),
            pltpu.VMEM((3,) + dg.shape, F32),
            pltpu.VMEM(dg.shape, F32),
            vm(act),
            vm(down),
            pltpu.VMEM((2, count, width // n), BF),
            dma((2,)),
            dma((2, n)),
            dma((2, n)),
            dma((n,)),
            dma((n,)),
            dma((n,)),
            dma((n,)),
            dma((3,)),
            dma((3,)),
            dma((n,)),
            dma((n,)),
            dma((2,)),
            dma((2,)),
        ],
        compiler_params=params(cid),
        name=f"give_back_part_{cid}",
    )(p, dg, act, down)


def last_kernel(n, dq, dkv, xt, sel, wq, wkv, hm, dh, unit, inv, gain, lo, gn2, gm, dg, gates, router, xq, *refs):
    grads_in, refs = refs[:5], refs[5:]
    all_dq, gkv, ha, gt_all, lo_all, gv_all, *grads_out = refs[:9]
    (wt, kwt, rows, pt, rc, sx, rx, near, kvs, kvr, stat, stats, gt, vs, vr,
     wl, own, qs, qr, ks, kr, cs, cr, xs, xr, ss, sr, ts, tr, vps, vpr, vws, vwr) = refs[9:42]
    held, (stage, gl, go, dgr, gs, gr, *dsems) = refs[42:47], refs[47:]
    e = lax.axis_index("ep")
    w, x, c, core, cross = ws_places()
    diag = (1 - x) * 2 + 1 - c
    mates = [{"ws": core}, {"ws": cross}, {"ws": diag}]
    pos = ring_pos(n)
    right = {"ep": ring_index((pos + 1) % n, n)}
    left = {"ep": ring_index((pos + n - 1) % n, n)}
    experts, cap, inner = dq.shape
    tokens, cols = dh.shape
    over_last = (((1,), (1,)), ((), ()))
    first = (((0,), (0,)), ((), ()))

    order = ((1 - x) * 2 + 1 - c, x * 2 + 1 - c, (1 - x) * 2 + c, x * 2 + c)

    def load(t):
        r = columns(order[t], cols)
        return (
            pltpu.make_async_copy(wq.at[:, r], wt.at[t % 2], wl.at[t % 2, 0]),
            pltpu.make_async_copy(wkv.at[:, r], kwt.at[t % 2], wl.at[t % 2, 1]),
        )

    for t in range(2):
        for copy in load(t):
            copy.start()
    meet([{"ep": (e + k) % n} for k in range(1, n)] + mates)

    terms = []
    for j, peer in enumerate(mates):
        copy = push(dg, dgr.at[j], gs.at[j], gr.at[j], peer)
        copy.start()
        terms.append(copy)

    each = experts // 4

    def dq_copy(f, s, fresh=False):
        peer, sign = (right, -1) if f % 2 == 0 else (left, 1)
        part = pl.ds((f % 2 * 2 + f // 2) * each, each)
        dst = all_dq.at[ring_index((pos + n + sign * s) % n, n), part]
        return push(dq.at[part] if fresh else dst, dst, qs.at[f, s], qr.at[f, s], peer)

    for f in range(4):
        dq_copy(f, 0, True).start()
    mine = pltpu.make_async_copy(dq, all_dq.at[e], own.at[0])
    mine.start()

    def dq_step(s):
        for f in range(4):
            dq_copy(f, s - 1).wait_recv()

            @pl.when(s < n - 1)
            def _():
                dq_copy(f, s).start()

    def kv_copy(k, s):
        return push(kvs.at[k, s], kvr.at[k, s], ks.at[k, s], kr.at[k, s], left if k else right)

    def kv_step(s, begin=False):
        for k in range(2):
            ahead = s + 1 if k else n - 1 - s
            block = ring_index((pos + ahead) % n, n)
            value = jnp.dot(xt[block], dkv[k], preferred_element_type=F32)
            if not begin:
                kv_copy(k, s - 1).wait_recv()
                value = value + kvr[k, s - 1].astype(F32)

            @pl.when(s < n - 1)
            def _():
                kvs[k, s] = value.astype(BF)
                kv_copy(k, s).start()

            @pl.when(s == n - 1)
            def _():
                gkv[k] = value

    def share(src, dst, j):
        place = dst.at[:, columns(w, cols)]
        local = pltpu.make_async_copy(src, place, own.at[1 + j])
        over = push(src, place, xs.at[1 + j], xr.at[1 + j], {"ws": cross})
        beside = push(src, place, ts.at[j, 0], tr.at[j, 0], {"ws": core})
        for copy in (local, over, beside):
            copy.start()
        return local, over, beside

    def hand_on(dst, j, over):
        over.wait_recv()
        block = dst.at[:, columns(cross, cols)]
        copy = push(block, block, ts.at[j, 1], tr.at[j, 1], {"ws": core})
        copy.start()
        return copy

    kv_step(0, True)
    spread = Dispatch(n, (0,), (hm,), (ha,), *dsems)
    spread.start()

    def tile(t):
        for copy in load(t):
            copy.wait()

        @pl.loop(0, experts)
        def _(i):
            part = lax.dot_general(dq[i], wt[t % 2, i], over_last, preferred_element_type=F32)
            rows[pl.ds(pl.multiple_of(i * cap, cap), cap)] = part.astype(BF)

        total = lax.dot_general(sel[...], rows[...], first, preferred_element_type=F32)
        for k in range(2):
            total += lax.dot_general(dkv[k], kwt[t % 2, k], over_last, preferred_element_type=F32)
        if t < 2:
            for copy in load(t + 2):
                copy.start()
        return total

    coring = []
    for j in range(2):
        pt[j] = tile(j).astype(BF)
        copy = push(pt.at[j], rc.at[j], cs.at[j], cr.at[j], {"ws": core})
        copy.start()
        coring.append(copy)
    kv_step(1)
    dq_step(1)
    total = tile(2)
    coring[0].wait_recv()
    sx[...] = (total + rc[0].astype(F32)).astype(BF)
    crossing = push(sx, rx, xs.at[0], xr.at[0], {"ws": cross})
    crossing.start()
    total = tile(3)
    coring[1].wait_recv()
    near[...] = total + rc[1].astype(F32)
    kv_step(2)
    dq_step(2)
    loads = []
    for i in range(5):
        copy = pltpu.make_async_copy(grads_in[i], held[i], gl.at[i])
        copy.start()
        loads.append(copy)
    for copy in terms:
        copy.wait()
    line = dg[...] + dgr[0] + dgr[1] + dgr[2]
    picks = (gates.shape[0], experts * cap)
    owner = lax.broadcasted_iota(jnp.int32, picks, 1) // cap
    line = jnp.where(
        lax.broadcasted_iota(jnp.int32, picks, 0) == owner, jnp.broadcast_to(line[:1], picks), 0.0
    )
    dgate = None
    for _ in range(3):
        high = line.astype(BF)
        line = line - high.astype(F32)
        part = jnp.dot(high, sel[...], preferred_element_type=F32)
        dgate = part if dgate is None else dgate + part
    g = gates[...]
    d_logits = (g * (dgate - jnp.sum(g * dgate, axis=0, keepdims=True))).astype(BF)
    ga = jnp.dot(d_logits, xq[...], preferred_element_type=F32)[:experts]
    extra = lax.dot_general(d_logits, router[...], first, preferred_element_type=F32)
    crossing.wait_recv()
    d_xn = near[...] + rx[...].astype(F32) + extra
    u = unit[...]
    row = lax.broadcasted_iota(jnp.int32, gn2.shape, 0)
    vs[:8] = jnp.where(row == 0, jnp.sum(d_xn * u, axis=0, keepdims=True), gn2[...])
    vs[8 : 8 + experts] = ga
    vs[8 + experts :] = gm[...]
    weighted = d_xn * gain[...]
    near[...] = weighted
    across = jnp.sum(weighted * u, axis=1, keepdims=True)
    stat[...] = jnp.broadcast_to(across, (tokens, 128)).T[:8]
    sums = []
    for j, peer in enumerate(mates):
        copy = push(stat, stats.at[j], ss.at[j], sr.at[j], peer)
        copy.start()
        sums.append(copy)
    gains = []
    for k in range(1, n):
        copy = push(vs, vr.at[k - 1], vps.at[k], vpr.at[k], {"ep": (e + k) % n})
        copy.start()
        gains.append(copy)
    for copy in sums:
        copy.wait_recv()
    mean = (stat[...] + stats[0] + stats[1] + stats[2]) / (4 * cols)
    mean = jnp.broadcast_to(mean[:1], (128, tokens)).T[:, :1]
    gt[...] = (dh[...] + inv[...] * (near[...] - u * mean)).astype(BF)
    gt_copies = share(gt, gt_all, 1)
    lo_copies = share(lo, lo_all, 0)
    kv_step(3)
    dq_step(3)
    spread.hand_on()
    for copy in loads:
        copy.wait()

    size = grads_out[0].shape[0] // 8
    rows_in, dy_in, dgate_in, dup_in, down_in = held

    def out_copy(i, j):
        dst = grads_out[j].at[pl.ds(pl.multiple_of(i * size, size), size)]
        return pltpu.make_async_copy(stage.at[j], dst, go.at[j])

    @pl.loop(4, n)
    def _(s):
        kv_step(s)
        dq_step(s)

        @pl.loop(0, 2)
        def _(h):
            i = (s - 4) * 2 + h
            for j, (a, b) in enumerate(((rows_in, dgate_in), (rows_in, dup_in), (dy_in, down_in))):
                grad = lax.dot_general(
                    a[:, columns(i, size)], b[...], first, preferred_element_type=F32
                )

                @pl.when(i > 0)
                def _():
                    out_copy(i - 1, j).wait()

                stage[j] = grad.astype(BF)
                out_copy(i, j).start()

    gt_core = hand_on(gt_all, 1, gt_copies[1])
    lo_core = hand_on(lo_all, 0, lo_copies[1])
    spread.onward()
    for copy in gains:
        copy.wait_recv()
    vs_total = vs[...]
    for k in range(n - 1):
        vs_total += vr[k]
    for copy in gains:
        copy.wait_send()
    vs[...] = vs_total
    place = gv_all.at[:, columns(w, cols)]
    gv_copies = [pltpu.make_async_copy(vs, place, own.at[3])]
    for j, peer in enumerate(mates):
        gv_copies.append(push(vs, place, vws.at[j], vwr.at[j], peer))
    for copy in gv_copies:
        copy.start()
    for j in range(3):
        out_copy(7, j).wait()
    mine.wait()
    for copy in gv_copies + [lo_copies[0], lo_copies[2], gt_copies[0], gt_copies[2], lo_core, gt_core]:
        copy.wait()
    for copy in coring + sums + [crossing, lo_copies[1], gt_copies[1]]:
        copy.wait_send()
    for f in range(4):
        dq_copy(f, 0, True).wait_send()

    @pl.loop(1, n - 1)
    def _(s):
        for f in range(4):
            dq_copy(f, s).wait_send()

    @pl.loop(0, n - 1)
    def _(s):
        for k in range(2):
            kv_copy(k, s).wait_send()

    spread.finish()


def last_stage(cid, dq, dkv, xt, sel, wq, wkv, hm, dh, unit, inv, gain, lo, gn2, gm, dg, gates, router, xq, *grads):
    n = xt.shape[0]
    experts, cap, inner = dq.shape
    tokens, cols = dh.shape
    block = xt.shape[1]
    dma = pltpu.SemaphoreType.DMA
    vm, hbm = vmem_spec(), any_spec()
    small = (8 + experts + gm.shape[0], cols)
    width, f = grads[0].shape[1], grads[2].shape[1]
    wide = jax.ShapeDtypeStruct((tokens, 4 * cols), BF)
    return pl.pallas_call(
        functools.partial(last_kernel, n),
        out_shape=[
            jax.ShapeDtypeStruct((n,) + dq.shape, BF),
            jax.ShapeDtypeStruct((2, block, inner), F32),
            dispatched(hm, 0),
            wide,
            wide,
            jax.ShapeDtypeStruct((small[0], 4 * cols), F32),
        ]
        + [jax.ShapeDtypeStruct((width, f), BF)] * 3,
        in_specs=[vm] * 4 + [hbm] * 3 + [vm] * 11 + [hbm] * 5,
        out_specs=[hbm, vm] + [hbm] * 7,
        scratch_shapes=[
            pltpu.VMEM((2, experts, cols, inner), BF),
            pltpu.VMEM((2, 2, cols, inner), BF),
            pltpu.VMEM((experts * cap, cols), BF),
            pltpu.VMEM((2, tokens, cols), BF),
            pltpu.VMEM((2, tokens, cols), BF),
            pltpu.VMEM((tokens, cols), BF),
            pltpu.VMEM((tokens, cols), BF),
            pltpu.VMEM((tokens, cols), F32),
            pltpu.VMEM((2, n - 1, block, inner), BF),
            pltpu.VMEM((2, n - 1, block, inner), BF),
            pltpu.VMEM((8, tokens), F32),
            pltpu.VMEM((3, 8, tokens), F32),
            pltpu.VMEM((tokens, cols), BF),
            pltpu.VMEM(small, F32),
            pltpu.VMEM((n - 1,) + small, F32),
            dma((2, 2)),
            dma((4,)),
            dma((4, n)),
            dma((4, n)),
            dma((2, n)),
            dma((2, n)),
            dma((2,)),
            dma((2,)),
            dma((3,)),
            dma((3,)),
            dma((3,)),
            dma((3,)),
            dma((2, 2)),
            dma((2, 2)),
            dma((n,)),
            dma((n,)),
            dma((3,)),
            dma((3,)),
        ]
        + [pltpu.VMEM(a.shape, a.dtype) for a in grads]
        + [pltpu.VMEM((3, width // 8, f), BF), dma((5,)), dma((3,))]
        + [pltpu.VMEM((3,) + dg.shape, F32), dma((3,)), dma((3,))]
        + dispatch_sems(1, n),
        compiler_params=params(cid),
        name=f"last_{cid}",
    )(dq, dkv, xt, sel, wq, wkv, hm, dh, unit, inv, gain, lo, gn2, gm, dg, gates, router, xq, *grads)


def grad_slots_kernel(n, dest, x, y, o, picked, ys):
    e = pl.program_id(0)
    cap = y.shape[2]
    index = e * cap + lax.broadcasted_iota(jnp.int32, (cap, x.shape[1]), 0)
    for g in range(n):
        hit = (dest[g, 0:1, :] == index) | (dest[g, 1:2, :] == index)
        sel = jnp.where(hit, 1.0, 0.0).astype(BF)
        r = pl.ds(g * cap, cap)
        picked[r] = jnp.dot(sel, x[g], preferred_element_type=F32).astype(BF)
        ys[r] = y[g, 0]
    o[0] = lax.dot_general(
        picked[...], ys[...], (((0,), (0,)), ((), ())), preferred_element_type=F32
    )


def grad_slots(dest, x, y):
    n, tokens, block = x.shape
    experts, cap, cols = y.shape[1:]
    return pl.pallas_call(
        functools.partial(grad_slots_kernel, n),
        grid=(experts,),
        out_shape=jax.ShapeDtypeStruct((experts, block, cols), F32),
        in_specs=[
            pl.BlockSpec(dest.shape, lambda i: (0, 0, 0)),
            pl.BlockSpec(x.shape, lambda i: (0, 0, 0)),
            pl.BlockSpec((n, 1, cap, cols), lambda i: (0, i, 0, 0)),
        ],
        out_specs=pl.BlockSpec((1, block, cols), lambda i: (i, 0, 0)),
        scratch_shapes=[pltpu.VMEM((n * cap, block), BF), pltpu.VMEM((n * cap, cols), BF)],
        compiler_params=pltpu.CompilerParams(vmem_limit_bytes=VMEM_CAP),
        cost_estimate=pl.CostEstimate(
            flops=2 * experts * n * cap * block * (tokens + cols),
            bytes_accessed=2 * (x.size + y.size) + 4 * experts * block * cols,
            transcendentals=0,
        ),
        name="grad_slots",
    )(dest, x, y)


def collect_kernel(n, v, o, got, part, own, ps, pr, ws, wr):
    e, w = lax.axis_index("ep"), lax.axis_index("ws")
    cols = v.shape[1]
    peers = [{"ep": (e + k) % n} for k in range(1, n)]
    mates = [{"ws": (w + k) % 4} for k in range(1, 4)]
    meet(peers + mates)
    first = []
    for k in range(1, n):
        copy = push(v, got.at[k - 1], ps.at[k], pr.at[k], peers[k - 1])
        copy.start()
        first.append(copy)
    total = v[...]
    for k in range(1, n):
        first[k - 1].wait_recv()
        total += got[k - 1]
    part[...] = total
    mine = o.at[:, columns(w, cols)]
    local = pltpu.make_async_copy(part, mine, own)
    local.start()
    second = []
    for k in range(3):
        copy = push(part, mine, ws.at[k], wr.at[k], mates[k])
        copy.start()
        second.append(copy)
    local.wait()
    for copy in second:
        copy.wait()
    for copy in first:
        copy.wait_send()


def collect(v, cid):
    n = lax.axis_size("ep")
    rows, cols = v.shape
    dma = pltpu.SemaphoreType.DMA
    return pl.pallas_call(
        functools.partial(collect_kernel, n),
        out_shape=jax.ShapeDtypeStruct((rows, 4 * cols), F32),
        in_specs=[vmem_spec()],
        out_specs=vmem_spec(),
        scratch_shapes=[
            pltpu.VMEM((n - 1, rows, cols), F32),
            pltpu.VMEM((rows, cols), F32),
            dma,
            dma((n,)),
            dma((n,)),
            dma((3,)),
            dma((3,)),
        ],
        compiler_params=params(cid),
        name=f"collect_{cid}",
    )(v)


def ring_kernel(n, m, splits, axes, *refs):
    p = len(axes)
    xs, qs, refs = refs[:m], refs[m : m + p], refs[m + p :]
    os, qos, refs = refs[:m], refs[m : m + p], refs[m + p :]
    own, send, recv, *sems = refs
    pos, me = ring_pos(n), lax.axis_index("ep")
    right = {"ep": ring_index((pos + 1) % n, n)}
    left = {"ep": ring_index((pos + n - 1) % n, n)}
    _, _, _, core, cross = ws_places()
    meet([{"ep": (me + k) % n} for k in range(1, n)] + [{"ws": core}, {"ws": cross}])
    flows = []
    for i in range(m):
        part = xs[i].shape[0] // (2 * splits[i])
        for k in range(splits[i]):
            flows.append((i, k * part, part, right, -1))
            flows.append((i, (splits[i] + k) * part, part, left, 1))

    def window(i, first, part, owner):
        size = xs[i].shape[1]
        return os[i].at[pl.ds(first, part), pl.ds(pl.multiple_of(owner * size, size), size)]

    def start(f, s):
        i, first, part, peer, sign = flows[f]
        owner = ring_index((pos + n + sign * s) % n, n)
        dst = window(i, first, part, owner)
        src = xs[i].at[pl.ds(first, part)] if s == 0 else dst
        copy = push(src, dst, send.at[f, s], recv.at[f, s], peer)
        copy.start()
        return copy

    live = [start(f, 0) for f in range(len(flows))]
    work = Dispatch(n, axes, qs, qos, *sems)
    work.start()
    locals_ = []
    for i in range(m):
        copy = pltpu.make_async_copy(xs[i], window(i, 0, xs[i].shape[0], me), own.at[i])
        copy.start()
        locals_.append(copy)
    done = []
    for s in range(1, n):
        for f in range(len(flows)):
            live[f].wait_recv()
            done.append(live[f])
            if s < n - 1:
                live[f] = start(f, s)
        if s == 1:
            work.run()
    work.finish()
    for copy in locals_:
        copy.wait()
    for copy in done:
        copy.wait_send()


def ring_kernel_gather(cid, splits, xs, payloads):
    n, m = lax.axis_size("ep"), len(xs)
    dma = pltpu.SemaphoreType.DMA
    flows = 2 * sum(splits)
    out = pl.pallas_call(
        functools.partial(ring_kernel, n, m, splits, [axis for _, axis in payloads]),
        out_shape=[jax.ShapeDtypeStruct((x.shape[0], n * x.shape[1], x.shape[2]), x.dtype) for x in xs]
        + [dispatched(*payload) for payload in payloads],
        in_specs=[any_spec()] * (m + len(payloads)),
        out_specs=[any_spec()] * (m + len(payloads)),
        scratch_shapes=[dma((m,)), dma((flows, n)), dma((flows, n))] + dispatch_sems(len(payloads), n),
        compiler_params=params(cid),
        name=f"ring_{cid}",
    )(*xs, *[q for q, _ in payloads])
    return out[:m], out[m:]


def project_kernel(experts, parts, extra, sel, y, *rest):
    weights, rest = rest[:parts], rest[parts:]
    if extra:
        kv, kv_weight, o, rows = rest
    else:
        o, rows = rest
    each = experts // parts
    cap = y.shape[1]
    over_last = (((1,), (1,)), ((), ()))
    for i in range(experts):
        weight = weights[i // each][i % each]
        part = lax.dot_general(y[i], weight, over_last, preferred_element_type=F32)
        rows[pl.ds(i * cap, cap)] = part.astype(BF)
    total = lax.dot_general(sel[...], rows[...], (((0,), (0,)), ((), ())), preferred_element_type=F32)
    if extra:
        for i in range(2):
            total += lax.dot_general(kv[i], kv_weight[i], over_last, preferred_element_type=F32)
    o[...] = total.astype(BF)


def project_back(sel, y, weight, kv=None, kv_weight=None, tile=512):
    experts, cap, inner = y.shape
    width, tokens = weight[0].shape[1], sel.shape[1]
    whole = lambda a: pl.BlockSpec(a.shape, lambda i: (0,) * a.ndim)
    tiled = lambda a: pl.BlockSpec((a.shape[0], tile, a.shape[2]), lambda i: (0, i, 0))
    args, specs = [sel, y, *weight], [whole(sel), whole(y), *map(tiled, weight)]
    if kv is not None:
        args += [kv, kv_weight]
        specs += [whole(kv), tiled(kv_weight)]
    flops = 2 * experts * cap * inner * width + 2 * tokens * experts * cap * width
    return pl.pallas_call(
        functools.partial(project_kernel, experts, len(weight), kv is not None),
        grid=(width // tile,),
        out_shape=jax.ShapeDtypeStruct((tokens, width), BF),
        in_specs=specs,
        out_specs=pl.BlockSpec((tokens, tile), lambda i: (0, i)),
        scratch_shapes=[pltpu.VMEM((experts * cap, tile), BF)],
        compiler_params=pltpu.CompilerParams(vmem_limit_bytes=VMEM_CAP),
        cost_estimate=pl.CostEstimate(
            flops=flops, bytes_accessed=2 * (sum(a.size for a in weight) + sel.size + y.size), transcendentals=0
        ),
        name="project_back",
    )(*args)


def beside(n, axes, qs, os, sems):
    step, last = pl.program_id(0), pl.num_programs(0) - 1

    @pl.when(step == 0)
    def _():
        meet(dispatch_peers(n))
        Dispatch(n, axes, qs, os, *sems).start()

    @pl.when(step == last)
    def _():
        Dispatch(n, axes, qs, os, *sems).hand_on()

    def finish():
        @pl.when(step == last)
        def _():
            work = Dispatch(n, axes, qs, os, *sems)
            work.onward()
            work.finish()

    return finish


def expert_kernel(owners, n, axes, rows, other, dy_down, router, wg, wu, *refs):
    m = len(axes)
    qs, refs = refs[:m], refs[m:]
    d_gate, d_up, act_o, down_o, part, dg = refs[:6]
    finish = beside(n, axes, qs, refs[6 : 6 + m], refs[6 + m :]) if m else None
    expert = lax.axis_index("ep") // owners
    tile, cap = rows.shape[0], dg.shape[2]
    x = rows[...]
    logits = jnp.dot(x, router[...], preferred_element_type=F32)
    index = lax.broadcasted_iota(jnp.int32, logits.shape, 1)
    own = jnp.sum(jnp.where(index == expert, logits, 0.0), axis=1, keepdims=True)
    oth = jnp.sum(jnp.where(index == other[...], logits, 0.0), axis=1, keepdims=True)
    top = jnp.maximum(own, oth)
    own, oth = jnp.exp(own - top), jnp.exp(oth - top)
    gate = own / (own + oth)
    gate_pre = jnp.dot(x, wg[...], preferred_element_type=F32)
    up_pre = jnp.dot(x, wu[...], preferred_element_type=F32)
    sig = 1.0 / (1.0 + jnp.exp(-gate_pre))
    silu = gate_pre * sig
    act = silu * up_pre
    dy = dy_down[...]
    act_o[...] = act.astype(BF)
    down_o[...] = (act * gate).astype(BF)
    dgate = jnp.sum(act * dy, axis=1, keepdims=True)
    d_act = dy * gate
    dgb = (d_act * up_pre * sig * (1.0 + gate_pre * (1.0 - sig))).astype(BF)
    dub = (d_act * silu).astype(BF)
    d_gate[...] = dgb
    d_up[...] = dub
    over_last = (((1,), (1,)), ((), ()))
    total = lax.dot_general(dgb, wg[...], over_last, preferred_element_type=F32)
    total += lax.dot_general(dub, wu[...], over_last, preferred_element_type=F32)
    part[...] = total.astype(BF)
    lane = lax.broadcasted_iota(jnp.int32, (tile, 128), 1)
    both = jnp.where(lane < 4, dgate, 0.25 * gate).T[:8]
    for j in range(tile // cap):
        dg[j] = both[:, j * cap : (j + 1) * cap]
    if m:
        finish()


def expert_pass(rows, other, dy_down, router, wg, wu, owners, cap, payloads, cid, tile=256):
    n, m = lax.axis_size("ep"), len(payloads)
    count, width = rows.shape
    f = wg.shape[1]
    by_row = lambda c: pl.BlockSpec((tile, c), lambda i: (i, 0))
    once = lambda a: pl.BlockSpec(a.shape, lambda i: (0, 0), pipeline_mode=pl.Buffered(1))
    wide = jax.ShapeDtypeStruct((count, f), BF)
    return pl.pallas_call(
        functools.partial(expert_kernel, owners, n, [axis for _, axis in payloads]),
        grid=(count // tile,),
        out_shape=(wide,) * 4
        + (
            jax.ShapeDtypeStruct((count, width), BF),
            jax.ShapeDtypeStruct((count // cap, 8, cap), F32),
            *[dispatched(*payload) for payload in payloads],
        ),
        in_specs=[by_row(width), by_row(1), by_row(f), once(router), once(wg), once(wu)]
        + [any_spec()] * m,
        out_specs=(by_row(f),) * 4
        + (by_row(width), pl.BlockSpec((tile // cap, 8, cap), lambda i: (i, 0, 0)))
        + (any_spec(),) * m,
        scratch_shapes=dispatch_sems(m, n) if m else [],
        compiler_params=params(cid) if m else pltpu.CompilerParams(vmem_limit_bytes=VMEM_CAP),
        cost_estimate=pl.CostEstimate(
            flops=8 * count * width * f, bytes_accessed=4 * width * f + 12 * count * f, transcendentals=count * f
        ),
        name="expert_pass",
    )(rows, other, dy_down, router, wg, wu, *[q for q, _ in payloads])


def turn(v, cos, sin, sign):
    return v * cos + sign * (pltpu.roll(v, HD // 2, 1) * sin)


def masked_scores(q, k, token):
    raw = lax.dot_general(q, k, (((1,), (1,)), ((), ())), preferred_element_type=F32)
    key = lax.broadcasted_iota(jnp.int32, (1, k.shape[0]), 1)
    _, key_segment = place_of(key)
    _, segment = place_of(token)
    allowed = (key <= token) & ((key_segment == 0) | (key_segment == segment))
    return jnp.where(allowed, raw * (1.0 / math.sqrt(HD)), MASKED)


ROWS = 256


def attend_kernel(q_pre, k_pre, v_pre, q_cos, q_sin, cos, sin, token, gate, q, k, v, o, gated, lse):
    k[...] = turn(k_pre[...], cos[...], sin[...], 1).astype(BF)
    v[...] = v_pre[...].astype(BF)
    for i in range(q.shape[0] // ROWS):
        r = pl.ds(i * ROWS, ROWS)
        q[r] = turn(q_pre[r], q_cos[r], q_sin[r], 1).astype(BF)
        scores = masked_scores(q[r], k[...], token[r])
        peak = jnp.max(scores, axis=1, keepdims=True)
        exponent = jnp.exp(scores - peak)
        total = jnp.sum(exponent, axis=1, keepdims=True)
        lse[0, r] = peak + jnp.log(total)
        probs = (exponent / total).astype(BF)
        out = jnp.dot(probs, v[...], preferred_element_type=F32)
        o[r] = out.astype(BF)
        gated[r] = (out * gate[r]).astype(BF)


def attend_specs(slots, tokens):
    head = lambda rows: pl.BlockSpec((rows, HD), lambda h: (0, h))
    table = lambda rows: pl.BlockSpec((rows, HD), lambda h: (0, 0))
    column = pl.BlockSpec((slots, 1), lambda h: (0, 0))
    line = pl.BlockSpec((1, slots, 1), lambda h: (h, 0, 0))
    return head, table, column, line


def attend(q_pre, k_pre, v_pre, q_cos, q_sin, cos, sin, token, gate):
    slots, inner = q_pre.shape
    tokens = k_pre.shape[0]
    head, table, column, line = attend_specs(slots, tokens)
    wide, narrow = jax.ShapeDtypeStruct((slots, inner), BF), jax.ShapeDtypeStruct((tokens, inner), BF)
    return pl.pallas_call(
        attend_kernel,
        grid=(inner // HD,),
        out_shape=(wide, narrow, narrow, wide, wide, jax.ShapeDtypeStruct((inner // HD, slots, 1), F32)),
        in_specs=[head(slots), head(tokens), head(tokens), table(slots), table(slots), table(tokens), table(tokens)]
        + [column] * 2,
        out_specs=(head(slots), head(tokens), head(tokens), head(slots), head(slots), line),
        compiler_params=pltpu.CompilerParams(vmem_limit_bytes=VMEM_CAP),
        cost_estimate=pl.CostEstimate(
            flops=4 * slots * tokens * inner, bytes_accessed=16 * slots * inner, transcendentals=slots * tokens
        ),
        name="attend",
    )(q_pre, k_pre, v_pre, q_cos, q_sin, cos, sin, token, gate)


def attend_back_kernel(n, axes, raw, o, gate, q, k, v, lse, q_cos, q_sin, cos, sin, token, *refs):
    m = len(axes)
    qs, refs = refs[:m], refs[m:]
    dq, dkv, dgate = refs[:3]
    finish = beside(n, axes, qs, refs[3 : 3 + m], refs[3 + m :]) if m else None
    scale = 1.0 / math.sqrt(HD)
    first = (((0,), (0,)), ((), ()))
    over_last = (((1,), (1,)), ((), ()))
    dk, dv = None, None
    for i in range(q.shape[0] // ROWS):
        r = pl.ds(i * ROWS, ROWS)
        across = jnp.sum(raw[r] * o[r].astype(F32), axis=1, keepdims=True)
        line = jnp.broadcast_to(across, (ROWS, 128)).T[:8]
        lanes = pl.ds(i * ROWS, ROWS)

        @pl.when(pl.program_id(0) == 0)
        def _():
            dgate[:, lanes] = line

        @pl.when(pl.program_id(0) > 0)
        def _():
            dgate[:, lanes] += line

        d_o = (raw[r] * gate[r]).astype(BF)
        probs = jnp.exp(masked_scores(q[r], k[...], token[r]) - lse[0, r])
        d_probs = lax.dot_general(d_o, v[...], over_last, preferred_element_type=F32)
        inside = jnp.sum(probs * d_probs, axis=1, keepdims=True)
        d_scores = (probs * (d_probs - inside)).astype(BF)
        part = jnp.dot(d_scores, k[...], preferred_element_type=F32) * scale
        dq[r] = turn(part, q_cos[r], q_sin[r], -1).astype(BF)
        dk_part = lax.dot_general(d_scores, q[r], first, preferred_element_type=F32)
        dv_part = lax.dot_general(probs.astype(BF), d_o, first, preferred_element_type=F32)
        dk = dk_part if dk is None else dk + dk_part
        dv = dv_part if dv is None else dv + dv_part
    dkv[0] = turn(dk * scale, cos[...], sin[...], -1).astype(BF)
    dkv[1] = dv.astype(BF)
    if m:
        finish()


def attend_back(raw, o, gate, q, k, v, lse, q_cos, q_sin, cos, sin, token, payloads, cid):
    n, m = lax.axis_size("ep"), len(payloads)
    slots, inner = q.shape
    tokens = k.shape[0]
    head, table, column, line = attend_specs(slots, tokens)
    return pl.pallas_call(
        functools.partial(attend_back_kernel, n, [axis for _, axis in payloads]),
        grid=(inner // HD,),
        out_shape=(
            jax.ShapeDtypeStruct((slots, inner), BF),
            jax.ShapeDtypeStruct((2, tokens, inner), BF),
            jax.ShapeDtypeStruct((8, slots), F32),
            *[dispatched(*payload) for payload in payloads],
        ),
        in_specs=[head(slots), head(slots), column, head(slots), head(tokens), head(tokens), line]
        + [table(slots), table(slots), table(tokens), table(tokens), column]
        + [any_spec()] * m,
        out_specs=(
            head(slots),
            pl.BlockSpec((2, tokens, HD), lambda h: (0, 0, h)),
            pl.BlockSpec((8, slots), lambda h: (0, 0)),
        )
        + (any_spec(),) * m,
        scratch_shapes=dispatch_sems(m, n) if m else [],
        compiler_params=params(cid) if m else pltpu.CompilerParams(vmem_limit_bytes=VMEM_CAP),
        cost_estimate=pl.CostEstimate(
            flops=10 * slots * tokens * inner, bytes_accessed=16 * slots * inner, transcendentals=slots * tokens
        ),
        name="attend_back",
    )(raw, o, gate, q, k, v, lse, q_cos, q_sin, cos, sin, token, *[v for v, _ in payloads])


def arrivals(rings, n):
    args, specs = [], []
    for p, got in enumerate([got for ring in rings for got in ring.got]):
        each = got[0].shape[0]
        for v in got:
            args.append(v)
            specs.append(
                pl.BlockSpec(
                    (1,) + v.shape[1:],
                    lambda i, p=p, each=each: (jnp.clip(i - p * each, 0, each - 1), 0, 0),
                )
            )
    return args, specs


def out_kernel(n, each, sel, y, *refs):
    blocks, (o, rows) = refs[:-2], refs[-2:]
    e, pos = pl.program_id(0), ring_pos(n)
    cap = y.shape[1]
    size = blocks[0].shape[1]
    here = pl.ds(pl.multiple_of(e * cap, cap), cap)

    def project(p):
        for s in range(n):
            g = ring_index((pos + n + (2 * (p % 2) - 1) * s) % n, n)
            part = lax.dot_general(
                y[0], blocks[p * n + s][0], (((1,), (1,)), ((), ())), preferred_element_type=F32
            )
            rows[here, columns(g, size)] = part.astype(BF)

    for p in range(len(blocks) // n):
        pl.when(e // each == p)(functools.partial(project, p))

    @pl.when(e == pl.num_programs(0) - 1)
    def _():
        tile = o.shape[1] // 4
        for t in range(4):
            c = pl.ds(t * tile, tile)
            o[:, c] = lax.dot_general(
                sel[...], rows[:, c], (((0,), (0,)), ((), ())), preferred_element_type=F32
            ).astype(BF)


def out_project(sel, y, rings, width):
    n = lax.axis_size("ep")
    experts, cap, inner = y.shape
    tokens = sel.shape[1]
    args, specs = arrivals(rings, n)
    return pl.pallas_call(
        functools.partial(out_kernel, n, args[0].shape[0]),
        grid=(experts,),
        out_shape=jax.ShapeDtypeStruct((tokens, width), BF),
        in_specs=[
            pl.BlockSpec(sel.shape, lambda i: (0, 0)),
            pl.BlockSpec((1, cap, inner), lambda i: (i, 0, 0)),
        ]
        + specs,
        out_specs=pl.BlockSpec((tokens, width), lambda i: (0, 0)),
        scratch_shapes=[pltpu.VMEM((experts * cap, width), BF)],
        compiler_params=pltpu.CompilerParams(vmem_limit_bytes=VMEM_CAP),
        cost_estimate=pl.CostEstimate(
            flops=2 * experts * cap * width * (inner + tokens),
            bytes_accessed=2 * experts * inner * width,
            transcendentals=0,
        ),
        name="out_project",
    )(sel, y, *args)


def back_kernel(n, each, sel, d, *refs):
    blocks, (o, rows) = refs[:-2], refs[-2:]
    e, pos = pl.program_id(0), ring_pos(n)
    size = blocks[0].shape[1]
    rows[...] = jnp.dot(sel[...], d[...], preferred_element_type=F32).astype(BF)

    def project(p):
        total = None
        for s in range(n):
            g = ring_index((pos + n + (2 * (p % 2) - 1) * s) % n, n)
            part = jnp.dot(
                rows[:, columns(g, size)], blocks[p * n + s][0], preferred_element_type=F32
            )
            total = part if total is None else total + part
        o[0] = total

    for p in range(len(blocks) // n):
        pl.when(e // each == p)(functools.partial(project, p))


def out_back(sel, d, rings, experts):
    n = lax.axis_size("ep")
    tokens, width = d.shape
    cap = sel.shape[0] // experts
    args, specs = arrivals(rings, n)
    inner = args[0].shape[2]
    return pl.pallas_call(
        functools.partial(back_kernel, n, args[0].shape[0]),
        grid=(experts,),
        out_shape=jax.ShapeDtypeStruct((experts, cap, inner), F32),
        in_specs=[
            pl.BlockSpec((cap, tokens), lambda i: (i, 0)),
            pl.BlockSpec((tokens, width), lambda i: (0, 0)),
        ]
        + specs,
        out_specs=pl.BlockSpec((1, cap, inner), lambda i: (i, 0, 0)),
        scratch_shapes=[pltpu.VMEM((cap, width), BF)],
        compiler_params=pltpu.CompilerParams(vmem_limit_bytes=VMEM_CAP),
        cost_estimate=pl.CostEstimate(
            flops=2 * experts * cap * width * (inner + tokens),
            bytes_accessed=2 * experts * inner * width,
            transcendentals=0,
        ),
        name="out_back",
    )(sel, d, *args)


def grad_rows_kernel(n, half, dest, x, *refs):
    low, high = refs[:n], refs[n : 2 * n]
    o, picked, y = refs[2 * n :]
    e = pl.program_id(0)
    pos = ring_pos(n)
    cap = low[0].shape[1]
    index = e * cap + lax.broadcasted_iota(jnp.int32, (cap, x.shape[1]), 0)

    def gather(sources, sign):
        for s in range(n):
            g = ring_index((pos + n + sign * s) % n, n)
            hit = (dest[g, 0:1, :] == index) | (dest[g, 1:2, :] == index)
            sel = jnp.where(hit, 1.0, 0.0).astype(BF)
            r = pl.ds(s * cap, cap)
            picked[r] = jnp.dot(sel, x[g], preferred_element_type=F32).astype(BF)
            y[r] = sources[s][0]

    pl.when(e < half)(lambda: gather(low, -1))
    pl.when(e >= half)(lambda: gather(high, 1))
    o[0] = lax.dot_general(
        picked[...], y[...], (((0,), (0,)), ((), ())), preferred_element_type=F32
    )


def grad_rows(dest, x, got):
    n, tokens, block = x.shape
    half, cap, cols = got[0][0].shape
    experts = 2 * half
    low = pl.BlockSpec((1, cap, cols), lambda i: (jnp.minimum(i, half - 1), 0, 0))
    high = pl.BlockSpec((1, cap, cols), lambda i: (jnp.maximum(i - half, 0), 0, 0))
    return pl.pallas_call(
        functools.partial(grad_rows_kernel, n, half),
        grid=(experts,),
        out_shape=jax.ShapeDtypeStruct((experts, block, cols), F32),
        in_specs=[
            pl.BlockSpec(dest.shape, lambda i: (0, 0, 0)),
            pl.BlockSpec(x.shape, lambda i: (0, 0, 0)),
        ]
        + [low] * n
        + [high] * n,
        out_specs=pl.BlockSpec((1, block, cols), lambda i: (i, 0, 0)),
        scratch_shapes=[pltpu.VMEM((n * cap, block), BF), pltpu.VMEM((n * cap, cols), BF)],
        compiler_params=pltpu.CompilerParams(vmem_limit_bytes=VMEM_CAP),
        cost_estimate=pl.CostEstimate(
            flops=2 * experts * n * cap * block * (tokens + cols),
            bytes_accessed=2 * (x.size + experts * n * cap * cols) + 4 * experts * block * cols,
            transcendentals=0,
        ),
        name="grad_rows",
    )(dest, x, *got[0], *got[1])


def slot_dest(routes, order, experts, capacity):
    pairs = routes.shape[0] * 2
    expert = routes.reshape(pairs)
    index = jnp.arange(pairs, dtype=jnp.int32)
    place = jnp.sum(
        jnp.where(order.reshape(1, pairs) == index[:, None], index[None, :], 0), axis=1
    )
    ahead = (place[None, :] < place[:, None]) & (expert[None, :] == expert[:, None])
    slot = jnp.sum(ahead.astype(jnp.int32), axis=1)
    dest = jnp.where(slot < capacity, expert * capacity + slot, -1)
    return dest.reshape(-1, 2)


def slot_onehot(dest, slots):
    index = jnp.arange(slots, dtype=jnp.int32)[:, None]
    return ((dest[None, :, 0] == index) | (dest[None, :, 1] == index)).astype(BF)


def slot_values(dest, values, slots):
    index = jnp.arange(slots, dtype=jnp.int32)[:, None]
    zero = jnp.zeros((), values.dtype)
    return jnp.sum(
        jnp.where(dest[None, :, 0] == index, values[None, :, 0], zero)
        + jnp.where(dest[None, :, 1] == index, values[None, :, 1], zero),
        axis=1,
    )


def router_gates(logits, hot):
    top = jnp.max(jnp.where(hot, logits, MASKED), axis=1, keepdims=True)
    e = jnp.where(hot, jnp.exp(logits - top), 0.0)
    return e / jnp.sum(e, axis=1, keepdims=True)


def chosen(gates, routes):
    index = jnp.arange(gates.shape[1], dtype=jnp.int32)
    return jnp.sum(jnp.where(routes[:, :, None] == index, gates[:, None, :], 0.0), axis=2)


def angles(positions):
    half = HD // 2
    freq = ROPE_BASE ** (-(jnp.arange(half, dtype=F32) * 2.0) / HD)
    a = positions.astype(F32)[:, None] * freq[None, :]
    return jnp.tile(jnp.cos(a), (1, 2)), jnp.concatenate([-jnp.sin(a), jnp.sin(a)], axis=1)


def place_of(index):
    tail = jnp.maximum(index - PROMPT, 0)
    position = jnp.where(index < PROMPT, index, PROMPT + tail % CLEN)
    segment = jnp.where(index < PROMPT, 0, 1 + tail // CLEN)
    return position, segment


def per_device(
    tokens,
    grad_out,
    norm1_gain,
    attn_router,
    attn_routes,
    attn_order,
    w_query,
    w_kv,
    w_attn_out,
    norm2_gain,
    mlp_router,
    mlp_routes,
    mlp_order,
    w_gate,
    w_up,
    w_down,
):
    glen, width = tokens.shape
    n = lax.axis_size("ep")
    nw = lax.axis_size("ws")
    ep, ws = lax.axis_index("ep"), lax.axis_index("ws")
    ea, em = attn_router.shape[1], mlp_router.shape[1]
    acap, mcap = 2 * glen // ea, 2 * glen // em
    owners = n // em
    slots, mslots = ea * acap, em * mcap
    heads = w_query.shape[2] // HD
    block = w_query.shape[1]
    quarter = width // nw
    cut = lambda v: lax.dynamic_slice_in_dim(v, ws * quarter, quarter, v.ndim - 1)
    cut0 = lambda v: lax.dynamic_slice_in_dim(v, ws * quarter, quarter, 0)

    on_ring = n <= RING_MAX
    ring_a = [GatherRing(w_attn_out[: ea // 2])] if on_ring else []
    hop(ring_a)

    a_dest = slot_dest(attn_routes, attn_order, ea, acap)
    m_dest = slot_dest(mlp_routes, mlp_order, em, mcap)
    lock(ring_a)
    hop(ring_a)
    a_dest, m_dest = lock(ring_a, a_dest, m_dest)
    hop(ring_a)
    a_sel = slot_onehot(a_dest, slots)
    m_sel = slot_onehot(m_dest, mslots)
    a_hot = jnp.any(attn_routes[:, :, None] == jnp.arange(ea, dtype=jnp.int32), axis=1)
    m_hot = jnp.any(mlp_routes[:, :, None] == jnp.arange(em, dtype=jnp.int32), axis=1)
    token_index = jnp.arange(glen, dtype=jnp.int32)
    a_token = slot_values(a_dest, jnp.stack([token_index, token_index], 1), slots)
    other = slot_values(m_dest, mlp_routes[:, ::-1], mslots).reshape(em, mcap)
    x = tokens.astype(F32)
    inv1 = lax.rsqrt(jnp.mean(x * x, axis=1, keepdims=True) + EPS)
    xn = (x * inv1 * norm1_gain).astype(BF)
    a_sel, m_sel, a_token, xn, other = lock(ring_a, a_sel, m_sel, a_token, xn, other)
    hop(ring_a)
    slot_in = mm("st,td->sd", a_sel, xn).astype(BF).reshape(ea, acap, width)
    xn_turned = jnp.transpose(xn.reshape(glen, n, block), (1, 2, 0))
    part_w = glen // nw
    x_mine = lax.dynamic_slice_in_dim(xn, ws * part_w, part_w, 0)
    x_mine = jnp.transpose(x_mine.reshape(part_w, n, block), (1, 0, 2))
    dest_mine = lax.dynamic_slice_in_dim(a_dest.T, ws * part_w, part_w, 1)
    dest_mine = jnp.broadcast_to(jnp.tile(dest_mine, (4, 1))[None], (n, 8, part_w))
    slot_in, xn_turned, x_mine, dest_mine = lock(ring_a, slot_in, xn_turned, x_mine, dest_mine)
    hop(ring_a)
    q_cos, q_sin = angles(place_of(a_token)[0])
    cos, sin = angles(place_of(token_index)[0])
    q_cos, q_sin, cos, sin = lock(ring_a, q_cos, q_sin, cos, sin)
    hop(ring_a)
    a_logits = mm("td,de->te", xn, attn_router)
    a_gate = router_gates(a_logits, a_hot)
    a_slot_gate = slot_values(a_dest, chosen(a_gate, attn_routes), slots)
    dy_q = cut(grad_out)
    dy_slots = mm("st,td->sd", m_sel, dy_q).astype(BF)
    a_column, gate_column = a_token[:, None], a_slot_gate[:, None]
    a_column, gate_column, dy_slots, a_gate = lock(ring_a, a_column, gate_column, dy_slots, a_gate)
    hop(ring_a)
    w_kv, w_query = lock(ring_a, w_kv, w_query)
    dy_send = jnp.repeat(dy_slots.reshape(em, mcap, quarter), owners, axis=0)
    other = jnp.broadcast_to(jnp.repeat(other, owners, axis=0)[:, None], (n, 8, mcap))
    payloads = ((dy_send, 1), (other, 0), (x_mine, 0), (dest_mine, 1))
    if on_ring:
        (full_kv, full_query), (dy_rows, other, x_all, all_dest) = ring_kernel_gather(8, (1, 2), (w_kv, w_query), payloads)
        ring_b = [GatherRing(after(w_attn_out[ea // 2 :], full_query))]
    else:
        gather = lambda v: lax.all_gather(v, "ep", axis=1, tiled=True)
        full_kv, full_query, full_out = gather(w_kv), gather(w_query), gather(w_attn_out)
        dy_rows, other = dispatch(8, *payloads[:2])
        ring_b = []
    dy_rows, other = dy_rows.reshape(n * mcap, width), other[:, 0].reshape(-1)
    hop(ring_b)
    q_pre = mm("ecd,edj->ecj", slot_in, full_query)
    (q_pre,) = lock(ring_b, q_pre)
    hop(ring_b)
    k_pre = mm("td,dj->tj", xn, full_kv[0])
    v_pre = mm("td,dj->tj", xn, full_kv[1])
    k_pre, v_pre = lock(ring_b, k_pre, v_pre)
    hop(ring_b)
    q, k, v, attn_o, gated_o, lse = attend(
        q_pre.reshape(slots, -1), k_pre, v_pre, q_cos, q_sin, cos, sin, a_column, gate_column
    )
    (gated_o,) = lock(ring_b, gated_o)
    hop(ring_b)
    dy_down = mm("rd,df->rf", dy_rows, w_down)
    (dy_down,) = lock(ring_b, dy_down)
    for _ in range(3):
        hop(ring_b)
    gated_o = gated_o.reshape(ea, acap, heads * HD)
    slots_travel = n <= RING_MAX and n * slots <= ea * width
    ring_o = [GatherRing(gated_o)] if slots_travel else []
    hop(ring_o)
    if on_ring:
        branch = out_project(a_sel, gated_o, ring_a + ring_b, width)
    else:
        branch = project_back(a_sel, gated_o, (full_out,))
    (branch,) = lock(ring_o, branch)
    hop(ring_o)
    gain2 = cut0(norm2_gain)[None]
    hidden, inv2, hn, hn_slots = mix(branch, cut(tokens), gain2, m_sel, 0)
    hidden, inv2, hn, hn_slots = lock(ring_o, hidden, inv2, hn, hn_slots)
    x_q = cut(tokens).astype(F32)
    router_q = lax.dynamic_slice_in_dim(mlp_router, ws * quarter, quarter, 0)
    hn_slots = jnp.repeat(hn_slots.reshape(em, mcap, quarter), owners, axis=0)
    rows = dispatch(1, (hn_slots, 1))[0].reshape(n * mcap, width)
    (rows,) = lock(ring_o, rows)

    rows_w = glen // nw

    def mine(v):
        v = lax.dynamic_slice_in_dim(v, ws * rows_w, rows_w, 0)
        return jnp.transpose(v.reshape(rows_w, n, block), (1, 0, 2))

    hop(ring_o)
    d_gate, d_up, act_bf, down_bf, d_part, row_dgate, *spread = expert_pass(
        rows, other[:, None], dy_down, mlp_router, w_gate, w_up, owners, mcap,
        (), 6,
    )
    d_gate, d_up, act_bf, down_bf, d_part, row_dgate = lock(
        ring_o, d_gate, d_up, act_bf, down_bf, d_part, row_dgate
    )
    hop(ring_o)
    d_part = d_part.reshape(n, mcap, width)
    if on_ring:
        d_rows, m_dgate, *part = give_back_part(d_part, row_dgate, act_bf, w_down, 2)
    else:
        d_rows, m_dgate = give_back(d_part, row_dgate, 2)
        part = quarters(mm("rf,df->rd", act_bf, w_down).astype(BF))
        grad_gate = mm("rd,rf->df", rows, d_gate)
        grad_up = mm("rd,rf->df", rows, d_up)
        grad_down = mm("rd,rf->df", dy_rows, down_bf)
    d_rows, m_dgate, *part = lock(ring_o, d_rows, m_dgate, *part)
    hop(ring_o)
    far, near = lax.ppermute(part[0], "ws", CORE), lax.ppermute(part[1], "ws", CORE)
    far = (part[2].astype(F32) + far.astype(F32)).astype(BF)
    m_slot_gate = m_dgate[:, 4].reshape(em, owners, mcap)[:, 0].reshape(mslots)
    m_dgate = jnp.sum(m_dgate[:, 0].reshape(em, owners, mcap), axis=1).reshape(mslots, 1)

    def by_owner(v):
        if owners > 1:
            v = jnp.sum(v.astype(F32).reshape(em, owners, mcap, quarter), axis=1).astype(BF)
        return v.reshape(mslots, quarter)

    d_rows = by_owner(d_rows)
    def per_expert(sel, values, experts):
        terms = sel.reshape(experts, -1, glen).astype(F32) * values.reshape(experts, -1, 1)
        return jnp.sum(terms, axis=1).T

    def router_back(dgate, gates):
        return (gates * (dgate - jnp.sum(gates * dgate, axis=1, keepdims=True))).astype(BF)

    m_gate = per_expert(m_sel, m_slot_gate, em)
    kept = jnp.sum(m_gate, axis=1, keepdims=True)
    m_kept = jnp.any(m_sel.reshape(em, -1, glen) > 0, axis=1).T
    m_gate = jnp.where(m_hot & ~m_kept, jnp.maximum(1.0 - kept, 0.0), m_gate)
    d_m_logits = router_back(per_expert(m_sel, m_dgate, em), m_gate)
    grad_mlp_router = mm("td,te->ed", hn, d_m_logits)
    d_hn = mm("te,de->td", d_m_logits, router_q)
    d_hidden, grad_norm2, d_hid = home(m_sel, d_rows, d_hn, hidden, inv2, gain2, dy_q, 3)
    d_hid, far, near = lock(ring_o, d_hid, far, near)
    hop(ring_o)
    far = lax.ppermute(far, "ws", CROSS)

    if on_ring:
        raw_do = out_back(a_sel, d_hid, ring_a + ring_b, ea).reshape(slots, heads * HD)
    else:
        dh_slots = mm("st,td->sd", a_sel, d_hid).astype(BF).reshape(ea, acap, width)
        raw_do = mm("ecd,edj->ecj", dh_slots, full_out).reshape(slots, heads * HD)
    raw_do, far, near = lock(ring_o, raw_do, far, near)
    hop(ring_o)
    part = (part[3].astype(F32) + near.astype(F32) + far.astype(F32)).astype(BF)
    part = lax.all_to_all(part.reshape(n, mcap, quarter), "ep", 0, 0, tiled=True)
    d_q, d_kv, a_dgate, *spread = attend_back(
        raw_do, attn_o, gate_column, q, k, v, lse, q_cos, q_sin, cos, sin, a_column,
        (), 7,
    )
    d_q = d_q.reshape(ea, acap, heads * HD)
    d_q, d_kv, part = lock(ring_o, d_q, d_kv, part)

    arouter_q = lax.dynamic_slice_in_dim(attn_router, ws * quarter, quarter, 0)
    xn_q = cut(xn)
    unit1 = x_q * inv1
    gain1 = cut0(norm1_gain)[None]
    expert_out = by_owner(part)
    mlp_branch = mm("st,sd->td", m_sel, (expert_out.astype(F32) * m_slot_gate[:, None]).astype(BF))
    layer_out = (hidden + mlp_branch).astype(BF)

    if slots_travel:
        pad = lambda v: jnp.pad(v, ((0, 16 - ea), (0, 0)))
        all_dq, grad_kv, h_all, grad_tokens, layer_out, stats, *grads = last_stage(
            9, d_q, d_kv, xn_turned, a_sel, full_query, full_kv, mine(d_hid), d_hidden, unit1, inv1, gain1, layer_out, grad_norm2, grad_mlp_router, a_dgate, pad(a_gate.T),
            pad(arouter_q.T), xn_q,
            rows, dy_rows, d_gate, d_up, down_bf,
        )
        grad_gate, grad_up, grad_down = [g.astype(F32) for g in grads]
        grad_query = grad_slots(all_dest, x_all, all_dq)
        grad_attn_out = grad_rows(all_dest, h_all, ring_o[0].got)
    else:
        a_dgate = lax.psum(a_dgate[0], "ws")
        d_a_logits = router_back(per_expert(a_sel, a_dgate, ea), a_gate)
        grad_attn_router = mm("td,te->ed", xn_q, d_a_logits)
        d_xn = ws_reduce(project_back(a_sel, d_q, (full_query,), d_kv, full_kv), 4)
        d_xn = d_xn + mm("te,de->td", d_a_logits, arouter_q)
        grad_norm1 = jnp.sum(d_xn * unit1, axis=0, keepdims=True)
        w1 = d_xn * gain1
        mean1 = lax.psum(jnp.sum(w1 * unit1, axis=1, keepdims=True), "ws") / width
        grad_tokens = (d_hidden + inv1 * (w1 - unit1 * mean1)).astype(BF)
        grad_tokens = ws_spread(grad_tokens, 5)
        dh_slots = mm("st,td->sd", a_sel, d_hid).astype(BF).reshape(ea, acap, width)
        scatter = lambda g: lax.psum_scatter(g.astype(BF), "ep", scatter_dimension=1, tiled=True)
        grad_query = scatter(mm("ecd,ecj->edj", slot_in, d_q)).astype(F32)
        grad_attn_out = scatter(mm("ecd,ecj->edj", dh_slots, gated_o)).astype(F32)
        grad_kv = scatter(mm("td,ktj->kdj", xn, d_kv)).astype(F32)
        layer_out = ws_gather(layer_out)
        norms = jnp.where(jnp.arange(8)[:, None] == 0, grad_norm1, grad_norm2)
        stats = collect(jnp.concatenate([norms, grad_attn_router, grad_mlp_router]), 10)
    grad_tokens = grad_tokens.astype(F32)

    grad_norm1, grad_norm2 = stats[0], stats[1]
    grad_attn_router, grad_mlp_router = stats[8 : 8 + ea].T, stats[8 + ea :].T
    return (
        layer_out,
        grad_tokens,
        grad_norm1,
        grad_attn_router,
        grad_query,
        grad_kv,
        grad_attn_out,
        grad_norm2,
        grad_mlp_router,
        grad_gate,
        grad_up,
        grad_down,
    )


def solution(mesh):
    rows, wide = P("ep", None), P(None, ("ep", "ws"))
    attn = P(None, "ep", "ws")
    return jax.shard_map(
        per_device,
        mesh=mesh,
        in_specs=(rows, rows, P(), P(), rows, rows, attn, attn, attn, P(), P(), rows, rows)
        + (wide,) * 3,
        out_specs=(rows, rows, P(), P(), attn, attn, attn, P(), P()) + (wide,) * 3,
        check_vma=False,
    )
```
